32 devices in a mesh: ctx: 8 (over z, x), fsdp: 4 (over y, core).
Axes of the slice: x: 2, y: 2, z: 4, core: 2. Of those that a mesh axis runs over, the one named last changes fastest.
Arguments:
- tokens: bfloat16 [4, 4096, 768], P('fsdp', 'ctx'), may hold values from -6 to 6
- doc_lengths: int32 [4, 16], P('fsdp'), may hold values from 1 to 512, 4096 in all within a row
- cotangent: bfloat16 [4, 4096, 768], P('fsdp', 'ctx'), may hold values from -6 to 6
- w_query: bfloat16 [768, 768], P('fsdp'), may hold values from -0.21875 to 0.21875
- w_key: bfloat16 [768, 768], P('fsdp'), may hold values from -0.21875 to 0.21875
- w_value: bfloat16 [768, 768], P('fsdp'), may hold values from -0.21875 to 0.21875
- w_output: bfloat16 [768, 768], P('fsdp'), may hold values from -0.625 to 0.625
- w_inner: bfloat16 [768, 3072], P('fsdp'), may hold values from -0.21875 to 0.21875
- w_outer: bfloat16 [3072, 768], P('fsdp'), may hold values from -0.109375 to 0.109375
- b_query: bfloat16 [768], P('fsdp'), may hold values from -3 to 3
- b_value: bfloat16 [768], P('fsdp'), may hold values from -3 to 3
- b_output: bfloat16 [768], P('fsdp'), may hold values from -3 to 3
- b_inner: bfloat16 [3072], P('fsdp'), may hold values from -3 to 3
- b_outer: bfloat16 [768], P('fsdp'), may hold values from -3 to 3
- gain_attn: bfloat16 [768], P('fsdp'), may hold values from 0.5 to 1.5
- shift_attn: bfloat16 [768], P('fsdp'), may hold values from -3 to 3
- gain_ffn: bfloat16 [768], P('fsdp'), may hold values from 0.5 to 1.5
- shift_ffn: bfloat16 [768], P('fsdp'), may hold values from -3 to 3
Outputs:
- layer_out: bfloat16 [4, 4096, 768], P('fsdp', 'ctx')
- grad_tokens: float32 [4, 4096, 768], P('fsdp', 'ctx')
- grad_w_query: float32 [768, 768], P('fsdp')
- grad_w_key: float32 [768, 768], P('fsdp')
- grad_w_value: float32 [768, 768], P('fsdp')
- grad_w_output: float32 [768, 768], P('fsdp')
- grad_w_inner: float32 [768, 3072], P('fsdp')
- grad_w_outer: float32 [3072, 768], P('fsdp')
- grad_b_query: float32 [768], P('fsdp')
- grad_b_value: float32 [768], P('fsdp')
- grad_b_output: float32 [768], P('fsdp')
- grad_b_inner: float32 [3072], P('fsdp')
- grad_b_outer: float32 [768], P('fsdp')
- grad_gain_attn: float32 [768], P('fsdp')
- grad_shift_attn: float32 [768], P('fsdp')
- grad_gain_ffn: float32 [768], P('fsdp')
- grad_shift_ffn: float32 [768], P('fsdp')
The draws below stay inside these ranges and needn't reach their ends.
Inputs may be any that keep to these rules, and one draw needn't show every extreme that they name: `doc_lengths`: each stream's 16 lengths sum to 4096; the longest is exactly 512.
All inputs are finite; a program needn't handle non-finite values.
Results may differ from the reference program's by a relative error of at most 0.019.
Values may be sent and summed in bfloat16 or wider, within the bound.
A program may use at most 128 MiB of HBM per device.

```python
import math
import jax
import jax.numpy as jnp
import numpy as np
from jax import lax

D = 768
FF = 3072
HEADS = 12
HEAD_DIM = 64
STREAM = 4096
STREAMS = 4
DOC_MOST = 512
DOCS = 16


def shard_levels(own_key, shape, cuts, least, largest):
    level = 1.0
    for dim, blocks in cuts:
        heights = jax.random.uniform(jax.random.fold_in(jax.random.fold_in(own_key, 6), dim), (blocks,), jnp.float32, least / len(cuts), largest / len(cuts))
        level = level * jnp.repeat(jnp.exp(heights), shape[dim] // blocks).reshape((-1,) + (1,) * (len(shape) - 1 - dim))
    return level


def length_profile(count, total, reach, skew):
    weights = [(1 << 20) // math.isqrt(standing ** skew) + 1 for standing in range(2, count + 1)]
    spare, holding = total - reach - (count - 1), [1] * (count - 1)
    while spare > 0:
        candidates = [i for i in range(count - 1) if holding[i] < reach]
        mass, remaining = sum([weights[i] for i in candidates]), spare
        for i in candidates:
            more = min(reach - holding[i], max(1, remaining * weights[i] // mass), spare)
            holding[i] = holding[i] + more
            spare = spare - more
    return np.array([reach] + holding)


def uneven(key, amount, total, most, lean):
    if amount == 2:
        one = jax.random.randint(key, (), max(1, total - most), min(most, total - 1) + 1)
        return jnp.stack([one, total - one])
    sizes = jnp.asarray(length_profile(amount, total, most, lean), jnp.int32)
    couples = (amount - 1) // 2
    giver, receiver = sizes[1:1 + 2 * couples:2], sizes[2:2 + 2 * couples:2]
    room = jnp.minimum(giver - 1, most - receiver)
    moved = jax.random.randint(jax.random.fold_in(key, 1), (couples,), 0, 1 << 20) % (room + 1)
    sizes = sizes.at[1:1 + 2 * couples:2].set(giver - moved).at[2:2 + 2 * couples:2].set(receiver + moved)
    return sizes[jax.random.permutation(jax.random.fold_in(key, 2), amount)]


def normal_values(stream_key, shape, scale, limit, cuts=(), kind=jnp.bfloat16):
    array = jax.random.normal(stream_key, shape, jnp.float32) * scale
    if len(cuts) > 0:
        array = shard_levels(stream_key, shape, cuts, -0.22, 0.18) * array
    return jnp.clip(array, min=-limit, max=limit).astype(kind)


def setup_inputs(seed: int = 0) -> dict:
    splits = jax.random.split(jax.random.key(seed), 19)
    return {
        "tokens": normal_values(splits[0], (STREAMS, STREAM, D), 1.0, 6.0, ((0, 4), (1, 8))),
        "doc_lengths": jax.vmap(lambda own: uneven(own, DOCS, STREAM, DOC_MOST, 2))(jax.random.split(splits[1], STREAMS)).reshape((STREAMS, DOCS)).astype(jnp.int32),
        "cotangent": normal_values(splits[2], (STREAMS, STREAM, D), 1.0, 6.0, ((0, 4), (1, 8))),
        "w_query": normal_values(splits[3], (D, D), D ** -0.5, 0.21875, ((0, 4),)),
        "w_key": normal_values(splits[4], (D, D), D ** -0.5, 0.21875, ((0, 4),)),
        "w_value": normal_values(splits[5], (D, D), D ** -0.5, 0.21875, ((0, 4),)),
        "w_output": normal_values(splits[6], (D, D), (D // 8) ** -0.5, 0.625, ((0, 4),)),
        "w_inner": normal_values(splits[7], (D, FF), D ** -0.5, 0.21875, ((0, 4),)),
        "w_outer": normal_values(splits[8], (FF, D), FF ** -0.5, 0.109375, ((0, 4),)),
        "b_query": normal_values(splits[9], (D,), 0.5, 3.0, ((0, 4),)),
        "b_value": normal_values(splits[10], (D,), 0.5, 3.0, ((0, 4),)),
        "b_output": normal_values(splits[11], (D,), 0.5, 3.0, ((0, 4),)),
        "b_inner": normal_values(splits[12], (FF,), 0.5, 3.0, ((0, 4),)),
        "b_outer": normal_values(splits[13], (D,), 0.5, 3.0, ((0, 4),)),
        "gain_attn": jnp.clip(1.0 + 0.1 * jax.random.normal(splits[14], (D,), jnp.float32), 0.5, 1.5).astype(jnp.bfloat16),
        "shift_attn": normal_values(splits[15], (D,), 0.5, 3.0, ((0, 4),)),
        "gain_ffn": jnp.clip(1.0 + 0.1 * jax.random.normal(splits[16], (D,), jnp.float32), 0.5, 1.5).astype(jnp.bfloat16),
        "shift_ffn": normal_values(splits[17], (D,), 0.5, 3.0, ((0, 4),)),
    }


@jax.custom_vjp
def low(v):
    return lax.optimization_barrier(v.astype(jnp.bfloat16)).astype(jnp.float32)

@jax.custom_vjp
def low_back(v):
    return v

def low_keep(v):
    return (low(v), None)

def low_pass(kept, grad):
    return (grad,)

def back_keep(v):
    return (v, None)

def back_low(kept, grad):
    return (low(grad),)
low.defvjp(low_keep, low_pass)
low_back.defvjp(back_keep, back_low)
EPS = 1e-12
SCALE = 0.125
HIGHEST = lax.Precision.HIGHEST

def layer_norm(hidden, gain_vec, shift_vec):
    centre = hidden - lax.optimization_barrier(jnp.mean(hidden, -1, keepdims=True))
    spread = lax.optimization_barrier(jnp.mean(centre * centre, -1, keepdims=True))
    return centre * lax.rsqrt(spread + EPS) * gain_vec + shift_vec

def segment_ids(lengths, row_count):
    starts = jnp.cumsum(lengths) - lengths
    positions = jnp.arange(row_count, dtype=jnp.int32)
    found = lax.optimization_barrier(jnp.sum((positions[:, None] >= starts[None, :]).astype(jnp.int32), -1)) - 1
    return found.astype(jnp.int32)

def attend_stream(query, key_rows, value_rows, segment):
    row_count = query.shape[0]
    block_rows = math.gcd(row_count, 512)
    key_heads = key_rows.reshape(row_count, HEADS, HEAD_DIM)
    value_heads = value_rows.reshape(row_count, HEADS, HEAD_DIM)

    def one_block(pieces):
        query_blk, segment_blk = pieces
        scores = low_back(jnp.einsum('qhd,khd->qhk', query_blk, key_heads, precision=HIGHEST) * SCALE)
        key_mask = segment_blk[:, None] == segment[None, :]
        exp_scores = jnp.where(key_mask[:, None, :], jnp.exp(scores), 0.0)
        row_total = lax.optimization_barrier(jnp.sum(exp_scores, -1))
        numerator = low_back(jnp.einsum('qhk,khd->qhd', low(exp_scores), value_heads, precision=HIGHEST))
        return (numerator / row_total[..., None]).reshape(block_rows, D)
    blocks = (query.reshape(row_count // block_rows, block_rows, HEADS, HEAD_DIM), segment.reshape(row_count // block_rows, block_rows))
    return lax.map(jax.checkpoint(one_block), blocks).reshape(row_count, D)

def forward(inputs, params, segment):
    w_query, w_key, w_value, w_output, w_inner, w_outer, b_query, b_value, b_output, b_inner, b_outer, gain_attn, shift_attn, gain_ffn, shift_ffn = params
    query = low(low_back(jnp.dot(inputs, w_query, precision=HIGHEST) + b_query))
    key_rows = low(low_back(jnp.dot(inputs, w_key, precision=HIGHEST)))
    value_rows = low(low_back(jnp.dot(inputs, w_value, precision=HIGHEST) + b_value))
    context = low(low_back(attend_stream(query, key_rows, value_rows, segment)))
    hidden_one = inputs + low_back(jnp.dot(context, w_output, precision=HIGHEST) + b_output)
    normed = low(layer_norm(hidden_one, gain_attn, shift_attn))
    inner_pre = low_back(jnp.dot(normed, w_inner, precision=HIGHEST) + b_inner)
    active = low(jax.nn.gelu(inner_pre, approximate=False))
    hidden_two = normed + low_back(jnp.dot(active, w_outer, precision=HIGHEST) + b_outer)
    return layer_norm(hidden_two, gain_ffn, shift_ffn)

def reference(tokens, doc_lengths, cotangent, w_query, w_key, w_value, w_output, w_inner, w_outer, b_query, b_value, b_output, b_inner, b_outer, gain_attn, shift_attn, gain_ffn, shift_ffn):
    params = tuple((p.astype(jnp.float32) for p in (w_query, w_key, w_value, w_output, w_inner, w_outer, b_query, b_value, b_output, b_inner, b_outer, gain_attn, shift_attn, gain_ffn, shift_ffn)))

    def one_stream(grad_sums, pieces):
        inputs, lengths, incoming = pieces
        segment = segment_ids(lengths, inputs.shape[0])

        def apply_layer(layer_in, *weights):
            return forward(layer_in, weights, segment)
        result, pullback = jax.vjp(apply_layer, inputs.astype(jnp.float32), *params)
        grads = pullback(incoming.astype(jnp.float32))
        updated = tuple((running + fresh for running, fresh in zip(grad_sums, grads[1:])))
        return (updated, (result.astype(jnp.bfloat16), grads[0]))
    start_sums = tuple((jnp.zeros_like(p) for p in params))
    grad_sums, (layer_out, grad_tokens) = lax.scan(one_stream, start_sums, (tokens, doc_lengths, cotangent))
    return (layer_out, grad_tokens, grad_sums[0], grad_sums[1], grad_sums[2], grad_sums[3], grad_sums[4], grad_sums[5], grad_sums[6], grad_sums[7], grad_sums[8], grad_sums[9], grad_sums[10], grad_sums[11], grad_sums[12], grad_sums[13], grad_sums[14])
```

```python
import functools

import jax
import jax.numpy as jnp
from jax import lax
from jax.experimental import pallas as pl
from jax.experimental.pallas import tpu as pltpu
from jax.sharding import PartitionSpec as P

bf = jnp.bfloat16
f32 = jnp.float32
MESH = pl.DeviceIdType.MESH
VM = pltpu.VMEM
DMA = pltpu.SemaphoreType.DMA
D = 768
EPS = 1e-12
BIG = 1e30
C2 = 0.125 * 1.4426950408889634
RSQ2 = 0.7071067811865476
RS2PI = 0.3989422804014327
BQ = 256
WIN = BQ + 1024
TOKP = 4
HS = 192
VLIM = 58 * 2**20
FULL = pl.BlockSpec(memory_space=pltpu.VMEM)


def nt(a, b):
    return lax.dot_general(a, b, (((1,), (1,)), ((), ())), preferred_element_type=f32)


def nn(a, b):
    return lax.dot_general(a, b, (((1,), (0,)), ((), ())), preferred_element_type=f32)


def tn(a, b):
    return lax.dot_general(a, b, (((0,), (0,)), ((), ())), preferred_element_type=f32)


def bit(i, b):
    return lax.rem(lax.div(i, b), 2)


def flip(i, b):
    return i + b * (1 - 2 * bit(i, b))


def remote(src, dst, send, recv, device):
    return pltpu.make_async_remote_copy(
        src_ref=src, dst_ref=dst, send_sem=send, recv_sem=recv, device_id=device, device_id_type=MESH
    )


def greet(peers, others):
    bar = pltpu.get_barrier_semaphore()
    for d in peers:
        pl.semaphore_signal(bar, inc=1, device_id=d, device_id_type=MESH)
    for cond, d in others:

        @pl.when(cond)
        def _():
            pl.semaphore_signal(bar, inc=1, device_id=d, device_id_type=MESH)

    pl.semaphore_wait(bar, len(peers) + sum(cond.astype(jnp.int32) for cond, _ in others))


PIECES = [(0, 0, 192, 0, 768, 2), (1, 0, 192, 0, 768, 2), (2, 0, 192, 0, 768, 2), (3, 0, 192, 0, 768, 1)]
PIECES += [(4, 0, 192, 768 * j, 768, 1 if j < 3 else 2) for j in range(4)]
PIECES += [(5, 192 * j, 192, 0, 768, 1 if j in (1, 3) else 2) for j in range(4)]


def gather_kernel(n, *refs):
    nt_ = 6
    tok = refs[0]
    sh = refs[1 : 1 + nt_]
    vec = refs[1 + nt_]
    tok_o = refs[2 + nt_]
    full = refs[3 + nt_ : 3 + 2 * nt_]
    vec_o = refs[3 + 2 * nt_]
    ts, tr, ws, wr, vs, vr = refs[4 + 2 * nt_ :]
    c = lax.axis_index("ctx")
    f = lax.axis_index("fsdp")
    sib = (c, flip(f, 1))
    yp = (c, flip(f, 2))
    dg = (c, flip(flip(f, 1), 2))
    c1 = (flip(c, 1), f)
    c2 = (flip(c, 2), f)
    even = bit(c, 1) == 0
    fwd = jnp.where(even, c + 2, c - 2)
    src = jnp.where(even, c - 2, c + 2)
    has_fwd = jnp.logical_and(fwd >= 0, fwd < n)
    has_src = jnp.logical_and(src >= 0, src < n)
    oth = jnp.where(bit(c, 2) == 0, c - 2, c + 2)
    has_oth = jnp.logical_and(oth >= 0, oth < n)
    greet((sib, yp, dg, c1, c2), ((has_oth, (oth, f)),))
    rows = tok.shape[0]
    pr = rows // TOKP
    pslot = jnp.where(even, 2 * rows, 0)
    dslot = jnp.where(even, 0, 2 * rows)
    fslot = jnp.where(even, 0, 2 * rows)
    tcp = [
        remote(
            tok.at[pl.ds(i * pr, pr)],
            tok_o.at[pl.ds(pl.multiple_of(dslot + i * pr, pr), pr)],
            ts.at[0, i],
            tr.at[0, i],
            c1,
        )
        for i in range(TOKP)
    ]
    vcp = [remote(vec, vec_o.at[f], vs.at[i], vr.at[i], (sib, yp, dg)[i]) for i in range(3)]
    wcp = []
    fy = flip(f, 2)
    for k, (t, r0, R, c0, C, route) in enumerate(PIECES):
        s = sh[t]
        w = full[t]
        SR = s.shape[0]
        H = R // 2
        p = c1 if route == 1 else c2
        hb = bit(c, route)
        cs = slice(c0, c0 + C)
        own = pl.multiple_of(f * SR + r0, 16)
        mine = pl.multiple_of(f * SR + r0 + hb * H, 16)
        gy = pl.multiple_of(fy * SR + r0 + hb * H, 16)
        gx = pl.multiple_of(fy * SR + r0 + (1 - hb) * H, 16)
        wcp.append(
            [
                remote(s.at[pl.ds(r0, R), cs], w.at[pl.ds(own, R), cs], ws.at[k, 0], wr.at[k, 0], sib),
                remote(
                    s.at[pl.ds(pl.multiple_of(r0 + hb * H, 16), H), cs],
                    w.at[pl.ds(mine, H), cs],
                    ws.at[k, 1],
                    wr.at[k, 1],
                    yp,
                ),
                remote(w.at[pl.ds(gy, H), cs], w.at[pl.ds(gy, H), cs], ws.at[k, 2], wr.at[k, 2], p),
                remote(w.at[pl.ds(gy, H), cs], w.at[pl.ds(gy, H), cs], ws.at[k, 3], wr.at[k, 3], sib),
                remote(w.at[pl.ds(gx, H), cs], w.at[pl.ds(gx, H), cs], ws.at[k, 4], wr.at[k, 4], sib),
            ]
        )
    NP = len(PIECES)
    for t in tcp:
        t.start()
    for k in range(NP):
        wcp[k][1].start()
    for v in vcp:
        v.start()
    for k in range(NP):
        wcp[k][0].start()
    for k in range(nt_):
        R = sh[k].shape[0]
        full[k][pl.ds(pl.multiple_of(f * R, 16), R), :] = sh[k][...]
    tok_o[pl.ds(rows, rows), :] = tok[...]
    vec_o[f] = vec[...]

    @pl.when(jnp.logical_not(has_src))
    def _():
        tok_o[pl.ds(pl.multiple_of(fslot, rows), rows), :] = jnp.zeros((rows, D), bf)

    tfw = [
        remote(
            tok_o.at[pl.ds(pl.multiple_of(pslot + i * pr, pr), pr)],
            tok_o.at[pl.ds(pl.multiple_of(fslot + i * pr, pr), pr)],
            ts.at[1, i],
            tr.at[1, i],
            (fwd, f),
        )
        for i in range(TOKP)
    ]

    def ystep(k):
        wcp[k][1].wait_recv()
        wcp[k][2].start()
        wcp[k][3].start()

    def xstep(k):
        wcp[k][2].wait_recv()
        wcp[k][4].start()

    def tstep(i):
        tcp[i].wait_recv()

        @pl.when(has_fwd)
        def _():
            tfw[i].start()

    seq = [(ystep, 0), (tstep, 0), (ystep, 1), (tstep, 1), (ystep, 2), (xstep, 0), (tstep, 2)]
    seq += [(ystep, 3), (xstep, 1), (xstep, 2), (tstep, 3), (ystep, 4), (xstep, 3)]
    for k in range(5, NP):
        seq += [(ystep, k), (xstep, k - 1)]
    seq += [(xstep, NP - 1)]
    for step, k in seq:
        step(k)
    for i in range(TOKP):

        @pl.when(has_src)
        def _():
            tfw[i].wait_recv()

        @pl.when(has_fwd)
        def _():
            tfw[i].wait_send()

        tcp[i].wait_send()
    for k in range(NP):
        for i in (0, 3, 4):
            wcp[k][i].wait_recv()
        for cp in wcp[k]:
            cp.wait_send()
    for v in vcp:
        v.wait()


def gather(n, tokens, shards, vec):
    nt_ = len(shards)
    rows = tokens.shape[0]
    NP = len(PIECES)
    S = jax.ShapeDtypeStruct
    outs = [S((3 * rows, D), bf)]
    outs += [S((4 * s.shape[0], s.shape[1]), bf) for s in shards]
    outs += [S((4,) + vec.shape, bf)]
    return pl.pallas_call(
        functools.partial(gather_kernel, n),
        out_shape=outs,
        in_specs=[FULL] * (nt_ + 2),
        out_specs=[FULL] * (nt_ + 2),
        scratch_shapes=[DMA((2, TOKP)), DMA((2, TOKP)), DMA((NP, 5)), DMA((NP, 5)), DMA((3,)), DMA((3,))],
        compiler_params=pltpu.CompilerParams(collective_id=1, has_side_effects=True, vmem_limit_bytes=VLIM),
        name="gather",
    )(tokens, *shards, vec)


def vecs_of(vec):
    return (vec[0].astype(f32) + vec[1].astype(f32)) + (vec[2].astype(f32) + vec[3].astype(f32))


def member(pos0, rows, se):
    pos = pos0 + lax.broadcasted_iota(jnp.int32, (rows, 128), 0)
    return jnp.logical_and(pos >= se[0:1, :], pos < se[1:2, :])


def fwd_kernel(x, wq, wk, wv, vec, se, q_o, k_o, v_o, att_o, ctx_o, rt_o, nseg):
    R = x.shape[0] // 3
    anchor = lax.axis_index("ctx") * R
    V = vecs_of(vec)
    bq = V[0:1, :]
    bv = V[1:2, :]

    def proj(i, _):
        r = pl.ds(pl.multiple_of(i * 256, 256), 256)
        xb = x[r, :]
        k_o[r, :] = nn(xb, wk[...]).astype(bf)
        v_o[r, :] = (nn(xb, wv[...]) + bv).astype(bf)
        m = member(anchor - R + i * 256, 256, se)
        nseg[r, :] = jnp.where(m, 0.0, 1.0).astype(bf)
        return 0

    lax.fori_loop(0, 3 * R // 256, proj, 0)

    def projq(i, _):
        r = pl.ds(pl.multiple_of(R + i * 256, 256), 256)
        q_o[pl.ds(pl.multiple_of(i * 256, 256), 256), :] = (nn(x[r, :], wq[...]) + bq).astype(bf)
        return 0

    lax.fori_loop(0, R // 256, projq, 0)
    lane = lax.broadcasted_iota(jnp.int32, (BQ, 128), 1)

    def att(i, _):
        qb = lax.div(i, 6)
        hp = lax.rem(i, 6)
        qr = pl.ds(pl.multiple_of(qb * BQ, BQ), BQ)
        wr = pl.ds(pl.multiple_of(qb * BQ, BQ), WIN)
        hc = pl.ds(pl.multiple_of(hp * 128, 128), 128)
        oh = jnp.where(nseg[pl.ds(pl.multiple_of(R + qb * BQ, BQ), BQ), :] == 0, -BIG, 0.0).astype(bf)
        qp = q_o[qr, hc]
        kk = jnp.concatenate([k_o[wr, hc], nseg[wr, :]], 1)
        vv = v_o[wr, hc]
        res = []
        for h in range(2):
            sel = (lane < 64) if h == 0 else (lane >= 64)
            qa = jnp.concatenate([jnp.where(sel, qp, jnp.zeros_like(qp)), oh], 1)
            p = jnp.exp2(nt(qa, kk) * C2)
            res.append((nn(p.astype(bf), vv), jnp.sum(p, 1, keepdims=True)))
        o = jnp.where(lane < 64, res[0][0], res[1][0])
        rt = jnp.where(lane < 64, res[0][1], res[1][1])
        a = o / rt
        att_o[qr, hc] = a
        ctx_o[qr, hc] = a.astype(bf)
        rt_o[qr, hc] = rt
        return 0

    lax.fori_loop(0, (R // BQ) * 6, att, 0)


def attn_fwd(x, wq, wk, wv, vec, se):
    R = x.shape[0] // 3
    S = jax.ShapeDtypeStruct
    return pl.pallas_call(
        fwd_kernel,
        out_shape=[S((R, D), bf), S((3 * R, D), bf), S((3 * R, D), bf), S((R, D), f32), S((R, D), bf), S((R, D), f32)],
        in_specs=[FULL] * 6,
        out_specs=[FULL] * 6,
        scratch_shapes=[VM((3 * R, 128), bf)],
        compiler_params=pltpu.CompilerParams(vmem_limit_bytes=VLIM),
        name="attn_fwd",
    )(x, wq, wk, wv, vec, se)


def norm(h):
    c = h - jnp.mean(h, 1, keepdims=True)
    r = lax.rsqrt(jnp.mean(c * c, 1, keepdims=True) + EPS)
    return c * r, r


def mid_kernel(x, ctx, wo, wi, wu, vec, cot, out_o, gu_o, gi_o, go_o, gv_o, cd_o, g1_o, act, dg, idel, xh1, nrm, acc, g2, od, r1s):
    R = x.shape[0]
    B = 256
    NB = R // B
    V = vecs_of(vec)

    def row(i):
        return V[i : i + 1, :]

    gv_o[...] = jnp.zeros_like(gv_o)

    def rows(i):
        return pl.ds(pl.multiple_of(i * B, B), B)

    def p1(i, _):
        r = rows(i)
        h = x[r, :].astype(f32) + nn(ctx[r, :], wo[...]) + row(2)
        xh, rr = norm(h)
        xh1[r, :] = xh
        r1s[r, :] = jnp.broadcast_to(rr, (B, 128))
        nrm[r, :] = (xh * row(4) + row(5)).astype(bf)
        return 0

    lax.fori_loop(0, NB, p1, 0)
    for j in range(4):
        cs = slice(768 * j, 768 * j + 768)
        bi = row(8 + j)

        def p2(i, _, cs=cs, bi=bi, j=j):
            r = rows(i)
            pre = nn(nrm[r, :], wi[:, cs]) + bi
            cdf = 0.5 + 0.5 * lax.erf(pre * RSQ2)
            pdf = jnp.exp(pre * pre * -0.5) * RS2PI
            a = (pre * cdf).astype(bf)
            act[r, cs] = a
            dg[r, cs] = (cdf + pre * pdf).astype(bf)
            o = nn(a, wu[cs, :])
            if j == 0:
                acc[r, :] = o
            else:
                acc[r, :] += o
            return 0

        lax.fori_loop(0, NB, p2, 0)

    def p3(i, _):
        r = rows(i)
        h = nrm[r, :].astype(f32) + acc[r, :] + row(3)
        xh, rr = norm(h)
        out_o[r, :] = (xh * row(6) + row(7)).astype(bf)
        g = cot[r, :].astype(f32)
        gv_o[6:7, :] += jnp.sum(g * xh, 0, keepdims=True)
        gv_o[7:8, :] += jnp.sum(g, 0, keepdims=True)
        e = g * row(6)
        d = rr * (e - jnp.mean(e, 1, keepdims=True) - xh * jnp.mean(e * xh, 1, keepdims=True))
        g2[r, :] = d
        db = d.astype(bf)
        od[r, :] = db
        gv_o[3:4, :] += jnp.sum(db.astype(f32), 0, keepdims=True)
        return 0

    lax.fori_loop(0, NB, p3, 0)
    for j in range(4):
        cs = slice(768 * j, 768 * j + 768)

        def p4(i, _, cs=cs, j=j):
            r = rows(i)
            d = (nt(od[r, :], wu[cs, :]) * dg[r, cs].astype(f32)).astype(bf)
            idel[r, cs] = d
            gv_o[8 + j : 9 + j, :] += jnp.sum(d.astype(f32), 0, keepdims=True)
            g2[r, :] += nt(d, wi[:, cs])
            return 0

        lax.fori_loop(0, NB, p4, 0)

    def p5(i, _):
        r = rows(i)
        g = g2[r, :]
        xh = xh1[r, :]
        rr = r1s[r, 0:1]
        gv_o[4:5, :] += jnp.sum(g * xh, 0, keepdims=True)
        gv_o[5:6, :] += jnp.sum(g, 0, keepdims=True)
        e = g * row(4)
        d = rr * (e - jnp.mean(e, 1, keepdims=True) - xh * jnp.mean(e * xh, 1, keepdims=True))
        g1_o[r, :] = d
        db = d.astype(bf)
        gv_o[2:3, :] += jnp.sum(db.astype(f32), 0, keepdims=True)
        cd_o[r, :] = nt(db, wo[...]).astype(bf)
        return 0

    lax.fori_loop(0, NB, p5, 0)
    for j in range(4):
        cs = slice(768 * j, 768 * j + 768)
        gu_o[cs, :] = tn(act[:, cs], od[...]).astype(bf)
    for j in range(4):
        cs = slice(768 * j, 768 * j + 768)
        gi_o[:, cs] = tn(nrm[...], idel[:, cs]).astype(bf)
    go_o[...] = tn(ctx[...], g1_o[...].astype(bf)).astype(bf)


def mid(x, ctx, wo, wi, wu, vec, cot):
    R = x.shape[0]
    S = jax.ShapeDtypeStruct
    F = wi.shape[1]
    return pl.pallas_call(
        mid_kernel,
        out_shape=[S((R, D), bf), S((F, D), bf), S((D, F), bf), S((D, D), bf), S((16, D), f32), S((R, D), bf), S((R, D), f32)],
        in_specs=[FULL] * 7,
        out_specs=[FULL] * 7,
        scratch_shapes=[
            VM((R, F), bf),
            VM((R, F), bf),
            VM((R, F), bf),
            VM((R, D), f32),
            VM((R, D), bf),
            VM((R, D), f32),
            VM((R, D), f32),
            VM((R, D), bf),
            VM((R, 128), f32),
        ],
        compiler_params=pltpu.CompilerParams(vmem_limit_bytes=VLIM),
        name="mid",
    )(x, ctx, wo, wi, wu, vec, cot)


def bwd_kernel(q, k, v, att, rt, cd, se, x, wq, wk, wv, g1, gvin, gx_o, hl_o, hr_o, gq_o, gk_o, gw_o, gv_o, nseg, dk, dv, dqb, dkb, dvb):
    R = q.shape[0]
    anchor = lax.axis_index("ctx") * R

    def prep(i, _):
        r = pl.ds(pl.multiple_of(i * 256, 256), 256)
        nseg[r, :] = jnp.where(member(anchor - R + i * 256, 256, se), 0.0, 1.0).astype(bf)
        dk[r, :] = jnp.zeros((256, 128), f32)
        dv[r, :] = jnp.zeros((256, 128), f32)
        return 0

    lax.fori_loop(0, 3 * R // 256, prep, 0)
    lane = lax.broadcasted_iota(jnp.int32, (BQ, 128), 1)

    def head(hp, _):
        hc = pl.ds(pl.multiple_of(hp * 128, 128), 128)
        for qb in range(R // BQ):
            qr = pl.ds(qb * BQ, BQ)
            wr = pl.ds(qb * BQ, WIN)
            oh = jnp.where(nseg[pl.ds(R + qb * BQ, BQ), :] == 0, -BIG, 0.0).astype(bf)
            qp = q[qr, hc]
            c = cd[qr, hc].astype(f32)
            rtb = rt[qr, hc]
            sd = (c / rtb).astype(bf)
            t = c * att[qr, hc] / rtb
            kp = k[wr, hc]
            vp = v[wr, hc]
            kk = jnp.concatenate([kp, nseg[wr, :]], 1)
            z = jnp.zeros_like(qp)
            dkp = []
            dvp = []
            dqs = []
            for h in range(2):
                sel = (lane < 64) if h == 0 else (lane >= 64)
                qm = jnp.where(sel, qp, z)
                sm = jnp.where(sel, sd, z)
                corr = jnp.sum(jnp.where(sel, t, 0.0), 1, keepdims=True)
                corr_row = jnp.transpose(jnp.broadcast_to(corr, (BQ, 128)), (1, 0))[0:1, :]
                p = jnp.exp2(nt(kk, jnp.concatenate([qm, oh], 1)) * C2)
                dp = nt(vp, sm)
                ds = (p * (dp - corr_row)).astype(bf)
                dvp.append(nn(p.astype(bf), sm))
                dkp.append(nn(ds, qm))
                dqs.append(tn(ds, kp))
            dk[wr, :] += dkp[0] + dkp[1]
            dv[wr, :] += dvp[0] + dvp[1]
            dqb[qr, hc] = (jnp.where(lane < 64, dqs[0], dqs[1]) * 0.125).astype(bf)

        def fin(i, _):
            r = pl.ds(pl.multiple_of(i * 256, 256), 256)
            dkb[r, hc] = (dk[r, :] * 0.125).astype(bf)
            dvb[r, hc] = dv[r, :].astype(bf)
            dk[r, :] = jnp.zeros((256, 128), f32)
            dv[r, :] = jnp.zeros((256, 128), f32)
            return 0

        lax.fori_loop(0, 3 * R // 256, fin, 0)
        return 0

    lax.fori_loop(0, 6, head, 0)
    gv_o[...] = gvin[...]
    gv_o[0:1, :] = jnp.sum(dqb[...].astype(f32), 0, keepdims=True)
    gv_o[1:2, :] = jnp.sum(dvb[...].astype(f32), 0, keepdims=True)
    own = slice(R, 2 * R)
    for dst, r in ((hl_o, slice(0, R)), (hr_o, slice(2 * R, 3 * R))):
        dst[...] = (nt(dkb[r, :], wk[...]) + nt(dvb[r, :], wv[...])).astype(bf)
    gx_o[...] = g1[...] + nt(dqb[...], wq[...]) + nt(dkb[own, :], wk[...]) + nt(dvb[own, :], wv[...])
    gq_o[...] = tn(x[own, :], dqb[...]).astype(bf)
    gk_o[...] = tn(x[...], dkb[...]).astype(bf)
    gw_o[...] = tn(x[...], dvb[...]).astype(bf)


def attn_bwd(q, k, v, att, rt, cd, se, x, wq, wk, wv, g1, gv):
    R = q.shape[0]
    S = jax.ShapeDtypeStruct
    return pl.pallas_call(
        bwd_kernel,
        out_shape=[S((R, D), f32), S((R, D), bf), S((R, D), bf)] + [S((D, D), bf)] * 3 + [S((16, D), f32)],
        in_specs=[FULL] * 13,
        out_specs=[FULL] * 7,
        scratch_shapes=[
            VM((3 * R, 128), bf),
            VM((3 * R, 128), f32),
            VM((3 * R, 128), f32),
            VM((R, D), bf),
            VM((3 * R, D), bf),
            VM((3 * R, D), bf),
        ],
        compiler_params=pltpu.CompilerParams(vmem_limit_bytes=VLIM),
        name="attn_bwd",
    )(q, k, v, att, rt, cd, se, x, wq, wk, wv, g1, gv)


PANELS = [(5, 192 * j, 0) for j in range(4)] + [(4, 0, 768 * j) for j in range(4)] + [(3, 0, 0), (2, 0, 0), (1, 0, 0), (0, 0, 0)]
ORD = (0, 1, 2)
WINDOW = 2


def extra_bits(n):
    return [1 << j for j in range(3, 16) if (1 << j) < n]


def add_rows(dst, a, b, rows, step=32):
    def body(i, _):
        r = pl.ds(pl.multiple_of(i * step, 16), step)
        dst[r, :] = (a[r, :].astype(f32) + b[r, :].astype(f32)).astype(dst.dtype)
        return 0

    lax.fori_loop(0, rows // step, body, 0)


def reduce_kernel(n, *refs):
    nt_ = 6
    g = refs[:nt_]
    vec, hl, hr = refs[nt_ : nt_ + 3]
    out = refs[nt_ + 3 : 2 * nt_ + 3]
    vout, hin = refs[2 * nt_ + 3 : 2 * nt_ + 5]
    RC, RY, RX, RZ, RW, RE, EX, ACC, VR, vacc, HR, cs, cr, ss, sr, vs, vr, hs, hrs = refs[2 * nt_ + 5 :]
    NP = len(PANELS)
    extra = extra_bits(n)
    c = lax.axis_index("ctx")
    f = lax.axis_index("fsdp")
    cb = bit(f, 1)
    yb = bit(f, 2)
    sib = (c, flip(f, 1))
    yp = (c, flip(f, 2))
    peers = [sib, yp] + [(flip(c, 1 << j), f) for j in range(3)] + [(flip(c, b), f) for b in extra]
    odd = bit(c, 1) == 1
    fwd = jnp.where(odd, c + 2, c - 2)
    src = jnp.where(odd, c - 2, c + 2)
    has_fwd = jnp.logical_and(fwd >= 0, fwd < n)
    has_src = jnp.logical_and(src >= 0, src < n)
    oth = jnp.where(bit(c, 2) == 0, c - 2, c + 2)
    has_oth = jnp.logical_and(oth >= 0, oth < n)
    greet(peers, ((has_oth, (oth, f)),))

    def quarter(k, q):
        t, r0, c0 = PANELS[k]
        SR = g[t].shape[0] // 4
        return g[t].at[pl.ds(pl.multiple_of(q * SR + r0, 16), HS), c0 : c0 + 768]

    core = [
        [remote(quarter(k, 2 * yy + (1 - cb)), RC.at[k, yy], cs.at[k, yy], cr.at[k, yy], sib) for yy in range(2)]
        for k in range(NP)
    ]
    st = []
    regs = []
    b = [bit(c, 1 << j) for j in ORD]
    p = [(flip(c, 1 << j), f) for j in ORD]
    r96 = pl.multiple_of(b[0] * 96, 16)
    r96o = pl.multiple_of((1 - b[0]) * 96, 16)
    r48 = pl.multiple_of(b[0] * 96 + b[1] * 48, 16)
    r48o = pl.multiple_of(b[0] * 96 + (1 - b[1]) * 48, 16)
    cc = pl.multiple_of(b[2] * 384, 128)
    cco = pl.multiple_of((1 - b[2]) * 384, 128)
    for k in range(NP):
        a = ACC.at[k]

        def s(i, k=k):
            return (ss.at[k, i], sr.at[k, i])

        keep1 = a.at[pl.ds(r96, 96)]
        give1 = a.at[pl.ds(r96o, 96)]
        keep2 = a.at[pl.ds(r48, 48)]
        give2 = a.at[pl.ds(r48o, 48)]
        keep3 = a.at[pl.ds(r48, 48), pl.ds(cc, 384)]
        give3 = a.at[pl.ds(r48, 48), pl.ds(cco, 384)]
        t, r0, c0 = PANELS[k]
        res3 = out[t].at[pl.ds(pl.multiple_of(r0 + r48, 16), 48), pl.ds(pl.multiple_of(c0 + cc, 128), 384)]
        res2 = out[t].at[pl.ds(pl.multiple_of(r0 + r48, 16), 48), c0 : c0 + 768]
        res1 = out[t].at[pl.ds(pl.multiple_of(r0 + r96, 16), 96), c0 : c0 + 768]
        st.append(
            [
                remote(RC.at[k, 1 - yb], RY.at[k], *s(0), yp),
                remote(give1, RX.at[k], *s(1), p[0]),
                remote(give2, RZ.at[k], *s(2), p[1]),
                remote(give3, RW.at[k], *s(3), p[2]),
                remote(res3, res3, *s(4), p[2]),
                remote(res2, res2, *s(5), p[1]),
                remote(res1, res1, *s(6), p[0]),
            ]
            + [remote(EX.at[k, i], RE.at[k, i], *s(7 + i), (flip(c, e), f)) for i, e in enumerate(extra)]
        )
        regs.append((keep1, keep2, keep3, res3))
    hfl = remote(hl, HR.at[0], hs.at[0], hrs.at[0], (fwd, f))
    hfr = remote(hr, HR.at[0], hs.at[0], hrs.at[0], (fwd, f))
    hx = remote(HR.at[1], hin, hs.at[1], hrs.at[1], p[0])

    @pl.when(jnp.logical_and(has_fwd, odd))
    def _():
        hfr.start()

    @pl.when(jnp.logical_and(has_fwd, jnp.logical_not(odd)))
    def _():
        hfl.start()

    for k in range(NP):
        for yy in range(2):
            core[k][yy].start()
    vacc[0] = vec[...]
    vcp = [remote(vacc.at[i], VR.at[i], vs.at[i], vr.at[i], d) for i, d in enumerate(peers)]

    def s1(k):
        for yy in range(2):
            core[k][yy].wait_recv()
        for yy in range(2):
            add_rows(RC.at[k, yy], RC.at[k, yy], quarter(k, 2 * yy + cb), HS)
        if k < WINDOW:
            st[k][0].start()

    def s2(k):
        st[k][0].wait_recv()
        if k + WINDOW < NP:
            st[k + WINDOW][0].start()
        add_rows(ACC.at[k], RC.at[k, yb], RY.at[k], HS)
        st[k][1].start()

    def s3(k):
        st[k][1].wait_recv()
        add_rows(regs[k][0], regs[k][0], RX.at[k], 96)
        st[k][2].start()

    def s4(k):
        st[k][2].wait_recv()
        add_rows(regs[k][1], regs[k][1], RZ.at[k], 48, 16)
        st[k][3].start()

    def s5(k):
        st[k][3].wait_recv()
        last = regs[k][2]
        for i in range(len(extra)):
            add_rows(EX.at[k, i], last, RW.at[k] if i == 0 else RE.at[k, i - 1], 48, 16)
            last = EX.at[k, i]
            st[k][7 + i].start()
            st[k][7 + i].wait_recv()
        add_rows(regs[k][3], last, RE.at[k, len(extra) - 1] if extra else RW.at[k], 48, 16)
        st[k][4].start()

    def s6(k):
        st[k][4].wait_recv()
        st[k][5].start()

    def s7(k):
        st[k][5].wait_recv()
        st[k][6].start()

    def s8(k):
        st[k][6].wait_recv()
        for cp in st[k]:
            cp.wait_send()
        for yy in range(2):
            core[k][yy].wait_send()

    for k in range(NP):
        s1(k)

    H1 = HR.at[1]

    @pl.when(odd)
    def _():
        H1[...] = hl[...]

    @pl.when(jnp.logical_not(odd))
    def _():
        H1[...] = hr[...]

    @pl.when(has_src)
    def _():
        hfl.wait_recv()
        add_rows(H1, H1, HR.at[0], H1.shape[0])

    hx.start()
    stages = [s2, s3, s4, s5, s6, s7, s8]
    vstep = 0
    for step in range(NP + len(stages) - 1):
        for i in reversed(range(len(stages))):
            k = step - i
            if 0 <= k < NP:
                stages[i](k)
        if vstep <= len(peers):
            if vstep > 0:
                vcp[vstep - 1].wait()
                vacc[vstep] = vacc[vstep - 1] + VR[vstep - 1]
            if vstep < len(peers):
                vcp[vstep].start()
            vstep += 1
    vout[...] = vacc[len(peers)]
    hx.wait()

    @pl.when(has_fwd)
    def _():
        hfl.wait_send()


def reduce_grads(n, grads, vec, hl, hr, odt):
    nt_ = len(grads)
    NP = len(PANELS)
    ne = len(extra_bits(n))
    nv = 5 + ne
    S = jax.ShapeDtypeStruct
    outs = [S((s.shape[0] // 4, s.shape[1]), odt) for s in grads] + [S(vec.shape, f32), S(hl.shape, bf)]
    return pl.pallas_call(
        functools.partial(reduce_kernel, n),
        out_shape=outs,
        in_specs=[FULL] * (nt_ + 3),
        out_specs=[FULL] * (nt_ + 2),
        scratch_shapes=[
            VM((NP, 2, HS, D), bf),
            VM((NP, HS, D), bf),
            VM((NP, 96, D), bf),
            VM((NP, 48, D), bf),
            VM((NP, 48, 384), bf),
            VM((NP, max(ne, 1), 48, 384), bf),
            VM((NP, max(ne, 1), 48, 384), bf),
            VM((NP, HS, D), bf),
            VM((nv,) + vec.shape, f32),
            VM((nv + 1,) + vec.shape, f32),
            VM((2,) + hl.shape, bf),
            DMA((NP, 2)),
            DMA((NP, 2)),
            DMA((NP, 7 + ne)),
            DMA((NP, 7 + ne)),
            DMA((nv,)),
            DMA((nv,)),
            DMA((2,)),
            DMA((2,)),
        ],
        compiler_params=pltpu.CompilerParams(collective_id=2, has_side_effects=True, vmem_limit_bytes=VLIM),
        name="reduce",
    )(*grads, vec, hl, hr)


def local(n, tokens, doc_lengths, cotangent, wq, wk, wv, wo, wi, wu, bq, bv, bo, bi, bu, ga, sa, gf, sf):
    f = lax.axis_index("fsdp")
    x = tokens[0]
    lengths = doc_lengths[0]
    docs = lengths.shape[0]
    assert docs <= 128 and x.shape[0] == 512
    ends = jnp.cumsum(lengths)
    se = jnp.zeros((8, 128), jnp.int32)
    se = se.at[0, :docs].set(ends - lengths).at[1, :docs].set(ends)
    small = jnp.stack([bq, bv, bo, bu, ga, sa, gf, sf])
    w = small.shape[1]
    vec = jnp.zeros((16, D), bf)
    vec = lax.dynamic_update_slice(vec, small, (0, f * w))
    vec = lax.dynamic_update_slice(vec, bi[None], (8 + f, 0))
    xe, wq, wk, wv, wo, wi, wu, vec = gather(n, x, (wq, wk, wv, wo, wi, wu), vec)
    q, k, v, att, ctx, rt = attn_fwd(xe, wq, wk, wv, vec, se)
    layer_out, gu, gi, go, gv, cd, g1 = mid(x, ctx, wo, wi, wu, vec, cotangent[0])
    gx, hl, hr, gq, gk, gw, gv = attn_bwd(q, k, v, att, rt, cd, se, xe, wq, wk, wv, g1, gv)
    *gw6, gv, hin = reduce_grads(n, (gq, gk, gw, go, gi, gu), gv, hl, hr, bf)
    grads = [t.astype(f32) for t in gw6]
    gs = lax.dynamic_slice(gv, (0, f * w), (8, w))
    gbi = lax.dynamic_slice(gv, (8 + f, 0), (1, D))[0]
    grad_tokens = gx + hin.astype(f32)
    return (layer_out[None], grad_tokens[None], *grads, gs[0], gs[1], gs[2], gbi, gs[3], gs[4], gs[5], gs[6], gs[7])


def solution(mesh):
    n = mesh.shape["ctx"]
    tok = P("fsdp", "ctx", None)
    mat = P("fsdp", None)
    vec = P("fsdp")
    return jax.shard_map(
        functools.partial(local, n),
        mesh=mesh,
        in_specs=(tok, mat, tok) + (mat,) * 6 + (vec,) * 9,
        out_specs=(tok, tok) + (mat,) * 6 + (vec,) * 9,
        check_vma=False,
    )
```

```python
import functools

import jax
import jax.numpy as jnp
from jax import lax
from jax.experimental import pallas as pl
from jax.experimental.pallas import tpu as pltpu
from jax.sharding import PartitionSpec as P

bf = jnp.bfloat16
f32 = jnp.float32
MESH = pl.DeviceIdType.MESH
VM = pltpu.VMEM
DMA = pltpu.SemaphoreType.DMA
D = 768
EPS = 1e-12
BIG = 1e30
C2 = 0.125 * 1.4426950408889634
RSQ2 = 0.7071067811865476
RS2PI = 0.3989422804014327
BQ = 256
WIN = BQ + 1024
TOKP = 4
HS = 192
VLIM = 58 * 2**20
FULL = pl.BlockSpec(memory_space=pltpu.VMEM)


def nt(a, b):
    return lax.dot_general(a, b, (((1,), (1,)), ((), ())), preferred_element_type=f32)


def nn(a, b):
    return lax.dot_general(a, b, (((1,), (0,)), ((), ())), preferred_element_type=f32)


def tn(a, b):
    return lax.dot_general(a, b, (((0,), (0,)), ((), ())), preferred_element_type=f32)


def bit(i, b):
    return lax.rem(lax.div(i, b), 2)


def flip(i, b):
    return i + b * (1 - 2 * bit(i, b))


def remote(src, dst, send, recv, device):
    return pltpu.make_async_remote_copy(
        src_ref=src, dst_ref=dst, send_sem=send, recv_sem=recv, device_id=device, device_id_type=MESH
    )


def greet(peers, others):
    bar = pltpu.get_barrier_semaphore()
    for d in peers:
        pl.semaphore_signal(bar, inc=1, device_id=d, device_id_type=MESH)
    for cond, d in others:

        @pl.when(cond)
        def _():
            pl.semaphore_signal(bar, inc=1, device_id=d, device_id_type=MESH)

    pl.semaphore_wait(bar, len(peers) + sum(cond.astype(jnp.int32) for cond, _ in others))


PIECES = [(0, 0, 192, 0, 768, 2), (1, 0, 192, 0, 768, 2), (2, 0, 192, 0, 768, 2), (3, 0, 192, 0, 768, 1)]
PIECES += [(4, 0, 192, 768 * j, 768, 1 if j < 3 else 2) for j in range(4)]
PIECES += [(5, 192 * j, 192, 0, 768, 1 if j in (1, 3) else 2) for j in range(4)]


def gather_kernel(n, *refs):
    nt_ = 6
    tok = refs[0]
    sh = refs[1 : 1 + nt_]
    vec = refs[1 + nt_]
    tok_o = refs[2 + nt_]
    full = refs[3 + nt_ : 3 + 2 * nt_]
    vec_o = refs[3 + 2 * nt_]
    ts, tr, ws, wr, vs, vr = refs[4 + 2 * nt_ :]
    c = lax.axis_index("ctx")
    f = lax.axis_index("fsdp")
    sib = (c, flip(f, 1))
    yp = (c, flip(f, 2))
    dg = (c, flip(flip(f, 1), 2))
    c1 = (flip(c, 1), f)
    c2 = (flip(c, 2), f)
    even = bit(c, 1) == 0
    fwd = jnp.where(even, c + 2, c - 2)
    src = jnp.where(even, c - 2, c + 2)
    has_fwd = jnp.logical_and(fwd >= 0, fwd < n)
    has_src = jnp.logical_and(src >= 0, src < n)
    oth = jnp.where(bit(c, 2) == 0, c - 2, c + 2)
    has_oth = jnp.logical_and(oth >= 0, oth < n)
    greet((sib, yp, dg, c1, c2), ((has_oth, (oth, f)),))
    rows = tok.shape[0]
    pr = rows // TOKP
    pslot = jnp.where(even, 2 * rows, 0)
    dslot = jnp.where(even, 0, 2 * rows)
    fslot = jnp.where(even, 0, 2 * rows)
    tcp = [
        remote(
            tok.at[pl.ds(i * pr, pr)],
            tok_o.at[pl.ds(pl.multiple_of(dslot + i * pr, pr), pr)],
            ts.at[0, i],
            tr.at[0, i],
            c1,
        )
        for i in range(TOKP)
    ]
    vcp = [remote(vec, vec_o.at[f], vs.at[i], vr.at[i], (sib, yp, dg)[i]) for i in range(3)]
    wcp = []
    fy = flip(f, 2)
    for k, (t, r0, R, c0, C, route) in enumerate(PIECES):
        s = sh[t]
        w = full[t]
        SR = s.shape[0]
        H = R // 2
        p = c1 if route == 1 else c2
        hb = bit(c, route)
        cs = slice(c0, c0 + C)
        own = pl.multiple_of(f * SR + r0, 16)
        mine = pl.multiple_of(f * SR + r0 + hb * H, 16)
        gy = pl.multiple_of(fy * SR + r0 + hb * H, 16)
        gx = pl.multiple_of(fy * SR + r0 + (1 - hb) * H, 16)
        wcp.append(
            [
                remote(s.at[pl.ds(r0, R), cs], w.at[pl.ds(own, R), cs], ws.at[k, 0], wr.at[k, 0], sib),
                remote(
                    s.at[pl.ds(pl.multiple_of(r0 + hb * H, 16), H), cs],
                    w.at[pl.ds(mine, H), cs],
                    ws.at[k, 1],
                    wr.at[k, 1],
                    yp,
                ),
                remote(w.at[pl.ds(gy, H), cs], w.at[pl.ds(gy, H), cs], ws.at[k, 2], wr.at[k, 2], p),
                remote(w.at[pl.ds(gy, H), cs], w.at[pl.ds(gy, H), cs], ws.at[k, 3], wr.at[k, 3], sib),
                remote(w.at[pl.ds(gx, H), cs], w.at[pl.ds(gx, H), cs], ws.at[k, 4], wr.at[k, 4], sib),
            ]
        )
    NP = len(PIECES)
    for t in tcp:
        t.start()
    for k in range(NP):
        wcp[k][1].start()
    for v in vcp:
        v.start()
    for k in range(NP):
        wcp[k][0].start()
    for k in range(nt_):
        R = sh[k].shape[0]
        full[k][pl.ds(pl.multiple_of(f * R, 16), R), :] = sh[k][...]
    tok_o[pl.ds(rows, rows), :] = tok[...]
    vec_o[f] = vec[...]

    @pl.when(jnp.logical_not(has_src))
    def _():
        tok_o[pl.ds(pl.multiple_of(fslot, rows), rows), :] = jnp.zeros((rows, D), bf)

    tfw = [
        remote(
            tok_o.at[pl.ds(pl.multiple_of(pslot + i * pr, pr), pr)],
            tok_o.at[pl.ds(pl.multiple_of(fslot + i * pr, pr), pr)],
            ts.at[1, i],
            tr.at[1, i],
            (fwd, f),
        )
        for i in range(TOKP)
    ]

    def ystep(k):
        wcp[k][1].wait_recv()
        wcp[k][2].start()
        wcp[k][3].start()

    def xstep(k):
        wcp[k][2].wait_recv()
        wcp[k][4].start()

    def tstep(i):
        tcp[i].wait_recv()

        @pl.when(has_fwd)
        def _():
            tfw[i].start()

    seq = [(ystep, 0), (tstep, 0), (ystep, 1), (tstep, 1), (ystep, 2), (xstep, 0), (tstep, 2)]
    seq += [(ystep, 3), (xstep, 1), (xstep, 2), (tstep, 3), (ystep, 4), (xstep, 3)]
    for k in range(5, NP):
        seq += [(ystep, k), (xstep, k - 1)]
    seq += [(xstep, NP - 1)]
    for step, k in seq:
        step(k)
    for i in range(TOKP):

        @pl.when(has_src)
        def _():
            tfw[i].wait_recv()

        @pl.when(has_fwd)
        def _():
            tfw[i].wait_send()

        tcp[i].wait_send()
    for k in range(NP):
        for i in (0, 3, 4):
            wcp[k][i].wait_recv()
        for cp in wcp[k]:
            cp.wait_send()
    for v in vcp:
        v.wait()


def gather(n, tokens, shards, vec):
    nt_ = len(shards)
    rows = tokens.shape[0]
    NP = len(PIECES)
    S = jax.ShapeDtypeStruct
    outs = [S((3 * rows, D), bf)]
    outs += [S((4 * s.shape[0], s.shape[1]), bf) for s in shards]
    outs += [S((4,) + vec.shape, bf)]
    return pl.pallas_call(
        functools.partial(gather_kernel, n),
        out_shape=outs,
        in_specs=[FULL] * (nt_ + 2),
        out_specs=[FULL] * (nt_ + 2),
        scratch_shapes=[DMA((2, TOKP)), DMA((2, TOKP)), DMA((NP, 5)), DMA((NP, 5)), DMA((3,)), DMA((3,))],
        compiler_params=pltpu.CompilerParams(collective_id=1, has_side_effects=True, vmem_limit_bytes=VLIM),
        name="gather",
    )(tokens, *shards, vec)


def vecs_of(vec):
    return (vec[0].astype(f32) + vec[1].astype(f32)) + (vec[2].astype(f32) + vec[3].astype(f32))


def member(pos0, rows, se):
    pos = pos0 + lax.broadcasted_iota(jnp.int32, (rows, 128), 0)
    return jnp.logical_and(pos >= se[0:1, :], pos < se[1:2, :])


def fwd_kernel(x, wq, wk, wv, vec, se, q_o, k_o, v_o, ctx_o, rt_o, nseg):
    R = x.shape[0] // 3
    anchor = lax.axis_index("ctx") * R
    V = vecs_of(vec)
    bq = V[0:1, :]
    bv = V[1:2, :]

    def proj(i, _):
        r = pl.ds(pl.multiple_of(i * 256, 256), 256)
        xb = x[r, :]
        k_o[r, :] = nn(xb, wk[...]).astype(bf)
        v_o[r, :] = (nn(xb, wv[...]) + bv).astype(bf)
        m = member(anchor - R + i * 256, 256, se)
        nseg[r, :] = jnp.where(m, 0.0, 1.0).astype(bf)
        return 0

    lax.fori_loop(0, 3 * R // 256, proj, 0)

    def projq(i, _):
        r = pl.ds(pl.multiple_of(R + i * 256, 256), 256)
        q_o[pl.ds(pl.multiple_of(i * 256, 256), 256), :] = (nn(x[r, :], wq[...]) + bq).astype(bf)
        return 0

    lax.fori_loop(0, R // 256, projq, 0)
    lane = lax.broadcasted_iota(jnp.int32, (BQ, 128), 1)

    def att(i, _):
        qb = lax.div(i, 6)
        hp = lax.rem(i, 6)
        qr = pl.ds(pl.multiple_of(qb * BQ, BQ), BQ)
        wr = pl.ds(pl.multiple_of(qb * BQ, BQ), WIN)
        hc = pl.ds(pl.multiple_of(hp * 128, 128), 128)
        oh = jnp.where(nseg[pl.ds(pl.multiple_of(R + qb * BQ, BQ), BQ), :] == 0, -BIG, 0.0).astype(bf)
        qp = q_o[qr, hc]
        kk = jnp.concatenate([k_o[wr, hc], nseg[wr, :]], 1)
        vv = v_o[wr, hc]
        res = []
        for h in range(2):
            sel = (lane < 64) if h == 0 else (lane >= 64)
            qa = jnp.concatenate([jnp.where(sel, qp, jnp.zeros_like(qp)), oh], 1)
            p = jnp.exp2(nt(qa, kk) * C2)
            res.append((nn(p.astype(bf), vv), jnp.sum(p, 1, keepdims=True)))
        o = jnp.where(lane < 64, res[0][0], res[1][0])
        rt = jnp.where(lane < 64, res[0][1], res[1][1])
        a = o / rt
        ctx_o[qr, hc] = a.astype(bf)
        rt_o[qr, hc] = rt
        return 0

    lax.fori_loop(0, (R // BQ) * 6, att, 0)


def attn_fwd(x, wq, wk, wv, vec, se):
    R = x.shape[0] // 3
    S = jax.ShapeDtypeStruct
    return pl.pallas_call(
        fwd_kernel,
        out_shape=[S((R, D), bf), S((3 * R, D), bf), S((3 * R, D), bf), S((R, D), bf), S((R, D), f32)],
        in_specs=[FULL] * 6,
        out_specs=[FULL] * 5,
        scratch_shapes=[VM((3 * R, 128), bf)],
        compiler_params=pltpu.CompilerParams(vmem_limit_bytes=VLIM),
        name="attn_fwd",
    )(x, wq, wk, wv, vec, se)


def norm(h):
    c = h - jnp.mean(h, 1, keepdims=True)
    r = lax.rsqrt(jnp.mean(c * c, 1, keepdims=True) + EPS)
    return c * r, r


def mid_kernel(x, ctx, rt, wo, wi, wu, vec, cot, out_o, act, idel, od, nrm, ad_o, gv_o, sd_o, ct_o, g1_o, dg, xh1, acc, g2, r1s):
    R = x.shape[0]
    B = 256
    NB = R // B
    V = vecs_of(vec)

    def row(i):
        return V[i : i + 1, :]

    gv_o[...] = jnp.zeros_like(gv_o)

    def rows(i, j=0):
        return pl.ds(pl.multiple_of(j * R + i * B, B), B)

    def p1(i, _):
        r = rows(i)
        h = x[r, :].astype(f32) + nn(ctx[r, :], wo[...]) + row(2)
        xh, rr = norm(h)
        xh1[r, :] = xh
        r1s[r, :] = jnp.broadcast_to(rr, (B, 128))
        nrm[r, :] = (xh * row(4) + row(5)).astype(bf)
        return 0

    lax.fori_loop(0, NB, p1, 0)
    for j in range(4):
        cs = slice(768 * j, 768 * j + 768)
        bi = row(8 + j)

        def p2(i, _, cs=cs, bi=bi, j=j):
            r = rows(i)
            rj = rows(i, j)
            pre = nn(nrm[r, :], wi[:, cs]) + bi
            cdf = 0.5 + 0.5 * lax.erf(pre * RSQ2)
            pdf = jnp.exp(pre * pre * -0.5) * RS2PI
            a = (pre * cdf).astype(bf)
            act[rj, :] = a
            dg[rj, :] = (cdf + pre * pdf).astype(bf)
            o = nn(a, wu[cs, :])
            if j == 0:
                acc[r, :] = o
            else:
                acc[r, :] += o
            return 0

        lax.fori_loop(0, NB, p2, 0)

    def p3(i, _):
        r = rows(i)
        h = nrm[r, :].astype(f32) + acc[r, :] + row(3)
        xh, rr = norm(h)
        out_o[r, :] = (xh * row(6) + row(7)).astype(bf)
        g = cot[r, :].astype(f32)
        gv_o[6:7, :] += jnp.sum(g * xh, 0, keepdims=True)
        gv_o[7:8, :] += jnp.sum(g, 0, keepdims=True)
        e = g * row(6)
        d = rr * (e - jnp.mean(e, 1, keepdims=True) - xh * jnp.mean(e * xh, 1, keepdims=True))
        g2[r, :] = d
        db = d.astype(bf)
        od[r, :] = db
        gv_o[3:4, :] += jnp.sum(db.astype(f32), 0, keepdims=True)
        return 0

    lax.fori_loop(0, NB, p3, 0)
    for j in range(4):
        cs = slice(768 * j, 768 * j + 768)

        def p4(i, _, cs=cs, j=j):
            r = rows(i)
            rj = rows(i, j)
            d = (nt(od[r, :], wu[cs, :]) * dg[rj, :].astype(f32)).astype(bf)
            idel[rj, :] = d
            gv_o[8 + j : 9 + j, :] += jnp.sum(d.astype(f32), 0, keepdims=True)
            g2[r, :] += nt(d, wi[:, cs])
            return 0

        lax.fori_loop(0, NB, p4, 0)
    heads = lax.broadcasted_iota(jnp.int32, (16, D), 0)
    onehot = jnp.where(lax.div(lax.broadcasted_iota(jnp.int32, (16, D), 1), 64) == heads, 1.0, 0.0)
    for i in range(NB):
        r = slice(i * B, i * B + B)
        g = g2[r, :]
        xh = xh1[r, :]
        rr = r1s[r, 0:1]
        gv_o[4:5, :] += jnp.sum(g * xh, 0, keepdims=True)
        gv_o[5:6, :] += jnp.sum(g, 0, keepdims=True)
        e = g * row(4)
        d = rr * (e - jnp.mean(e, 1, keepdims=True) - xh * jnp.mean(e * xh, 1, keepdims=True))
        g1_o[r, :] = d
        db = d.astype(bf)
        ad_o[r, :] = db
        gv_o[2:3, :] += jnp.sum(db.astype(f32), 0, keepdims=True)
        cd = nt(db, wo[...]).astype(bf).astype(f32)
        inv = 1.0 / rt[r, :]
        sc = cd * inv
        sd_o[r, :] = sc.astype(bf)
        t = sc * ctx[r, :].astype(f32)
        ct_o[:, r] = lax.dot_general(
            onehot, t, (((1,), (1,)), ((), ())), preferred_element_type=f32, precision=lax.Precision.HIGHEST
        )


def mid(x, ctx, rt, wo, wi, wu, vec, cot):
    R = x.shape[0]
    S = jax.ShapeDtypeStruct
    return pl.pallas_call(
        mid_kernel,
        out_shape=[
            S((R, D), bf),
            S((4 * R, D), bf),
            S((4 * R, D), bf),
            S((R, D), bf),
            S((R, D), bf),
            S((R, D), bf),
            S((16, D), f32),
            S((R, D), bf),
            S((16, R), f32),
            S((R, D), f32),
        ],
        in_specs=[FULL] * 8,
        out_specs=[FULL] * 10,
        scratch_shapes=[VM((4 * R, D), bf), VM((R, D), f32), VM((R, D), f32), VM((R, D), f32), VM((R, 128), f32)],
        compiler_params=pltpu.CompilerParams(vmem_limit_bytes=VLIM),
        name="mid",
    )(x, ctx, rt, wo, wi, wu, vec, cot)


NP = 12
WINDOW = 2
LATE = 9


def extra_bits(n):
    return [1 << j for j in range(3, 16) if (1 << j) < n]


def add_rows(dst, a, b, rows, step=48):
    def body(i, _):
        r = pl.ds(pl.multiple_of(i * step, 16), step)
        dst[r, :] = a[r, :] + b[r, :]
        return 0

    lax.fori_loop(0, rows // step, body, 0)


def back_kernel(n, *refs):
    hbm = refs[:14]
    gvin, ct, se = refs[14:17]
    OUT, vout, hin, gx_o = refs[17:21]
    bufs = refs[21:32]
    A, od, nrm, I, ctx, ad, q, k_, v_, sd, xe = bufs
    wq = k_.at[pl.ds(0, D)]
    wk = v_.at[pl.ds(0, D)]
    wv = v_.at[pl.ds(D, D)]
    bufs = bufs + (wq, wk, wv)
    G, RC, RY, RX, RZ, RW, RE, VR, vacc, HR, nseg, dk, dv = refs[32:45]
    ld, cs, cr, ss, sr, vs, vr, hs, hrs = refs[45:]
    dqb = q
    R = q.shape[0]
    extra = extra_bits(n)
    c = lax.axis_index("ctx")
    f = lax.axis_index("fsdp")
    cb = bit(f, 1)
    yb = bit(f, 2)
    sib = (c, flip(f, 1))
    yp = (c, flip(f, 2))
    p = [(flip(c, 1 << j), f) for j in range(3)]
    peers = [sib, yp] + p + [(flip(c, b), f) for b in extra]
    odd = bit(c, 1) == 1
    fwd = jnp.where(odd, c + 2, c - 2)
    src = jnp.where(odd, c - 2, c + 2)
    has_fwd = jnp.logical_and(fwd >= 0, fwd < n)
    has_src = jnp.logical_and(src >= 0, src < n)
    oth = jnp.where(bit(c, 2) == 0, c - 2, c + 2)
    has_oth = jnp.logical_and(oth >= 0, oth < n)
    loads = [pltpu.make_async_copy(hbm[i], bufs[i], ld.at[i]) for i in range(14)]
    for cp in loads[:10]:
        cp.start()
    greet(peers, ((has_oth, (oth, f)),))
    loads[10].start()

    b = [bit(c, 1 << j) for j in range(3)]
    r96 = pl.multiple_of(b[0] * 96, 16)
    r96o = pl.multiple_of((1 - b[0]) * 96, 16)
    r48 = pl.multiple_of(b[0] * 96 + b[1] * 48, 16)
    r48o = pl.multiple_of(b[0] * 96 + (1 - b[1]) * 48, 16)
    cc = pl.multiple_of(b[2] * 384, 128)
    cco = pl.multiple_of((1 - b[2]) * 384, 128)

    def core(k, yy):
        return remote(G.at[k, 2 * yy + (1 - cb)], RC.at[k, yy], cs.at[k, yy], cr.at[k, yy], sib)

    def acc(k):
        return G.at[k, 2 * yb + cb]

    def spare(k, i):
        return RY.at[k, pl.ds(48 * (i % 4), 48), 384 * (i // 4) : 384 * (i // 4) + 384]

    def copy(k, i):
        a = acc(k)
        s = (ss.at[k, i], sr.at[k, i])
        if i == 0:
            return remote(G.at[k, 2 * (1 - yb) + cb], RY.at[k], *s, yp)
        if i == 1:
            return remote(a.at[pl.ds(r96o, 96)], RX.at[k], *s, p[0])
        if i == 2:
            return remote(a.at[pl.ds(r48o, 48)], RZ.at[k], *s, p[1])
        if i == 3:
            return remote(a.at[pl.ds(r48, 48), pl.ds(cco, 384)], RW.at[k], *s, p[2])
        if i == 4:
            o = OUT.at[k, pl.ds(r48, 48), pl.ds(cc, 384)]
            return remote(o, o, *s, p[2])
        if i == 5:
            o = OUT.at[k, pl.ds(r48, 48)]
            return remote(o, o, *s, p[1])
        if i == 6:
            o = OUT.at[k, pl.ds(r96, 96)]
            return remote(o, o, *s, p[0])
        e = extra[i - 7]
        return remote(spare(k, i - 7), RE.at[k, i - 7], *s, (flip(c, e), f))

    def give(k):
        for yy in range(2):
            core(k, yy).start()

    def s1(k):
        for yy in range(2):
            core(k, yy).wait_recv()
        for yy in range(2):
            g = G.at[k, 2 * yy + cb]
            add_rows(g, g, RC.at[k, yy], 192)

    def s2(k):
        copy(k, 0).wait_recv()
        if isinstance(k, int):
            if k + WINDOW < LATE:
                copy(k + WINDOW, 0).start()
        else:

            @pl.when(k + WINDOW < LATE)
            def _():
                copy(k + WINDOW, 0).start()

        add_rows(acc(k), acc(k), RY.at[k], 192)
        copy(k, 1).start()

    def s3(k):
        copy(k, 1).wait_recv()
        a = acc(k).at[pl.ds(r96, 96)]
        add_rows(a, a, RX.at[k], 96)
        copy(k, 2).start()

    def s4(k):
        copy(k, 2).wait_recv()
        a = acc(k).at[pl.ds(r48, 48)]
        add_rows(a, a, RZ.at[k], 48)
        copy(k, 3).start()

    def s5(k):
        copy(k, 3).wait_recv()
        last = acc(k).at[pl.ds(r48, 48), pl.ds(cc, 384)]
        got = RW.at[k]
        for i in range(len(extra)):
            add_rows(spare(k, i), last, got, 48)
            copy(k, 7 + i).start()
            copy(k, 7 + i).wait_recv()
            last = spare(k, i)
            got = RE.at[k, i]
        add_rows(OUT.at[k, pl.ds(r48, 48), pl.ds(cc, 384)], last, got, 48)
        copy(k, 4).start()

    def s6(k):
        copy(k, 4).wait_recv()
        copy(k, 5).start()

    def s7(k):
        copy(k, 5).wait_recv()
        copy(k, 6).start()

    def s8(k):
        copy(k, 6).wait_recv()

    stages = (s2, s3, s4, s5, s6, s7, s8)

    def tick(t):
        for i in reversed(range(len(stages))):
            k = t - i
            if isinstance(t, int):
                if 0 <= k < NP:
                    stages[i](k)
            else:

                @pl.when(jnp.logical_and(k >= 0, k < NP))
                def _():
                    stages[i](k)

    def outer(hh, qq):
        g = tn(A[pl.ds(pl.multiple_of(qq * R, R), R), 384 * hh : 384 * hh + 384], od[...]).astype(bf)
        G[2 * hh, qq] = g[:192]
        G[2 * hh + 1, qq] = g[192:]

    loads[0].wait()
    loads[1].wait()
    for hh in range(2):
        for yy in range(2):
            outer(hh, 2 * yy + (1 - cb))
        give(2 * hh)
        give(2 * hh + 1)
        for yy in range(2):
            outer(hh, 2 * yy + cb)
    for k in range(2):
        s1(k)
        copy(k, 0).start()
    loads[2].wait()
    loads[3].wait()
    for j in range(4):
        G[4 + j] = tn(nrm[...], I[R * j : R * j + R, :]).astype(bf).reshape(4, 192, D)
        give(4 + j)
        if j < 2:
            s1(2 + j)
    s1(4)
    loads[4].wait()
    loads[5].wait()
    G[8] = tn(ctx[...], ad[...]).astype(bf).reshape(4, 192, D)
    give(8)
    for k in (5, 6, 7):
        s1(k)
    tick(0)
    s1(8)

    anchor = c * R

    def prep(i, _):
        r = pl.ds(pl.multiple_of(i * 256, 256), 256)
        nseg[r, :] = jnp.where(member(anchor - R + i * 256, 256, se), 0.0, 1.0).astype(bf)
        dk[r, :] = jnp.zeros((256, 128), f32)
        dv[r, :] = jnp.zeros((256, 128), f32)
        return 0

    lax.fori_loop(0, 3 * R // 256, prep, 0)
    lane = lax.broadcasted_iota(jnp.int32, (BQ, 128), 1)
    nqb = R // BQ
    for i in range(6, 10):
        loads[i].wait()

    def head(i, _):
        hp = lax.div(i, nqb)
        qb = lax.rem(i, nqb)
        hc = pl.ds(pl.multiple_of(hp * 128, 128), 128)
        qr = pl.ds(pl.multiple_of(qb * BQ, BQ), BQ)
        wr = pl.ds(pl.multiple_of(qb * BQ, BQ), WIN)
        oh = jnp.where(nseg[pl.ds(pl.multiple_of(R + qb * BQ, BQ), BQ), :] == 0, -BIG, 0.0).astype(bf)
        qp = q[qr, hc]
        sp = sd[qr, hc]
        kp = k_[wr, hc]
        vp = v_[wr, hc]
        kk = jnp.concatenate([kp, nseg[wr, :]], 1)
        z = jnp.zeros_like(qp)
        dkp = []
        dvp = []
        dqs = []
        for h in range(2):
            sel = (lane < 64) if h == 0 else (lane >= 64)
            qm = jnp.where(sel, qp, z)
            sm = jnp.where(sel, sp, z)
            pr = jnp.exp2(nt(kk, jnp.concatenate([qm, oh], 1)) * C2)
            dp = nt(vp, sm)
            ds = (pr * (dp - ct[pl.ds(2 * hp + h, 1), qr])).astype(bf)
            dvp.append(nn(pr.astype(bf), sm))
            dkp.append(nn(ds, qm))
            dqs.append(tn(ds, kp))
        dk[wr, :] += dkp[0] + dkp[1]
        dv[wr, :] += dvp[0] + dvp[1]
        dqb[qr, hc] = (jnp.where(lane < 64, dqs[0], dqs[1]) * 0.125).astype(bf)

        @pl.when(qb == nqb - 1)
        def _():
            def fin(j, _):
                r = pl.ds(pl.multiple_of(j * 256, 256), 256)
                A[r, hc] = (dk[r, :] * 0.125).astype(bf)
                I[r, hc] = dv[r, :].astype(bf)
                dk[r, :] = jnp.zeros((256, 128), f32)
                dv[r, :] = jnp.zeros((256, 128), f32)
                return 0

            lax.fori_loop(0, 3 * R // 256, fin, 0)

        @pl.when(lax.rem(i, 3) == 2)
        def _():
            tick(lax.div(i, 3) + 1)

        return 0

    lax.fori_loop(0, 6 * nqb, head, 0)
    t = 2 * nqb + 1

    W3 = 3 * R
    own = slice(R, 2 * R)
    for cp in loads[11:]:
        cp.start()
    loads[10].wait()
    vacc[0] = gvin[...]
    vacc[0, 0:1, :] = jnp.sum(dqb[...].astype(f32), 0, keepdims=True)
    vacc[0, 1:2, :] = jnp.sum(I[0:W3, :].astype(f32), 0, keepdims=True)
    G[9] = tn(xe[...], I[0:W3, :]).astype(bf).reshape(4, 192, D)
    give(9)
    tick(t)
    G[10] = tn(xe[...], A[0:W3, :]).astype(bf).reshape(4, 192, D)
    give(10)
    s1(9)
    copy(9, 0).start()
    for cp in loads[11:]:
        cp.wait()
    for dst, r in ((od, slice(0, R)), (nrm, slice(2 * R, W3))):
        dst[...] = (nt(A[r, :], wk[...]) + nt(I[r, :], wv[...])).astype(bf)
    hfl = remote(od, HR, hs.at[0], hrs.at[0], (fwd, f))
    hfr = remote(nrm, HR, hs.at[0], hrs.at[0], (fwd, f))
    hx = remote(ad, hin, hs.at[1], hrs.at[1], p[0])

    @pl.when(jnp.logical_and(has_fwd, odd))
    def _():
        hfr.start()

    @pl.when(jnp.logical_and(has_fwd, jnp.logical_not(odd)))
    def _():
        hfl.start()

    G[11] = tn(xe[own, :], dqb[...]).astype(bf).reshape(4, 192, D)
    give(11)
    s1(10)
    copy(10, 0).start()
    tick(t + 1)
    ctx[...] = (nt(dqb[...], wq[...]) + nt(A[own, :], wk[...]) + nt(I[own, :], wv[...])).astype(bf)
    gxc = pltpu.make_async_copy(ctx, gx_o, ld.at[14])
    gxc.start()
    s1(11)
    copy(11, 0).start()

    @pl.when(odd)
    def _():
        ad[...] = od[...]

    @pl.when(jnp.logical_not(odd))
    def _():
        ad[...] = nrm[...]

    vround = 0
    for step in range(t + 2, NP + len(stages) - 1):
        tick(step)
        if step == t + 4:

            @pl.when(has_src)
            def _():
                hfl.wait_recv()
                add_rows(ad, ad, HR, R, 32)

            hx.start()
        if vround <= len(peers):
            if vround > 0:
                exchange.wait()
                vacc[vround] = vacc[vround - 1] + VR[vround - 1]
            if vround < len(peers):
                exchange = remote(vacc.at[vround], VR.at[vround], vs.at[vround], vr.at[vround], peers[vround])
                exchange.start()
            vround += 1
    while vround <= len(peers):
        exchange.wait()
        vacc[vround] = vacc[vround - 1] + VR[vround - 1]
        if vround < len(peers):
            exchange = remote(vacc.at[vround], VR.at[vround], vs.at[vround], vr.at[vround], peers[vround])
            exchange.start()
        vround += 1
    vout[...] = vacc[len(peers)]
    hx.wait()

    @pl.when(has_fwd)
    def _():
        hfl.wait_send()

    def done(k, _):
        for yy in range(2):
            core(k, yy).wait_send()
        for i in range(7 + len(extra)):
            copy(k, i).wait_send()
        return 0

    lax.fori_loop(0, NP, done, 0)
    gxc.wait()


def back(n, act, od, nrm, idel, ctx, ad, q, k, v, sd, xe, wq, wk, wv, gv, ct, se):
    R = q.shape[0]
    ne = len(extra_bits(n))
    nv = 5 + ne
    S = jax.ShapeDtypeStruct
    ANY = pl.BlockSpec(memory_space=pl.ANY)
    big = (act, od, nrm, idel, ctx, ad, q, k, v, sd, xe, wq, wk, wv)
    return pl.pallas_call(
        functools.partial(back_kernel, n),
        out_shape=[S((NP, 192, D), bf), S((16, D), f32), S((R, D), bf), S((R, D), bf)],
        in_specs=[ANY] * 14 + [FULL] * 3,
        out_specs=[FULL] * 3 + [ANY],
        scratch_shapes=[VM(t.shape, t.dtype) for t in big[:11]]
        + [
            VM((NP, 4, 192, D), bf),
            VM((NP, 2, 192, D), bf),
            VM((NP, 192, D), bf),
            VM((NP, 96, D), bf),
            VM((NP, 48, D), bf),
            VM((NP, 48, 384), bf),
            VM((NP, max(ne, 1), 48, 384), bf),
            VM((nv, 16, D), f32),
            VM((nv + 1, 16, D), f32),
            VM((R, D), bf),
            VM((3 * R, 128), bf),
            VM((3 * R, 128), f32),
            VM((3 * R, 128), f32),
            DMA((15,)),
            DMA((NP, 2)),
            DMA((NP, 2)),
            DMA((NP, 7 + ne)),
            DMA((NP, 7 + ne)),
            DMA((nv,)),
            DMA((nv,)),
            DMA((2,)),
            DMA((2,)),
        ],
        compiler_params=pltpu.CompilerParams(collective_id=2, has_side_effects=True, vmem_limit_bytes=60 * 2**20),
        name="back",
    )(*big, gv, ct, se)


def last_kernel(g, g1, gx, hin, gq, gk, gw, go, gi, gu, gt):
    for ref, k in ((gw, 9), (gk, 10), (gq, 11), (go, 8)):
        ref[...] = g[k].astype(f32)
    for j in range(4):
        gi[:, 768 * j : 768 * j + 768] = g[4 + j].astype(f32)
        gu[192 * j : 192 * j + 192, :] = g[j].astype(f32)
    gt[...] = g1[...] + gx[...].astype(f32) + hin[...].astype(f32)


def last(g, g1, gx, hin):
    R = g1.shape[0]
    S = jax.ShapeDtypeStruct
    return pl.pallas_call(
        last_kernel,
        out_shape=[S((192, D), f32)] * 4 + [S((192, 4 * D), f32), S((4 * 192, D), f32), S((R, D), f32)],
        in_specs=[FULL] * 4,
        out_specs=[FULL] * 7,
        compiler_params=pltpu.CompilerParams(vmem_limit_bytes=VLIM),
        name="last",
    )(g, g1, gx, hin)


def local(n, tokens, doc_lengths, cotangent, wq, wk, wv, wo, wi, wu, bq, bv, bo, bi, bu, ga, sa, gf, sf):
    f = lax.axis_index("fsdp")
    x = tokens[0]
    lengths = doc_lengths[0]
    docs = lengths.shape[0]
    assert docs <= 128 and x.shape[0] == 512
    ends = jnp.cumsum(lengths)
    se = jnp.zeros((8, 128), jnp.int32)
    se = se.at[0, :docs].set(ends - lengths).at[1, :docs].set(ends)
    small = jnp.stack([bq, bv, bo, bu, ga, sa, gf, sf])
    w = small.shape[1]
    vec = jnp.zeros((16, D), bf)
    vec = lax.dynamic_update_slice(vec, small, (0, f * w))
    vec = lax.dynamic_update_slice(vec, bi[None], (8 + f, 0))
    xe, wq, wk, wv, wo, wi, wu, vec = gather(n, x, (wq, wk, wv, wo, wi, wu), vec)
    q, k, v, ctx, rt = attn_fwd(xe, wq, wk, wv, vec, se)
    layer_out, act, idel, od, nrm, ad, gv, sd, ct, g1 = mid(x, ctx, rt, wo, wi, wu, vec, cotangent[0])
    g, gv, hin, gx = back(n, act, od, nrm, idel, ctx, ad, q, k, v, sd, xe, wq, wk, wv, gv, ct, se)
    *grads, gt = last(g, g1, gx, hin)
    gs = lax.dynamic_slice(gv, (0, f * w), (8, w))
    gbi = lax.dynamic_slice(gv, (8 + f, 0), (1, D))[0]
    gq, gk, gw, go, gi, gu = grads
    return (layer_out[None], gt[None], gq, gk, gw, go, gi, gu, gs[0], gs[1], gs[2], gbi, gs[3], gs[4], gs[5], gs[6], gs[7])


def solution(mesh):
    n = mesh.shape["ctx"]
    tok = P("fsdp", "ctx", None)
    mat = P("fsdp", None)
    vec = P("fsdp")
    return jax.shard_map(
        functools.partial(local, n),
        mesh=mesh,
        in_specs=(tok, mat, tok) + (mat,) * 6 + (vec,) * 9,
        out_specs=(tok, tok) + (mat,) * 6 + (vec,) * 9,
        check_vma=False,
    )
```

```python
import functools

import jax
import jax.numpy as jnp
from jax import lax
from jax.experimental import pallas as pl
from jax.experimental.pallas import tpu as pltpu
from jax.sharding import PartitionSpec as P

bf = jnp.bfloat16
f32 = jnp.float32
MESH = pl.DeviceIdType.MESH
VM = pltpu.VMEM
DMA = pltpu.SemaphoreType.DMA
D = 768
EPS = 1e-12
BIG = 1e30
C2 = 0.125 * 1.4426950408889634
RSQ2 = 0.7071067811865476
RS2PI = 0.3989422804014327
BQ = 256
WIN = BQ + 1024
TOKP = 4
HS = 192
VLIM = 58 * 2**20
FULL = pl.BlockSpec(memory_space=pltpu.VMEM)


def nt(a, b):
    return lax.dot_general(a, b, (((1,), (1,)), ((), ())), preferred_element_type=f32)


def nn(a, b):
    return lax.dot_general(a, b, (((1,), (0,)), ((), ())), preferred_element_type=f32)


def tn(a, b):
    return lax.dot_general(a, b, (((0,), (0,)), ((), ())), preferred_element_type=f32)


def bit(i, b):
    return lax.rem(lax.div(i, b), 2)


def flip(i, b):
    return i + b * (1 - 2 * bit(i, b))


def remote(src, dst, send, recv, device):
    return pltpu.make_async_remote_copy(
        src_ref=src, dst_ref=dst, send_sem=send, recv_sem=recv, device_id=device, device_id_type=MESH
    )


def greet(peers, others):
    bar = pltpu.get_barrier_semaphore()
    for d in peers:
        pl.semaphore_signal(bar, inc=1, device_id=d, device_id_type=MESH)
    for cond, d in others:

        @pl.when(cond)
        def _():
            pl.semaphore_signal(bar, inc=1, device_id=d, device_id_type=MESH)

    pl.semaphore_wait(bar, len(peers) + sum(cond.astype(jnp.int32) for cond, _ in others))


def vecs_of(vec):
    return (vec[0].astype(f32) + vec[1].astype(f32)) + (vec[2].astype(f32) + vec[3].astype(f32))


def member(pos0, rows, se):
    pos = pos0 + lax.broadcasted_iota(jnp.int32, (rows, 128), 0)
    return jnp.logical_and(pos >= se[0:1, :], pos < se[1:2, :])


def norm(h):
    c = h - jnp.mean(h, 1, keepdims=True)
    r = lax.rsqrt(jnp.mean(c * c, 1, keepdims=True) + EPS)
    return c * r, r


PIECES = [(0, 0, 192, 0, 768, 2), (1, 0, 192, 0, 768, 2), (2, 0, 192, 0, 768, 2), (3, 0, 192, 0, 768, 1)]
PIECES += [(4, 0, 192, 768 * j, 768, 1 if j < 3 else 2) for j in range(4)]
PIECES += [(5, 192 * j, 192, 0, 768, 1 if j in (1, 3) else 2) for j in range(4)]
YWIN = 4


def front_kernel(n, *refs):
    tok, *sh = refs[:7]
    *small, inner_v, cot_h, lens = refs[7:18]
    outs = refs[18:37]
    (xe, wq, wk, wv, wo, wi, wu, vecb, q_o, k_o, v_o, ctx, rt, nseg, act, dg, od, nrm, ad, sd, ct, gv, g2, xh1, acc, r1s, cot, lo, se, vec) = refs[37:67]
    ts, tr, ws, wr, vs, vr, ls, osem = refs[67:]
    full = (wq, wk, wv, wo, wi, wu)
    c = lax.axis_index("ctx")
    f = lax.axis_index("fsdp")
    sib = (c, flip(f, 1))
    yp = (c, flip(f, 2))
    dgn = (c, flip(flip(f, 1), 2))
    c1 = (flip(c, 1), f)
    c2 = (flip(c, 2), f)
    even = bit(c, 1) == 0
    fwd = jnp.where(even, c + 2, c - 2)
    src = jnp.where(even, c - 2, c + 2)
    has_fwd = jnp.logical_and(fwd >= 0, fwd < n)
    has_src = jnp.logical_and(src >= 0, src < n)
    oth = jnp.where(bit(c, 2) == 0, c - 2, c + 2)
    has_oth = jnp.logical_and(oth >= 0, oth < n)
    R = xe.shape[0] // 3

    locs = [pltpu.make_async_copy(tok, xe.at[pl.ds(R, R)], ls.at[0])]
    for i, (s, w) in enumerate(zip(sh, full)):
        H = s.shape[0]
        locs.append(pltpu.make_async_copy(s, w.at[pl.ds(pl.multiple_of(f * H, 16), H)], ls.at[1 + i]))
    locs.append(pltpu.make_async_copy(cot_h, cot, ls.at[7]))
    greet((sib, yp, dgn, c1, c2), ((has_oth, (oth, f)),))
    pr = R // TOKP
    pslot = jnp.where(even, 2 * R, 0)
    dslot = jnp.where(even, 0, 2 * R)
    tcp = [
        remote(
            tok.at[pl.ds(i * pr, pr)],
            xe.at[pl.ds(pl.multiple_of(dslot + i * pr, pr), pr)],
            ts.at[0, i],
            tr.at[0, i],
            c1,
        )
        for i in range(TOKP)
    ]
    vcp = [remote(vec, vecb.at[f], vs.at[i], vr.at[i], (sib, yp, dgn)[i]) for i in range(3)]
    wcp = []
    fy = flip(f, 2)
    for k, (t, r0, H2, c0, C, route) in enumerate(PIECES):
        s = sh[t]
        w = full[t]
        SR = s.shape[0]
        H = H2 // 2
        p = c1 if route == 1 else c2
        hb = bit(c, route)
        cs = slice(c0, c0 + C)
        own = pl.multiple_of(f * SR + r0, 16)
        mine = pl.multiple_of(f * SR + r0 + hb * H, 16)
        gy = pl.multiple_of(fy * SR + r0 + hb * H, 16)
        gx = pl.multiple_of(fy * SR + r0 + (1 - hb) * H, 16)
        wcp.append(
            [
                remote(s.at[pl.ds(r0, H2), cs], w.at[pl.ds(own, H2), cs], ws.at[k, 0], wr.at[k, 0], sib),
                remote(
                    s.at[pl.ds(pl.multiple_of(r0 + hb * H, 16), H), cs],
                    w.at[pl.ds(mine, H), cs],
                    ws.at[k, 1],
                    wr.at[k, 1],
                    yp,
                ),
                remote(w.at[pl.ds(gy, H), cs], w.at[pl.ds(gy, H), cs], ws.at[k, 2], wr.at[k, 2], p),
                remote(w.at[pl.ds(gy, H), cs], w.at[pl.ds(gy, H), cs], ws.at[k, 3], wr.at[k, 3], sib),
                remote(w.at[pl.ds(gx, H), cs], w.at[pl.ds(gx, H), cs], ws.at[k, 4], wr.at[k, 4], sib),
            ]
        )
    NPC = len(PIECES)
    for k in range(YWIN):
        wcp[k][1].start()
    for t in tcp[:2]:
        t.start()
    for cp in locs[:4]:
        cp.start()
    for k in range(3):
        wcp[k][0].start()

    w8 = D // 4
    sel = lax.broadcasted_iota(jnp.int32, (w8, D), 0) + f * w8 == lax.broadcasted_iota(jnp.int32, (w8, D), 1)
    place = jnp.where(sel, 1.0, 0.0).astype(bf)
    r8 = lax.broadcasted_iota(jnp.int32, (8, w8), 0)
    rows8 = jnp.zeros((8, w8), f32)
    for j, ref in enumerate(small):
        rows8 = jnp.where(r8 == j, jnp.broadcast_to(ref[...].astype(f32).reshape(1, w8), (8, w8)), rows8)
    rows8 = rows8.astype(bf)
    isf = lax.broadcasted_iota(jnp.int32, (8, D), 0) == f
    inner = jnp.where(isf, jnp.broadcast_to(inner_v[...].astype(f32).reshape(1, D), (8, D)), 0.0)
    vec[...] = jnp.concatenate([nn(rows8, place), inner], 0).astype(bf)
    for v in vcp:
        v.start()
    vecb[f] = vec[...]
    docs = lens.shape[1]
    ln8 = jnp.broadcast_to(lens[...].astype(f32), (8, docs))
    la = lax.broadcasted_iota(jnp.int32, (docs, 128), 0)
    lb = lax.broadcasted_iota(jnp.int32, (docs, 128), 1)
    upto = jnp.where(jnp.logical_and(la <= lb, lb < docs), 1.0, 0.0)
    below = jnp.where(jnp.logical_and(la < lb, lb < docs), 1.0, 0.0)
    hi = lax.Precision.HIGHEST
    ends = jnp.dot(ln8, upto, preferred_element_type=f32, precision=hi)
    starts = jnp.dot(ln8, below, preferred_element_type=f32, precision=hi)
    first_row = lax.broadcasted_iota(jnp.int32, (8, 128), 0) == 0
    se[...] = jnp.where(first_row, starts, ends).astype(jnp.int32)

    @pl.when(jnp.logical_not(has_src))
    def _():
        xe[pl.ds(pl.multiple_of(dslot, R), R), :] = jnp.zeros((R, D), bf)

    tfw = [
        remote(
            xe.at[pl.ds(pl.multiple_of(pslot + i * pr, pr), pr)],
            xe.at[pl.ds(pl.multiple_of(dslot + i * pr, pr), pr)],
            ts.at[1, i],
            tr.at[1, i],
            (fwd, f),
        )
        for i in range(TOKP)
    ]

    def y(k):
        wcp[k][1].wait_recv()
        wcp[k][2].start()
        wcp[k][3].start()
        if k + YWIN < NPC:
            wcp[k + YWIN][1].start()

    def x(k):
        wcp[k][2].wait_recv()
        wcp[k][4].start()

    def t(i):
        tcp[i].wait_recv()
        if i + 2 < TOKP:
            tcp[i + 2].start()

        @pl.when(has_fwd)
        def _():
            tfw[i].start()

    def ready(ks):
        for k in ks:
            for i in (0, 3, 4):
                wcp[k][i].wait_recv()

    y(0)
    t(0)
    y(1)
    t(1)
    y(2)
    x(0)
    for cp in locs[4:]:
        cp.start()
    for k in range(3, NPC):
        wcp[k][0].start()
    x(1)
    x(2)
    t(2)
    y(3)
    for cp in locs[:4]:
        cp.wait()
    for v in vcp:
        v.wait_recv()
    ready(range(3))
    anchor = c * R
    V = vecs_of(vecb)

    def row(i):
        return V[i : i + 1, :]

    def out(i, ref):
        cp = pltpu.make_async_copy(ref, outs[i], osem.at[i])
        cp.start()
        sent.append(cp)

    sent = []
    for i, w in enumerate((wq, wk, wv)):
        out(i, w)

    def proj(r):
        def body(i, _):
            rr = pl.ds(pl.multiple_of(r + i * 256, 256), 256)
            xb = xe[rr, :]
            k_o[rr, :] = nn(xb, wk[...]).astype(bf)
            v_o[rr, :] = (nn(xb, wv[...]) + row(1)).astype(bf)
            return 0

        lax.fori_loop(0, R // 256, body, 0)

    def projq(i, _):
        rr = pl.ds(pl.multiple_of(R + i * 256, 256), 256)
        q_o[pl.ds(pl.multiple_of(i * 256, 256), 256), :] = (nn(xe[rr, :], wq[...]) + row(0)).astype(bf)
        return 0

    def seg(i, _):
        rr = pl.ds(pl.multiple_of(i * 256, 256), 256)
        nseg[rr, :] = jnp.where(member(anchor - R + i * 256, 256, se), 0.0, 1.0).astype(bf)
        return 0

    lax.fori_loop(0, 3 * R // 256, seg, 0)
    lax.fori_loop(0, R // 256, projq, 0)
    t(3)
    proj(R)
    y(4)
    x(3)
    proj(pslot)
    y(5)
    x(4)
    for i in range(TOKP):

        @pl.when(has_src)
        def _():
            tfw[i].wait_recv()

    proj(dslot)
    out(18, se)
    out(3, xe)
    out(4, q_o)
    out(5, k_o)
    out(6, v_o)
    lane = lax.broadcasted_iota(jnp.int32, (BQ, 128), 1)
    nqb = R // BQ

    def att(i, _):
        qb = lax.div(i, 6)
        hp = lax.rem(i, 6)
        qr = pl.ds(pl.multiple_of(qb * BQ, BQ), BQ)
        wr_ = pl.ds(pl.multiple_of(qb * BQ, BQ), WIN)
        hc = pl.ds(pl.multiple_of(hp * 128, 128), 128)
        oh = jnp.where(nseg[pl.ds(pl.multiple_of(R + qb * BQ, BQ), BQ), :] == 0, -BIG, 0.0).astype(bf)
        qp = q_o[qr, hc]
        kk = jnp.concatenate([k_o[wr_, hc], nseg[wr_, :]], 1)
        vv = v_o[wr_, hc]
        res = []
        for h in range(2):
            sel = (lane < 64) if h == 0 else (lane >= 64)
            qa = jnp.concatenate([jnp.where(sel, qp, jnp.zeros_like(qp)), oh], 1)
            pe = jnp.exp2(nt(qa, kk) * C2)
            res.append((nn(pe.astype(bf), vv), jnp.sum(pe, 1, keepdims=True)))
        o = jnp.where(lane < 64, res[0][0], res[1][0])
        tot = jnp.where(lane < 64, res[0][1], res[1][1])
        ctx[qr, hc] = (o / tot).astype(bf)
        rt[qr, hc] = tot
        return 0

    pumps = ((y, 6), (x, 5), (y, 7), (x, 6)), ((y, 8), (x, 7), (y, 9), (x, 8))
    per = 6 * nqb // len(pumps)
    for gidx, steps in enumerate(pumps):
        lax.fori_loop(gidx * per, gidx * per + per, att, 0)
        for step, k in steps:
            step(k)
    out(7, ctx)

    B = 256
    NB = R // B

    def rows(i, j=0):
        return pl.ds(pl.multiple_of(j * R + i * B, B), B)

    ready((3,))
    locs[4].wait()
    gv[...] = jnp.zeros_like(gv)

    def p1(i, _):
        r = rows(i)
        h = xe[pl.ds(pl.multiple_of(R + i * B, B), B), :].astype(f32) + nn(ctx[r, :], wo[...]) + row(2)
        xh, rr = norm(h)
        xh1[r, :] = xh
        r1s[r, :] = jnp.broadcast_to(rr, (B, 128))
        nrm[r, :] = (xh * row(4) + row(5)).astype(bf)
        return 0

    lax.fori_loop(0, NB, p1, 0)
    out(8, nrm)
    y(10)
    x(9)
    y(11)
    x(10)
    x(11)
    for cp in locs[5:]:
        cp.wait()
    ready(range(4, NPC))

    for j in range(4):
        cs = slice(768 * j, 768 * j + 768)
        bi = row(8 + j)

        def p2(i, _, cs=cs, bi=bi, j=j):
            r = rows(i)
            rj = rows(i, j)
            pre = nn(nrm[r, :], wi[:, cs]) + bi
            cdf = 0.5 + 0.5 * lax.erf(pre * RSQ2)
            pdf = jnp.exp(pre * pre * -0.5) * RS2PI
            a = (pre * cdf).astype(bf)
            act[rj, :] = a
            dg[rj, :] = (cdf + pre * pdf).astype(bf)
            o = nn(a, wu[cs, :])
            if j == 0:
                acc[r, :] = o
            else:
                acc[r, :] += o
            return 0

        lax.fori_loop(0, NB, p2, 0)
    out(9, act)

    def p3(i, _):
        r = rows(i)
        h = nrm[r, :].astype(f32) + acc[r, :] + row(3)
        xh, rr = norm(h)
        lo[r, :] = (xh * row(6) + row(7)).astype(bf)
        g = cot[r, :].astype(f32)
        gv[6:7, :] += jnp.sum(g * xh, 0, keepdims=True)
        gv[7:8, :] += jnp.sum(g, 0, keepdims=True)
        e = g * row(6)
        d = rr * (e - jnp.mean(e, 1, keepdims=True) - xh * jnp.mean(e * xh, 1, keepdims=True))
        g2[r, :] = d
        db = d.astype(bf)
        od[r, :] = db
        gv[3:4, :] += jnp.sum(db.astype(f32), 0, keepdims=True)
        return 0

    lax.fori_loop(0, NB, p3, 0)
    out(10, lo)
    out(11, od)
    for j in range(4):
        cs = slice(768 * j, 768 * j + 768)

        def p4(i, _, cs=cs, j=j):
            r = rows(i)
            rj = rows(i, j)
            d = (nt(od[r, :], wu[cs, :]) * dg[rj, :].astype(f32)).astype(bf)
            dg[rj, :] = d
            gv[8 + j : 9 + j, :] += jnp.sum(d.astype(f32), 0, keepdims=True)
            g2[r, :] += nt(d, wi[:, cs])
            return 0

        lax.fori_loop(0, NB, p4, 0)
    out(12, dg)
    heads = lax.broadcasted_iota(jnp.int32, (16, D), 0)
    onehot = jnp.where(lax.div(lax.broadcasted_iota(jnp.int32, (16, D), 1), 64) == heads, 1.0, 0.0)
    for i in range(NB):
        r = slice(i * B, i * B + B)
        g = g2[r, :]
        xh = xh1[r, :]
        rr = r1s[r, 0:1]
        gv[4:5, :] += jnp.sum(g * xh, 0, keepdims=True)
        gv[5:6, :] += jnp.sum(g, 0, keepdims=True)
        e = g * row(4)
        d = rr * (e - jnp.mean(e, 1, keepdims=True) - xh * jnp.mean(e * xh, 1, keepdims=True))
        g2[r, :] = d
        db = d.astype(bf)
        ad[r, :] = db
        gv[2:3, :] += jnp.sum(db.astype(f32), 0, keepdims=True)
        cd = nt(db, wo[...]).astype(bf).astype(f32)
        sc = cd * (1.0 / rt[r, :])
        sd[r, :] = sc.astype(bf)
        ct[:, r] = lax.dot_general(
            onehot,
            sc * ctx[r, :].astype(f32),
            (((1,), (1,)), ((), ())),
            preferred_element_type=f32,
            precision=lax.Precision.HIGHEST,
        )
    for i, ref in ((13, ad), (14, sd), (15, ct), (16, gv), (17, g2)):
        out(i, ref)
    for i in range(TOKP):

        @pl.when(has_fwd)
        def _():
            tfw[i].wait_send()

        tcp[i].wait_send()
    for cps in wcp:
        for cp in cps:
            cp.wait_send()
    for v in vcp:
        v.wait_send()
    for cp in sent:
        cp.wait()


def front(n, tok, shards, vecs, cot, lens):
    R = tok.shape[0]
    S = jax.ShapeDtypeStruct
    ANY = pl.BlockSpec(memory_space=pl.ANY)
    F = shards[4].shape[1]
    NPC = len(PIECES)
    row = (R, D)
    W = (D, D)
    outs = [S(W, bf)] * 3 + [S((3 * R, D), bf), S(row, bf), S((3 * R, D), bf), S((3 * R, D), bf)]
    outs += [S(row, bf), S(row, bf), S((4 * R, D), bf), S(row, bf), S(row, bf), S((4 * R, D), bf)]
    outs += [S(row, bf), S(row, bf), S((16, R), f32), S((16, D), f32), S(row, f32), S((8, 128), jnp.int32)]
    scratch = [VM((3 * R, D), bf)] + [VM(W, bf)] * 4 + [VM((D, F), bf), VM((F, D), bf), VM((4, 16, D), bf)]
    scratch += [VM(row, bf), VM((3 * R, D), bf), VM((3 * R, D), bf), VM(row, bf), VM(row, f32), VM((3 * R, 128), bf)]
    scratch += [VM((4 * R, D), bf), VM((4 * R, D), bf)] + [VM(row, bf)] * 4
    scratch += [VM((16, R), f32), VM((16, D), f32), VM(row, f32), VM(row, f32), VM(row, f32), VM((R, 128), f32)]
    scratch += [VM(row, bf), VM(row, bf), VM((8, 128), jnp.int32), VM((16, D), bf)]
    scratch += [DMA((2, TOKP)), DMA((2, TOKP)), DMA((NPC, 5)), DMA((NPC, 5)), DMA((3,)), DMA((3,)), DMA((8,)), DMA((19,))]
    return pl.pallas_call(
        functools.partial(front_kernel, n),
        out_shape=outs,
        in_specs=[ANY] * 7 + [FULL] * 9 + [ANY, FULL],
        out_specs=[ANY] * 19,
        scratch_shapes=scratch,
        compiler_params=pltpu.CompilerParams(collective_id=1, has_side_effects=True, vmem_limit_bytes=VLIM),
        name="front",
    )(tok, *shards, *vecs, cot, lens)


NP = 12
NH = 2 * NP
WINDOW = 3
LATE = 18
LAG = 2
TURN = 3
HCH = 8
HLAG = 3


def extra_bits(n):
    return [1 << j for j in range(3, 16) if (1 << j) < n]


def add_rows(dst, a, b, rows, step=48):
    def body(i, _):
        r = pl.ds(pl.multiple_of(i * step, 16), step)
        dst[r, :] = a[r, :] + b[r, :]
        return 0

    lax.fori_loop(0, rows // step, body, 0)


def back_kernel(n, *refs):
    hbm = refs[:14]
    gvin, ct, se = refs[14:17]
    OUT, vout, hin, gx_o = refs[17:21]
    bufs = refs[21:32]
    A, od, nrm, I, ctx, ad, q, k_, v_, sd, xe = bufs
    wq = k_.at[pl.ds(0, D)]
    wk = v_.at[pl.ds(0, D)]
    wv = v_.at[pl.ds(D, D)]
    bufs = bufs + (wq, wk, wv)
    G, RC, RY, RX, RZ, RW, RE, VR, vacc, HR, nseg, dk, dv = refs[32:45]
    ld, cs, cr, ss, sr, vs, vr, hs, hrs = refs[45:]
    dqb = q
    R = q.shape[0]
    extra = extra_bits(n)
    c = lax.axis_index("ctx")
    f = lax.axis_index("fsdp")
    cb = bit(f, 1)
    yb = bit(f, 2)
    sib = (c, flip(f, 1))
    yp = (c, flip(f, 2))
    p = [(flip(c, 1 << j), f) for j in range(3)]
    peers = [sib, yp] + p + [(flip(c, b), f) for b in extra]
    odd = bit(c, 1) == 1
    fwd = jnp.where(odd, c + 2, c - 2)
    src = jnp.where(odd, c - 2, c + 2)
    has_fwd = jnp.logical_and(fwd >= 0, fwd < n)
    has_src = jnp.logical_and(src >= 0, src < n)
    oth = jnp.where(bit(c, 2) == 0, c - 2, c + 2)
    has_oth = jnp.logical_and(oth >= 0, oth < n)
    loads = [pltpu.make_async_copy(hbm[i], bufs[i], ld.at[i]) for i in range(14)]
    for cp in loads[:10]:
        cp.start()
    greet(peers, ((has_oth, (oth, f)),))
    loads[10].start()

    bit0 = bit(c, 1)
    bit1 = bit(c, 2)

    def turned(m):
        return (m % TURN == TURN - 1) if isinstance(m, int) else (lax.rem(m, TURN) == TURN - 1)

    def pick(m, one, two):
        t = turned(m)
        if isinstance(t, bool):
            return two if t else one
        return jnp.where(t, two, one)

    def core(k, yy):
        return remote(G.at[k, 2 * yy + (1 - cb)], RC.at[k, yy], cs.at[k, yy], cr.at[k, yy], sib)

    def place(m):
        k = m // 2 if isinstance(m, int) else lax.div(m, 2)
        h = m % 2 if isinstance(m, int) else lax.rem(m, 2)
        return k, pl.ds(h * 384 if isinstance(m, int) else pl.multiple_of(h * 384, 128), 384)

    def quarter(m, q):
        k, h = place(m)
        return G.at[k, q, :, h]

    def part(ref, m, r=None):
        k, h = place(m)
        return ref.at[k, :, h] if r is None else ref.at[k, r, h]

    def first(m):
        return pl.multiple_of(pick(m, bit0, bit1) * 96, 16)

    def second(m):
        return first(m) + pl.multiple_of(pick(m, bit1, bit0) * 48, 16)

    def rows_of(ref, m, r, size):
        return ref.at[pl.ds(pl.multiple_of(r, 16), size)]

    def acc(m):
        return quarter(m, 2 * yb + cb)

    def spare(m, i):
        return part(RY, m, pl.ds(48 * (i % 4), 48))

    def copy(m, i):
        s = (ss.at[m, i], sr.at[m, i])
        pa = (pick(m, flip(c, 1), flip(c, 2)), f)
        pb = (pick(m, flip(c, 2), flip(c, 1)), f)
        if i == 0:
            return remote(quarter(m, 2 * (1 - yb) + cb), part(RY, m), *s, yp)
        if i == 1:
            return remote(rows_of(acc(m), m, 96 - first(m), 96), part(RX, m), *s, pa)
        if i == 2:
            r = first(m) + 48 - pick(m, bit1, bit0) * 48
            return remote(rows_of(acc(m), m, r, 48), part(RZ, m), *s, pb)
        if i == 3:
            return remote(rows_of(acc(m), m, second(m), 48), part(RW, m), *s, p[2])
        if i == 4:
            o = part(OUT, m, pl.ds(pl.multiple_of(second(m), 16), 48))
            return remote(o, o, *s, pb)
        if i == 5:
            o = part(OUT, m, pl.ds(first(m), 96))
            return remote(o, o, *s, pa)
        e = extra[i - 6]
        return remote(spare(m, i - 6), part(RE.at[i - 6], m), *s, (flip(c, e), f))

    def give(k):
        for yy in range(2):
            core(k, yy).start()

    def s1(k):
        for yy in range(2):
            core(k, yy).wait_recv()
        for yy in range(2):
            g = G.at[k, 2 * yy + cb]
            add_rows(g, g, RC.at[k, yy], 192)

    def s2(m):
        copy(m, 0).wait_recv()
        if isinstance(m, int):
            if m + WINDOW < LATE:
                copy(m + WINDOW, 0).start()
        else:

            @pl.when(m + WINDOW < LATE)
            def _():
                copy(m + WINDOW, 0).start()

        add_rows(acc(m), acc(m), part(RY, m), 192)
        copy(m, 1).start()

    def s3(m):
        copy(m, 1).wait_recv()
        a = rows_of(acc(m), m, first(m), 96)
        add_rows(a, a, part(RX, m), 96)
        copy(m, 2).start()

    def s4(m):
        copy(m, 2).wait_recv()
        a = rows_of(acc(m), m, second(m), 48)
        add_rows(a, a, part(RZ, m), 48)
        copy(m, 3).start()

    def s5(m):
        copy(m, 3).wait_recv()
        last = rows_of(acc(m), m, second(m), 48)
        got = part(RW, m)
        for i in range(len(extra)):
            add_rows(spare(m, i), last, got, 48)
            copy(m, 6 + i).start()
            copy(m, 6 + i).wait_recv()
            last = spare(m, i)
            got = part(RE.at[i], m)
        add_rows(part(OUT, m, pl.ds(pl.multiple_of(second(m), 16), 48)), last, got, 48)
        copy(m, 4).start()

    def s6(m):
        copy(m, 4).wait_recv()
        copy(m, 5).start()

    def s7(m):
        copy(m, 5).wait_recv()

    stages = (s2, s3, s4, s5, s6, s7)

    def tick(t):
        for i in reversed(range(len(stages))):
            m = t - LAG * i
            if isinstance(t, int):
                if 0 <= m < NH:
                    stages[i](m)
            else:

                @pl.when(jnp.logical_and(m >= 0, m < NH))
                def _():
                    stages[i](m)

    def outer(hh, qq):
        g = tn(A[pl.ds(pl.multiple_of(qq * R, R), R), 384 * hh : 384 * hh + 384], od[...]).astype(bf)
        G[2 * hh, qq] = g[:192]
        G[2 * hh + 1, qq] = g[192:]

    loads[0].wait()
    loads[1].wait()
    for hh in range(2):
        for yy in range(2):
            outer(hh, 2 * yy + (1 - cb))
        give(2 * hh)
        give(2 * hh + 1)
        for yy in range(2):
            outer(hh, 2 * yy + cb)
    for k in range(2):
        s1(k)
        for m in (2 * k, 2 * k + 1):
            if m < WINDOW:
                copy(m, 0).start()
    loads[2].wait()
    loads[3].wait()
    for j in range(4):
        G[4 + j] = tn(nrm[...], I[R * j : R * j + R, :]).astype(bf).reshape(4, 192, D)
        give(4 + j)
        if j < 2:
            s1(2 + j)
        if j == 2:
            tick(0)
    s1(4)
    tick(1)
    loads[4].wait()
    loads[5].wait()
    G[8] = tn(ctx[...], ad[...]).astype(bf).reshape(4, 192, D)
    give(8)
    for k in (5, 6, 7):
        s1(k)
    tick(2)
    s1(8)

    anchor = c * R

    def prep(i, _):
        r = pl.ds(pl.multiple_of(i * 256, 256), 256)
        nseg[r, :] = jnp.where(member(anchor - R + i * 256, 256, se), 0.0, 1.0).astype(bf)
        dk[r, :] = jnp.zeros((256, 128), f32)
        dv[r, :] = jnp.zeros((256, 128), f32)
        return 0

    lax.fori_loop(0, 3 * R // 256, prep, 0)
    lane = lax.broadcasted_iota(jnp.int32, (BQ, 128), 1)
    nqb = R // BQ
    for i in range(6, 10):
        loads[i].wait()

    def head(i, _):
        hp = lax.div(i, nqb)
        qb = lax.rem(i, nqb)
        hc = pl.ds(pl.multiple_of(hp * 128, 128), 128)
        qr = pl.ds(pl.multiple_of(qb * BQ, BQ), BQ)
        wr = pl.ds(pl.multiple_of(qb * BQ, BQ), WIN)
        oh = jnp.where(nseg[pl.ds(pl.multiple_of(R + qb * BQ, BQ), BQ), :] == 0, -BIG, 0.0).astype(bf)
        qp = q[qr, hc]
        sp = sd[qr, hc]
        kp = k_[wr, hc]
        vp = v_[wr, hc]
        kk = jnp.concatenate([kp, nseg[wr, :]], 1)
        z = jnp.zeros_like(qp)
        dkp = []
        dvp = []
        dqs = []
        for h in range(2):
            sel = (lane < 64) if h == 0 else (lane >= 64)
            qm = jnp.where(sel, qp, z)
            sm = jnp.where(sel, sp, z)
            pr = jnp.exp2(nt(kk, jnp.concatenate([qm, oh], 1)) * C2)
            dp = nt(vp, sm)
            ds = (pr * (dp - ct[pl.ds(2 * hp + h, 1), qr])).astype(bf)
            dvp.append(nn(pr.astype(bf), sm))
            dkp.append(nn(ds, qm))
            dqs.append(tn(ds, kp))
        dk[wr, :] += dkp[0] + dkp[1]
        dv[wr, :] += dvp[0] + dvp[1]
        dqb[qr, hc] = (jnp.where(lane < 64, dqs[0], dqs[1]) * 0.125).astype(bf)

        @pl.when(qb == nqb - 1)
        def _():
            def fin(j, _):
                r = pl.ds(pl.multiple_of(j * 256, 256), 256)
                A[r, hc] = (dk[r, :] * 0.125).astype(bf)
                I[r, hc] = dv[r, :].astype(bf)
                dk[r, :] = jnp.zeros((256, 128), f32)
                dv[r, :] = jnp.zeros((256, 128), f32)
                return 0

            lax.fori_loop(0, 3 * R // 256, fin, 0)

        @pl.when(lax.rem(i, 3) > 0)
        def _():
            tick(2 * lax.div(i, 3) + lax.rem(i, 3) + 2)

        return 0

    lax.fori_loop(0, 6 * nqb, head, 0)
    t = 4 * nqb + 3

    W3 = 3 * R
    own = slice(R, 2 * R)
    for cp in loads[11:]:
        cp.start()
    loads[10].wait()
    vacc[0] = gvin[...]
    vacc[0, 0:1, :] = jnp.sum(dqb[...].astype(f32), 0, keepdims=True)
    vacc[0, 1:2, :] = jnp.sum(I[0:W3, :].astype(f32), 0, keepdims=True)
    for cp in loads[11:]:
        cp.wait()
    for dst, r in ((od, slice(0, R)), (nrm, slice(2 * R, W3))):
        dst[...] = (nt(A[r, :], wk[...]) + nt(I[r, :], wv[...])).astype(bf)

    @pl.when(odd)
    def _():
        ad[...] = od[...]

    @pl.when(jnp.logical_not(odd))
    def _():
        ad[...] = nrm[...]

    hn = R // HCH

    def leg1(ref, j):
        r = pl.ds(j * hn, hn)
        return remote(ref.at[r], HR.at[r], hs.at[0, j], hrs.at[0, j], (fwd, f))

    def leg2(j):
        r = pl.ds(j * hn, hn)
        return remote(ad.at[r], hin.at[r], hs.at[1, j], hrs.at[1, j], p[0])

    def halo(j):
        if 0 <= j < HCH:

            @pl.when(jnp.logical_and(has_fwd, odd))
            def _():
                leg1(nrm, j).start()

            @pl.when(jnp.logical_and(has_fwd, jnp.logical_not(odd)))
            def _():
                leg1(od, j).start()

        j = j - HLAG
        if 0 <= j < HCH:

            @pl.when(has_src)
            def _():
                leg1(od, j).wait_recv()
                r = pl.ds(j * hn, hn)
                add_rows(ad.at[r], ad.at[r], HR.at[r], hn, 32)

            leg2(j).start()

    halo(0)
    G[9] = tn(xe[...], I[0:W3, :]).astype(bf).reshape(4, 192, D)
    give(9)
    tick(t)
    halo(1)
    tick(t + 1)
    G[10] = tn(xe[...], A[0:W3, :]).astype(bf).reshape(4, 192, D)
    give(10)
    s1(9)
    copy(18, 0).start()
    copy(19, 0).start()
    halo(2)
    G[11] = tn(xe[own, :], dqb[...]).astype(bf).reshape(4, 192, D)
    give(11)
    s1(10)
    copy(20, 0).start()
    copy(21, 0).start()
    tick(t + 2)
    halo(3)
    tick(t + 3)
    ctx[...] = (nt(dqb[...], wq[...]) + nt(A[own, :], wk[...]) + nt(I[own, :], wv[...])).astype(bf)
    gxc = pltpu.make_async_copy(ctx, gx_o, ld.at[14])
    gxc.start()
    s1(11)
    copy(22, 0).start()
    copy(23, 0).start()
    vround = 0
    hj = 4
    for step in range(t + 4, NH + LAG * (len(stages) - 1)):
        tick(step)
        halo(hj)
        hj += 1
        if vround <= len(peers) and step % 2 == 0:
            if vround > 0:
                exchange.wait()
                vacc[vround] = vacc[vround - 1] + VR[vround - 1]
            if vround < len(peers):
                exchange = remote(vacc.at[vround], VR.at[vround], vs.at[vround], vr.at[vround], peers[vround])
                exchange.start()
            vround += 1
    while vround <= len(peers):
        exchange.wait()
        vacc[vround] = vacc[vround - 1] + VR[vround - 1]
        if vround < len(peers):
            exchange = remote(vacc.at[vround], VR.at[vround], vs.at[vround], vr.at[vround], peers[vround])
            exchange.start()
        vround += 1
    while hj < HCH + HLAG:
        halo(hj)
        hj += 1
    vout[...] = vacc[len(peers)]
    for j in range(HCH):
        leg2(j).wait()

        @pl.when(has_fwd)
        def _():
            leg1(od, j).wait_send()

    def done(m, _):
        core(lax.div(m, 2), lax.rem(m, 2)).wait_send()
        for i in range(6 + len(extra)):
            copy(m, i).wait_send()
        return 0

    lax.fori_loop(0, NH, done, 0)
    gxc.wait()


def back(n, act, od, nrm, idel, ctx, ad, q, k, v, sd, xe, wq, wk, wv, gv, ct, se):
    R = q.shape[0]
    ne = len(extra_bits(n))
    nv = 5 + ne
    S = jax.ShapeDtypeStruct
    ANY = pl.BlockSpec(memory_space=pl.ANY)
    big = (act, od, nrm, idel, ctx, ad, q, k, v, sd, xe, wq, wk, wv)
    return pl.pallas_call(
        functools.partial(back_kernel, n),
        out_shape=[S((NP, 192, D), bf), S((16, D), f32), S((R, D), bf), S((R, D), bf)],
        in_specs=[ANY] * 14 + [FULL] * 3,
        out_specs=[FULL] * 3 + [ANY],
        scratch_shapes=[VM(t.shape, t.dtype) for t in big[:11]]
        + [
            VM((NP, 4, 192, D), bf),
            VM((NP, 2, 192, D), bf),
            VM((NP, 192, D), bf),
            VM((NP, 96, D), bf),
            VM((NP, 48, D), bf),
            VM((NP, 48, D), bf),
            VM((max(ne, 1), NP, 48, D) if ne else (1, 1, 48, D), bf),
            VM((nv, 16, D), f32),
            VM((nv + 1, 16, D), f32),
            VM((R, D), bf),
            VM((3 * R, 128), bf),
            VM((3 * R, 128), f32),
            VM((3 * R, 128), f32),
            DMA((15,)),
            DMA((NP, 2)),
            DMA((NP, 2)),
            DMA((NH, 6 + ne)),
            DMA((NH, 6 + ne)),
            DMA((nv,)),
            DMA((nv,)),
            DMA((2, HCH)),
            DMA((2, HCH)),
        ],
        compiler_params=pltpu.CompilerParams(collective_id=2, has_side_effects=True, vmem_limit_bytes=61 * 2**20),
        name="back",
    )(*big, gv, ct, se)


def last_kernel(g, g1, gx, hin, gq, gk, gw, go, gi, gu, gt):
    for ref, k in ((gw, 9), (gk, 10), (gq, 11), (go, 8)):
        ref[...] = g[k].astype(f32)
    for j in range(4):
        gi[:, 768 * j : 768 * j + 768] = g[4 + j].astype(f32)
        gu[192 * j : 192 * j + 192, :] = g[j].astype(f32)
    gt[...] = g1[...] + gx[...].astype(f32) + hin[...].astype(f32)


def last(g, g1, gx, hin):
    R = g1.shape[0]
    S = jax.ShapeDtypeStruct
    return pl.pallas_call(
        last_kernel,
        out_shape=[S((192, D), f32)] * 4 + [S((192, 4 * D), f32), S((4 * 192, D), f32), S((R, D), f32)],
        in_specs=[FULL] * 4,
        out_specs=[FULL] * 7,
        compiler_params=pltpu.CompilerParams(vmem_limit_bytes=VLIM),
        name="last",
    )(g, g1, gx, hin)


def local(n, tokens, doc_lengths, cotangent, wq, wk, wv, wo, wi, wu, bq, bv, bo, bi, bu, ga, sa, gf, sf):
    f = lax.axis_index("fsdp")
    x = tokens[0]
    docs = doc_lengths.shape[1]
    assert docs <= 128 and x.shape[0] == 512
    vecs = (bq, bv, bo, bu, ga, sa, gf, sf, bi)
    wq, wk, wv, xe, q, k, v, ctx, nrm, act, layer_out, od, idel, ad, sd, ct, gv, g1, se = front(
        n, x, (wq, wk, wv, wo, wi, wu), vecs, cotangent[0], doc_lengths
    )
    g, gv, hin, gx = back(n, act, od, nrm, idel, ctx, ad, q, k, v, sd, xe, wq, wk, wv, gv, ct, se)
    *grads, gt = last(g, g1, gx, hin)
    w = bq.shape[0]
    gs = lax.dynamic_slice(gv, (0, f * w), (8, w))
    gbi = lax.dynamic_slice(gv, (8 + f, 0), (1, D))[0]
    gq, gk, gw, go, gi, gu = grads
    return (layer_out[None], gt[None], gq, gk, gw, go, gi, gu, gs[0], gs[1], gs[2], gbi, gs[3], gs[4], gs[5], gs[6], gs[7])


def solution(mesh):
    n = mesh.shape["ctx"]
    tok = P("fsdp", "ctx", None)
    mat = P("fsdp", None)
    vec = P("fsdp")
    return jax.shard_map(
        functools.partial(local, n),
        mesh=mesh,
        in_specs=(tok, mat, tok) + (mat,) * 6 + (vec,) * 9,
        out_specs=(tok, tok) + (mat,) * 6 + (vec,) * 9,
        check_vma=False,
    )
```

```python
import functools

import jax
import jax.numpy as jnp
from jax import lax
from jax.experimental import pallas as pl
from jax.experimental.pallas import tpu as pltpu
from jax.sharding import PartitionSpec as P

bf = jnp.bfloat16
f32 = jnp.float32
MESH = pl.DeviceIdType.MESH
VM = pltpu.VMEM
DMA = pltpu.SemaphoreType.DMA
D = 768
EPS = 1e-12
BIG = 1e30
C2 = 0.125 * 1.4426950408889634
RSQ2 = 0.7071067811865476
RS2PI = 0.3989422804014327
BQ = 256
WIN = BQ + 1024
TOKP = 8
HS = 192
VLIM = 58 * 2**20
FULL = pl.BlockSpec(memory_space=pltpu.VMEM)


def nt(a, b):
    return lax.dot_general(a, b, (((1,), (1,)), ((), ())), preferred_element_type=f32)


def nn(a, b):
    return lax.dot_general(a, b, (((1,), (0,)), ((), ())), preferred_element_type=f32)


def tn(a, b):
    return lax.dot_general(a, b, (((0,), (0,)), ((), ())), preferred_element_type=f32)


def bit(i, b):
    return lax.rem(lax.div(i, b), 2)


def flip(i, b):
    return i + b * (1 - 2 * bit(i, b))


def remote(src, dst, send, recv, device):
    return pltpu.make_async_remote_copy(
        src_ref=src, dst_ref=dst, send_sem=send, recv_sem=recv, device_id=device, device_id_type=MESH
    )


def greet(peers, others):
    bar = pltpu.get_barrier_semaphore()
    for d in peers:
        pl.semaphore_signal(bar, inc=1, device_id=d, device_id_type=MESH)
    for cond, d in others:

        @pl.when(cond)
        def _():
            pl.semaphore_signal(bar, inc=1, device_id=d, device_id_type=MESH)

    pl.semaphore_wait(bar, len(peers) + sum(cond.astype(jnp.int32) for cond, _ in others))


def vecs_of(vec):
    return (vec[0].astype(f32) + vec[1].astype(f32)) + (vec[2].astype(f32) + vec[3].astype(f32))


def member(pos0, rows, se):
    pos = pos0 + lax.broadcasted_iota(jnp.int32, (rows, 128), 0)
    return jnp.logical_and(pos >= se[0:1, :], pos < se[1:2, :])


def norm(h):
    c = h - jnp.mean(h, 1, keepdims=True)
    r = lax.rsqrt(jnp.mean(c * c, 1, keepdims=True) + EPS)
    return c * r, r


PIECES = [(0, 0, 192, 0, 768, 2), (1, 0, 192, 0, 768, 0), (2, 0, 192, 0, 768, 0), (3, 0, 192, 0, 768, 1)]
PIECES += [(4, 0, 192, None, 768, 1 if j < 3 else 2) for j in range(4)]
PIECES += [(5, 192 * j, 192, 0, 768, 1 if j in (1, 3) else 2) for j in range(4)]
YWIN = 4


def front_kernel(n, *refs):
    tok, *sh = refs[:7]
    *small, inner_v, cot_h, lens = refs[7:18]
    outs = refs[18:37]
    (xe, wq, wk, wv, wo, wi, wu, vecb, q_o, k_o, v_o, ctx, rt, nseg, act, dg, od, nrm, ad, sd, ct, gv, g2, xh1, acc, r1s, cot, lo, se, vec, vrow) = refs[37:68]
    ts, tr, ws, wr, vs, vr, ls, osem = refs[68:]
    full = (wq, wk, wv, wo, wi, wu)
    c = lax.axis_index("ctx")
    f = lax.axis_index("fsdp")
    sib = (c, flip(f, 1))
    yp = (c, flip(f, 2))
    dgn = (c, flip(flip(f, 1), 2))
    c1 = (flip(c, 1), f)
    c2 = (flip(c, 2), f)
    even = bit(c, 1) == 0
    fwd = jnp.where(even, c + 2, c - 2)
    src = jnp.where(even, c - 2, c + 2)
    has_fwd = jnp.logical_and(fwd >= 0, fwd < n)
    has_src = jnp.logical_and(src >= 0, src < n)
    oth = jnp.where(bit(c, 2) == 0, c - 2, c + 2)
    has_oth = jnp.logical_and(oth >= 0, oth < n)
    R = xe.shape[0] // 3

    locs = [pltpu.make_async_copy(tok, xe.at[pl.ds(R, R)], ls.at[0])]
    for i, (s, w) in enumerate(zip(sh, full)):
        H = s.shape[0]
        locs.append(pltpu.make_async_copy(s, w.at[pl.ds(pl.multiple_of(f * H, 16), H)], ls.at[1 + i]))
    locs.append(pltpu.make_async_copy(cot_h, cot, ls.at[7]))
    greet((sib, yp, dgn, c1, c2), ((has_oth, (oth, f)),))
    pr = R // TOKP
    pslot = jnp.where(even, 2 * R, 0)
    dslot = jnp.where(even, 0, 2 * R)
    tcp = [
        remote(
            tok.at[pl.ds(i * pr, pr)],
            xe.at[pl.ds(pl.multiple_of(dslot + i * pr, pr), pr)],
            ts.at[0, i],
            tr.at[0, i],
            c1,
        )
        for i in range(TOKP)
    ]
    vcp = [remote(vec, vecb.at[f], vs.at[i], vr.at[i], (sib, yp, dgn)[i]) for i in range(3)]
    wcp = []
    fy = flip(f, 2)
    for k, (t, r0, H2, c0, C, route) in enumerate(PIECES):
        s = sh[t]
        w = full[t]
        SR = s.shape[0]
        cg = cs_ = slice(c0, c0 + C) if c0 is not None else None
        if c0 is None:
            j = k - 4
            mix = flip(flip(f, 1), 2) if j == 3 else (flip(f, j) if j else f)
            far = flip(mix, 2)
            cg = pl.ds(pl.multiple_of(mix * C, 128), C)
            cs_ = pl.ds(pl.multiple_of(far * C, 128), C)
        own = pl.multiple_of(f * SR + r0, 16)
        if route == 0:
            other = pl.multiple_of(fy * SR + r0, 16)
            wcp.append(
                [
                    remote(s.at[pl.ds(r0, H2), cg], w.at[pl.ds(own, H2), cg], ws.at[k, 0], wr.at[k, 0], sib),
                    remote(s.at[pl.ds(r0, H2), cs_], w.at[pl.ds(own, H2), cs_], ws.at[k, 1], wr.at[k, 1], yp),
                    None,
                    remote(w.at[pl.ds(other, H2), cg], w.at[pl.ds(other, H2), cg], ws.at[k, 3], wr.at[k, 3], sib),
                    None,
                ]
            )
            continue
        H = H2 // 2
        p = c1 if route == 1 else c2
        hb = bit(c, route)
        mine = pl.multiple_of(f * SR + r0 + hb * H, 16)
        gy = pl.multiple_of(fy * SR + r0 + hb * H, 16)
        gx = pl.multiple_of(fy * SR + r0 + (1 - hb) * H, 16)
        wcp.append(
            [
                remote(s.at[pl.ds(r0, H2), cg], w.at[pl.ds(own, H2), cg], ws.at[k, 0], wr.at[k, 0], sib),
                remote(
                    s.at[pl.ds(pl.multiple_of(r0 + hb * H, 16), H), cs_],
                    w.at[pl.ds(mine, H), cs_],
                    ws.at[k, 1],
                    wr.at[k, 1],
                    yp,
                ),
                remote(w.at[pl.ds(gy, H), cg], w.at[pl.ds(gy, H), cg], ws.at[k, 2], wr.at[k, 2], p),
                remote(w.at[pl.ds(gy, H), cg], w.at[pl.ds(gy, H), cg], ws.at[k, 3], wr.at[k, 3], sib),
                remote(w.at[pl.ds(gx, H), cg], w.at[pl.ds(gx, H), cg], ws.at[k, 4], wr.at[k, 4], sib),
            ]
        )
    NPC = len(PIECES)
    for k in range(YWIN):
        wcp[k][1].start()
    for t in tcp[:2]:
        t.start()
    for cp in locs[:4]:
        cp.start()
    for k in range(3):
        wcp[k][0].start()

    w8 = D // 4
    sel = lax.broadcasted_iota(jnp.int32, (w8, D), 0) + f * w8 == lax.broadcasted_iota(jnp.int32, (w8, D), 1)
    place = jnp.where(sel, 1.0, 0.0).astype(bf)
    r8 = lax.broadcasted_iota(jnp.int32, (8, w8), 0)
    rows8 = jnp.zeros((8, w8), f32)
    for j, ref in enumerate(small):
        rows8 = jnp.where(r8 == j, jnp.broadcast_to(ref[...].astype(f32).reshape(1, w8), (8, w8)), rows8)
    rows8 = rows8.astype(bf)
    isf = lax.broadcasted_iota(jnp.int32, (8, D), 0) == f
    inner = jnp.where(isf, jnp.broadcast_to(inner_v[...].astype(f32).reshape(1, D), (8, D)), 0.0)
    vec[...] = jnp.concatenate([nn(rows8, place), inner], 0).astype(bf)
    for v in vcp:
        v.start()
    vecb[f] = vec[...]
    docs = lens.shape[1]
    ln8 = jnp.broadcast_to(lens[...].astype(f32), (8, docs))
    la = lax.broadcasted_iota(jnp.int32, (docs, 128), 0)
    lb = lax.broadcasted_iota(jnp.int32, (docs, 128), 1)
    upto = jnp.where(jnp.logical_and(la <= lb, lb < docs), 1.0, 0.0)
    below = jnp.where(jnp.logical_and(la < lb, lb < docs), 1.0, 0.0)
    hi = lax.Precision.HIGHEST
    ends = jnp.dot(ln8, upto, preferred_element_type=f32, precision=hi)
    starts = jnp.dot(ln8, below, preferred_element_type=f32, precision=hi)
    first_row = lax.broadcasted_iota(jnp.int32, (8, 128), 0) == 0
    se[...] = jnp.where(first_row, starts, ends).astype(jnp.int32)

    @pl.when(jnp.logical_not(has_src))
    def _():
        xe[pl.ds(pl.multiple_of(dslot, R), R), :] = jnp.zeros((R, D), bf)

    tfw = [
        remote(
            xe.at[pl.ds(pl.multiple_of(pslot + i * pr, pr), pr)],
            xe.at[pl.ds(pl.multiple_of(dslot + i * pr, pr), pr)],
            ts.at[1, i],
            tr.at[1, i],
            (fwd, f),
        )
        for i in range(TOKP)
    ]

    def y(k):
        wcp[k][1].wait_recv()
        if wcp[k][2] is not None:
            wcp[k][2].start()
        wcp[k][3].start()
        if k + YWIN < NPC:
            wcp[k + YWIN][1].start()

    def x(k):
        wcp[k][2].wait_recv()
        wcp[k][4].start()

    def t(i):
        tcp[i].wait_recv()
        if i + 2 < TOKP:
            tcp[i + 2].start()

        @pl.when(has_fwd)
        def _():
            tfw[i].start()

    def ready(ks, parts=(0, 3, 4)):
        for k in ks:
            for i in parts:
                if wcp[k][i] is not None:
                    wcp[k][i].wait_recv()

    t(0)
    y(0)
    t(1)
    t(2)
    x(0)
    for cp in locs[4:]:
        cp.start()
    for k in range(3, NPC):
        wcp[k][0].start()
    t(3)
    y(1)
    for i in range(4, TOKP - 1):
        t(i)
    y(2)
    t(TOKP - 1)
    for cp in locs[:4]:
        cp.wait()
    for v in vcp:
        v.wait_recv()
    ready(range(3))
    anchor = c * R
    V = vecs_of(vecb)
    vrow[...] = V

    def row(i):
        return V[i : i + 1, :]

    def out(i, ref):
        cp = pltpu.make_async_copy(ref, outs[i], osem.at[i])
        cp.start()
        sent.append(cp)

    sent = []
    for i, w in enumerate((wq, wk, wv)):
        out(i, w)

    def proj(r):
        def body(i, _):
            rr = pl.ds(pl.multiple_of(r + i * 256, 256), 256)
            xb = xe[rr, :]
            k_o[rr, :] = nn(xb, wk[...]).astype(bf)
            v_o[rr, :] = (nn(xb, wv[...]) + row(1)).astype(bf)
            return 0

        lax.fori_loop(0, R // 256, body, 0)

    def projq(i, _):
        rr = pl.ds(pl.multiple_of(R + i * 256, 256), 256)
        q_o[pl.ds(pl.multiple_of(i * 256, 256), 256), :] = (nn(xe[rr, :], wq[...]) + row(0)).astype(bf)
        return 0

    def seg(i, _):
        rr = pl.ds(pl.multiple_of(i * 256, 256), 256)
        nseg[rr, :] = jnp.where(member(anchor - R + i * 256, 256, se), 0.0, 1.0).astype(bf)
        return 0

    lax.fori_loop(0, 3 * R // 256, seg, 0)
    lax.fori_loop(0, R // 256, projq, 0)
    proj(R)
    y(3)
    proj(pslot)
    y(4)
    x(3)
    for i in range(TOKP):

        @pl.when(has_src)
        def _():
            tfw[i].wait_recv()

    proj(dslot)
    out(18, se)
    out(3, xe)
    out(4, q_o)
    out(5, k_o)
    out(6, v_o)
    lane = lax.broadcasted_iota(jnp.int32, (BQ, 128), 1)
    nqb = R // BQ

    def att(i, _):
        qb = lax.div(i, 6)
        hp = lax.rem(i, 6)
        qr = pl.ds(pl.multiple_of(qb * BQ, BQ), BQ)
        wr_ = pl.ds(pl.multiple_of(qb * BQ, BQ), WIN)
        hc = pl.ds(pl.multiple_of(hp * 128, 128), 128)
        oh = jnp.where(nseg[pl.ds(pl.multiple_of(R + qb * BQ, BQ), BQ), :] == 0, -BIG, 0.0).astype(bf)
        qp = q_o[qr, hc]
        kk = jnp.concatenate([k_o[wr_, hc], nseg[wr_, :]], 1)
        vv = v_o[wr_, hc]
        res = []
        for h in range(2):
            sel = (lane < 64) if h == 0 else (lane >= 64)
            qa = jnp.concatenate([jnp.where(sel, qp, jnp.zeros_like(qp)), oh], 1)
            pe = jnp.exp2(nt(qa, kk) * C2)
            res.append((nn(pe.astype(bf), vv), jnp.sum(pe, 1, keepdims=True)))
        o = jnp.where(lane < 64, res[0][0], res[1][0])
        tot = jnp.where(lane < 64, res[0][1], res[1][1])
        ctx[qr, hc] = (o / tot).astype(bf)
        rt[qr, hc] = tot
        return 0

    pumps = ((y, 5), (x, 4)), ((y, 6), (x, 5)), ((y, 7), (x, 6)), ((y, 8), (x, 7))
    per = 6 * nqb // len(pumps)
    for gidx, steps in enumerate(pumps):
        lax.fori_loop(gidx * per, gidx * per + per, att, 0)
        for step, k in steps:
            step(k)
    out(7, ctx)

    B = 256
    NB = R // B

    def rows(i, j=0):
        return pl.ds(pl.multiple_of(j * R + i * B, B), B)

    ready((3,))
    locs[4].wait()
    gv[...] = jnp.zeros_like(gv)

    def p1(i, _):
        r = rows(i)
        h = xe[pl.ds(pl.multiple_of(R + i * B, B), B), :].astype(f32) + nn(ctx[r, :], wo[...]) + row(2)
        xh, rr = norm(h)
        xh1[r, :] = xh
        r1s[r, :] = jnp.broadcast_to(rr, (B, 128))
        nrm[r, :] = (xh * row(4) + row(5)).astype(bf)
        return 0

    lax.fori_loop(0, NB, p1, 0)
    out(8, nrm)
    for cp in locs[5:]:
        cp.wait()
    ready((4, 5))
    ready(range(6, NPC), (0,))

    for jj in range(4):
        j = flip(flip(f, 1), 2) if jj == 3 else (flip(f, jj) if jj else f)
        if jj == 1:
            y(9)
            x(8)
        if jj == 2:
            y(10)
            x(9)
            y(11)
            x(10)
            x(11)
            ready(range(6, NPC), (3, 4))
        cs = pl.ds(pl.multiple_of(768 * j, 128), 768)
        ws_ = pl.ds(pl.multiple_of(768 * j, 16), 768)
        bi = vrow[pl.ds(8 + j, 1), :]

        def p2(i, _, cs=cs, ws_=ws_, bi=bi, j=j, jj=jj):
            r = rows(i)
            rj = rows(i, j)
            pre = nn(nrm[r, :], wi[:, cs]) + bi
            cdf = 0.5 + 0.5 * lax.erf(pre * RSQ2)
            pdf = jnp.exp(pre * pre * -0.5) * RS2PI
            a = (pre * cdf).astype(bf)
            act[rj, :] = a
            dg[rj, :] = (cdf + pre * pdf).astype(bf)
            o = nn(a, wu[ws_, :])
            if jj == 0:
                acc[r, :] = o
            else:
                acc[r, :] += o
            return 0

        lax.fori_loop(0, NB, p2, 0)
    out(9, act)

    def p3(i, _):
        r = rows(i)
        h = nrm[r, :].astype(f32) + acc[r, :] + row(3)
        xh, rr = norm(h)
        lo[r, :] = (xh * row(6) + row(7)).astype(bf)
        g = cot[r, :].astype(f32)
        gv[6:7, :] += jnp.sum(g * xh, 0, keepdims=True)
        gv[7:8, :] += jnp.sum(g, 0, keepdims=True)
        e = g * row(6)
        d = rr * (e - jnp.mean(e, 1, keepdims=True) - xh * jnp.mean(e * xh, 1, keepdims=True))
        g2[r, :] = d
        db = d.astype(bf)
        od[r, :] = db
        gv[3:4, :] += jnp.sum(db.astype(f32), 0, keepdims=True)
        return 0

    lax.fori_loop(0, NB, p3, 0)
    out(10, lo)
    out(11, od)
    for j in range(4):
        cs = slice(768 * j, 768 * j + 768)

        def p4(i, _, cs=cs, j=j):
            r = rows(i)
            rj = rows(i, j)
            d = (nt(od[r, :], wu[cs, :]) * dg[rj, :].astype(f32)).astype(bf)
            dg[rj, :] = d
            gv[8 + j : 9 + j, :] += jnp.sum(d.astype(f32), 0, keepdims=True)
            g2[r, :] += nt(d, wi[:, cs])
            return 0

        lax.fori_loop(0, NB, p4, 0)
    out(12, dg)
    heads = lax.broadcasted_iota(jnp.int32, (16, D), 0)
    onehot = jnp.where(lax.div(lax.broadcasted_iota(jnp.int32, (16, D), 1), 64) == heads, 1.0, 0.0)
    for i in range(NB):
        r = slice(i * B, i * B + B)
        g = g2[r, :]
        xh = xh1[r, :]
        rr = r1s[r, 0:1]
        gv[4:5, :] += jnp.sum(g * xh, 0, keepdims=True)
        gv[5:6, :] += jnp.sum(g, 0, keepdims=True)
        e = g * row(4)
        d = rr * (e - jnp.mean(e, 1, keepdims=True) - xh * jnp.mean(e * xh, 1, keepdims=True))
        g2[r, :] = d
        db = d.astype(bf)
        ad[r, :] = db
        gv[2:3, :] += jnp.sum(db.astype(f32), 0, keepdims=True)
        cd = nt(db, wo[...]).astype(bf).astype(f32)
        sc = cd * (1.0 / rt[r, :])
        sd[r, :] = sc.astype(bf)
        ct[:, r] = lax.dot_general(
            onehot,
            sc * ctx[r, :].astype(f32),
            (((1,), (1,)), ((), ())),
            preferred_element_type=f32,
            precision=lax.Precision.HIGHEST,
        )
    for i, ref in ((13, ad), (14, sd), (15, ct), (16, gv), (17, g2)):
        out(i, ref)
    for i in range(TOKP):

        @pl.when(has_fwd)
        def _():
            tfw[i].wait_send()

        tcp[i].wait_send()
    for cps in wcp:
        for cp in cps:
            if cp is not None:
                cp.wait_send()
    for v in vcp:
        v.wait_send()
    for cp in sent:
        cp.wait()


def front(n, tok, shards, vecs, cot, lens):
    R = tok.shape[0]
    S = jax.ShapeDtypeStruct
    ANY = pl.BlockSpec(memory_space=pl.ANY)
    F = shards[4].shape[1]
    NPC = len(PIECES)
    row = (R, D)
    W = (D, D)
    outs = [S(W, bf)] * 3 + [S((3 * R, D), bf), S(row, bf), S((3 * R, D), bf), S((3 * R, D), bf)]
    outs += [S(row, bf), S(row, bf), S((4 * R, D), bf), S(row, bf), S(row, bf), S((4 * R, D), bf)]
    outs += [S(row, bf), S(row, bf), S((16, R), f32), S((16, D), f32), S(row, f32), S((8, 128), jnp.int32)]
    scratch = [VM((3 * R, D), bf)] + [VM(W, bf)] * 4 + [VM((D, F), bf), VM((F, D), bf), VM((4, 16, D), bf)]
    scratch += [VM(row, bf), VM((3 * R, D), bf), VM((3 * R, D), bf), VM(row, bf), VM(row, f32), VM((3 * R, 128), bf)]
    scratch += [VM((4 * R, D), bf), VM((4 * R, D), bf)] + [VM(row, bf)] * 4
    scratch += [VM((16, R), f32), VM((16, D), f32), VM(row, f32), VM(row, f32), VM(row, f32), VM((R, 128), f32)]
    scratch += [VM(row, bf), VM(row, bf), VM((8, 128), jnp.int32), VM((16, D), bf), VM((16, D), f32)]
    scratch += [DMA((2, TOKP)), DMA((2, TOKP)), DMA((NPC, 5)), DMA((NPC, 5)), DMA((3,)), DMA((3,)), DMA((8,)), DMA((19,))]
    return pl.pallas_call(
        functools.partial(front_kernel, n),
        out_shape=outs,
        in_specs=[ANY] * 7 + [FULL] * 9 + [ANY, FULL],
        out_specs=[ANY] * 19,
        scratch_shapes=scratch,
        compiler_params=pltpu.CompilerParams(collective_id=1, has_side_effects=True, vmem_limit_bytes=VLIM),
        name="front",
    )(tok, *shards, *vecs, cot, lens)


NP = 12
NH = 2 * NP
WINDOW = 3
LATE = NH
LAG = 2
TURN = 3
HCH = 16
HLAG = 3


def extra_bits(n):
    return [1 << j for j in range(3, 16) if (1 << j) < n]


def add_rows(dst, a, b, rows, step=48):
    def body(i, _):
        r = pl.ds(pl.multiple_of(i * step, 16), step)
        dst[r, :] = a[r, :] + b[r, :]
        return 0

    lax.fori_loop(0, rows // step, body, 0)


def back_kernel(n, *refs):
    hbm = refs[:14]
    gvin, ct, se = refs[14:17]
    OUT, vout, hin, gx_o = refs[17:21]
    bufs = refs[21:32]
    A, od, nrm, I, ctx, ad, q, k_, v_, sd, xe = bufs
    wq = k_.at[pl.ds(0, D)]
    wk = v_.at[pl.ds(0, D)]
    wv = v_.at[pl.ds(D, D)]
    bufs = bufs + (wq, wk, wv)
    G, RC, RY, RX, RZ, RW, RE, VR, vacc, HR, nseg, dk, dv = refs[32:45]
    ld, cs, cr, ss, sr, vs, vr, hs, hrs = refs[45:]
    dqb = q
    R = q.shape[0]
    extra = extra_bits(n)
    c = lax.axis_index("ctx")
    f = lax.axis_index("fsdp")
    cb = bit(f, 1)
    yb = bit(f, 2)
    sib = (c, flip(f, 1))
    yp = (c, flip(f, 2))
    p = [(flip(c, 1 << j), f) for j in range(3)]
    peers = [sib, yp] + p + [(flip(c, b), f) for b in extra]
    odd = bit(c, 1) == 1
    fwd = jnp.where(odd, c + 2, c - 2)
    src = jnp.where(odd, c - 2, c + 2)
    has_fwd = jnp.logical_and(fwd >= 0, fwd < n)
    has_src = jnp.logical_and(src >= 0, src < n)
    oth = jnp.where(bit(c, 2) == 0, c - 2, c + 2)
    has_oth = jnp.logical_and(oth >= 0, oth < n)
    loads = [pltpu.make_async_copy(hbm[i], bufs[i], ld.at[i]) for i in range(14)]
    for cp in loads[:10]:
        cp.start()
    greet(peers, ((has_oth, (oth, f)),))
    loads[10].start()

    bit0 = bit(c, 1)
    bit1 = bit(c, 2)

    def turned(m):
        return (m % TURN == TURN - 1) if isinstance(m, int) else (lax.rem(m, TURN) == TURN - 1)

    def pick(m, one, two):
        t = turned(m)
        if isinstance(t, bool):
            return two if t else one
        return jnp.where(t, two, one)

    def core(k, yy):
        return remote(G.at[k, 2 * yy + (1 - cb)], RC.at[k, yy], cs.at[k, yy], cr.at[k, yy], sib)

    def place(m):
        return (m // 2, m % 2) if isinstance(m, int) else (lax.div(m, 2), lax.rem(m, 2))

    def quarter(m, q):
        k, h = place(m)
        return G.at[k, q, h]

    def part(ref, m, r=None):
        k, h = place(m)
        return ref.at[k, h] if r is None else ref.at[k, h, r]

    def put(k, g):
        for h in range(2):
            G[k, :, h] = g[:, 384 * h : 384 * h + 384].astype(bf).reshape(4, 192, 384)

    def first(m):
        return pl.multiple_of(pick(m, bit0, bit1) * 96, 16)

    def second(m):
        return first(m) + pl.multiple_of(pick(m, bit1, bit0) * 48, 16)

    def rows_of(ref, m, r, size):
        return ref.at[pl.ds(pl.multiple_of(r, 16), size)]

    def acc(m):
        return quarter(m, 2 * yb + cb)

    def spare(m, i):
        return part(RY, m, pl.ds(48 * (i % 4), 48))

    def copy(m, i):
        s = (ss.at[m, i], sr.at[m, i])
        pa = (pick(m, flip(c, 1), flip(c, 2)), f)
        pb = (pick(m, flip(c, 2), flip(c, 1)), f)
        if i == 0:
            return remote(quarter(m, 2 * (1 - yb) + cb), part(RY, m), *s, yp)
        if i == 1:
            return remote(rows_of(acc(m), m, 96 - first(m), 96), part(RX, m), *s, pa)
        if i == 2:
            r = first(m) + 48 - pick(m, bit1, bit0) * 48
            return remote(rows_of(acc(m), m, r, 48), part(RZ, m), *s, pb)
        if i == 3:
            return remote(rows_of(acc(m), m, second(m), 48), part(RW, m), *s, p[2])
        if i == 4:
            o = part(OUT, m, pl.ds(pl.multiple_of(second(m), 16), 48))
            return remote(o, o, *s, pb)
        if i == 5:
            o = part(OUT, m, pl.ds(first(m), 96))
            return remote(o, o, *s, pa)
        e = extra[i - 6]
        return remote(spare(m, i - 6), part(RE.at[i - 6], m), *s, (flip(c, e), f))

    def give(k):
        for yy in range(2):
            core(k, yy).start()

    def s1(k):
        for yy in range(2):
            core(k, yy).wait_recv()
        for yy in range(2):
            for h in range(2):
                g = G.at[k, 2 * yy + cb, h]
                add_rows(g, g, RC.at[k, yy, h], 192)

    def s2(m):
        copy(m, 0).wait_recv()
        if isinstance(m, int):
            if m + WINDOW < LATE:
                copy(m + WINDOW, 0).start()
        else:

            @pl.when(m + WINDOW < LATE)
            def _():
                copy(m + WINDOW, 0).start()

        add_rows(acc(m), acc(m), part(RY, m), 192)
        copy(m, 1).start()

    def s3(m):
        copy(m, 1).wait_recv()
        a = rows_of(acc(m), m, first(m), 96)
        add_rows(a, a, part(RX, m), 96)
        copy(m, 2).start()

    def s4(m):
        copy(m, 2).wait_recv()
        a = rows_of(acc(m), m, second(m), 48)
        add_rows(a, a, part(RZ, m), 48)
        copy(m, 3).start()

    def s5(m):
        copy(m, 3).wait_recv()
        last = rows_of(acc(m), m, second(m), 48)
        got = part(RW, m)
        for i in range(len(extra)):
            add_rows(spare(m, i), last, got, 48)
            copy(m, 6 + i).start()
            copy(m, 6 + i).wait_recv()
            last = spare(m, i)
            got = part(RE.at[i], m)
        add_rows(part(OUT, m, pl.ds(pl.multiple_of(second(m), 16), 48)), last, got, 48)
        copy(m, 4).start()

    def s6(m):
        copy(m, 4).wait_recv()
        copy(m, 5).start()

    def s7(m):
        copy(m, 5).wait_recv()

    stages = (s2, s3, s4, s5, s6, s7)

    def tick(t):
        for i in reversed(range(len(stages))):
            m = t - LAG * i
            if isinstance(t, int):
                if 0 <= m < NH:
                    stages[i](m)
            else:

                @pl.when(jnp.logical_and(m >= 0, m < NH))
                def _():
                    stages[i](m)

    def both(t):
        for i in reversed(range(len(stages))):
            for m in (t - LAG * i, t + 1 - LAG * i):
                if 0 <= m < NH:
                    stages[i](m)

    def outer(hh, qq):
        g = tn(A[pl.ds(pl.multiple_of(qq * R, R), R), 384 * hh : 384 * hh + 384], od[...]).astype(bf)
        for h in range(2):
            G[2 * hh, qq, h] = g[:192, 384 * h : 384 * h + 384]
            G[2 * hh + 1, qq, h] = g[192:, 384 * h : 384 * h + 384]

    loads[0].wait()
    loads[1].wait()
    for hh in range(2):
        for yy in range(2):
            outer(hh, 2 * yy + (1 - cb))
        give(2 * hh)
        give(2 * hh + 1)
        for yy in range(2):
            outer(hh, 2 * yy + cb)
    for k in range(2):
        s1(k)
        for m in (2 * k, 2 * k + 1):
            if m < WINDOW:
                copy(m, 0).start()
    loads[2].wait()
    loads[3].wait()
    for j in range(4):
        put(4 + j, tn(nrm[...], I[R * j : R * j + R, :]))
        give(4 + j)
        if j < 2:
            s1(2 + j)
        if j == 2:
            tick(0)
    s1(4)
    tick(1)
    loads[4].wait()
    loads[5].wait()
    put(8, tn(ctx[...], ad[...]))
    give(8)
    for k in (5, 6, 7):
        s1(k)
    tick(2)
    s1(8)

    anchor = c * R

    def prep(i, _):
        r = pl.ds(pl.multiple_of(i * 256, 256), 256)
        nseg[r, :] = jnp.where(member(anchor - R + i * 256, 256, se), 0.0, 1.0).astype(bf)
        dk[r, :] = jnp.zeros((256, 128), f32)
        dv[r, :] = jnp.zeros((256, 128), f32)
        return 0

    lax.fori_loop(0, 3 * R // 256, prep, 0)
    lane = lax.broadcasted_iota(jnp.int32, (BQ, 128), 1)
    nqb = R // BQ
    for i in range(6, 10):
        loads[i].wait()

    def head(i, _):
        hp = lax.div(i, nqb)
        qb = lax.rem(i, nqb)
        hc = pl.ds(pl.multiple_of(hp * 128, 128), 128)
        qr = pl.ds(pl.multiple_of(qb * BQ, BQ), BQ)
        wr = pl.ds(pl.multiple_of(qb * BQ, BQ), WIN)
        oh = jnp.where(nseg[pl.ds(pl.multiple_of(R + qb * BQ, BQ), BQ), :] == 0, -BIG, 0.0).astype(bf)
        qp = q[qr, hc]
        sp = sd[qr, hc]
        kp = k_[wr, hc]
        vp = v_[wr, hc]
        kk = jnp.concatenate([kp, nseg[wr, :]], 1)
        z = jnp.zeros_like(qp)
        dkp = []
        dvp = []
        dqs = []
        for h in range(2):
            sel = (lane < 64) if h == 0 else (lane >= 64)
            qm = jnp.where(sel, qp, z)
            sm = jnp.where(sel, sp, z)
            pr = jnp.exp2(nt(kk, jnp.concatenate([qm, oh], 1)) * C2)
            dp = nt(vp, sm)
            ds = (pr * (dp - ct[pl.ds(2 * hp + h, 1), qr])).astype(bf)
            dvp.append(nn(pr.astype(bf), sm))
            dkp.append(nn(ds, qm))
            dqs.append(tn(ds, kp))
        dk[wr, :] += dkp[0] + dkp[1]
        dv[wr, :] += dvp[0] + dvp[1]
        dqb[qr, hc] = (jnp.where(lane < 64, dqs[0], dqs[1]) * 0.125).astype(bf)

        @pl.when(qb == nqb - 1)
        def _():
            def fin(j, _):
                r = pl.ds(pl.multiple_of(j * 256, 256), 256)
                A[r, hc] = (dk[r, :] * 0.125).astype(bf)
                I[r, hc] = dv[r, :].astype(bf)
                dk[r, :] = jnp.zeros((256, 128), f32)
                dv[r, :] = jnp.zeros((256, 128), f32)
                return 0

            lax.fori_loop(0, 3 * R // 256, fin, 0)

        tick(i + 3)

        return 0

    lax.fori_loop(0, 6 * nqb, head, 0)
    t = 6 * nqb + 3

    W3 = 3 * R
    own = slice(R, 2 * R)
    for cp in loads[11:]:
        cp.start()
    loads[10].wait()
    vacc[0] = gvin[...]
    vacc[0, 0:1, :] = jnp.sum(dqb[...].astype(f32), 0, keepdims=True)
    vacc[0, 1:2, :] = jnp.sum(I[0:W3, :].astype(f32), 0, keepdims=True)
    for cp in loads[11:]:
        cp.wait()
    for dst, r in ((od, slice(0, R)), (nrm, slice(2 * R, W3))):
        dst[...] = (nt(A[r, :], wk[...]) + nt(I[r, :], wv[...])).astype(bf)

    @pl.when(odd)
    def _():
        ad[...] = od[...]

    @pl.when(jnp.logical_not(odd))
    def _():
        ad[...] = nrm[...]

    hn = R // HCH

    def leg1(ref, j):
        r = pl.ds(j * hn, hn)
        return remote(ref.at[r], HR.at[r], hs.at[0, j], hrs.at[0, j], (fwd, f))

    def leg2(j):
        r = pl.ds(j * hn, hn)
        return remote(ad.at[r], hin.at[r], hs.at[1, j], hrs.at[1, j], p[0])

    def halo(j):
        if 0 <= j < HCH:

            @pl.when(jnp.logical_and(has_fwd, odd))
            def _():
                leg1(nrm, j).start()

            @pl.when(jnp.logical_and(has_fwd, jnp.logical_not(odd)))
            def _():
                leg1(od, j).start()

        j = j - HLAG
        if 0 <= j < HCH:

            @pl.when(has_src)
            def _():
                leg1(od, j).wait_recv()
                r = pl.ds(j * hn, hn)
                add_rows(ad.at[r], ad.at[r], HR.at[r], hn, 32)

            leg2(j).start()

    halo(0)
    put(9, tn(xe[...], I[0:W3, :]))
    give(9)
    halo(1)
    put(10, tn(xe[...], A[0:W3, :]))
    give(10)
    s1(9)
    tick(t)
    halo(2)
    tick(t + 1)
    put(11, tn(xe[own, :], dqb[...]))
    give(11)
    s1(10)
    tick(t + 2)
    halo(3)
    tick(t + 3)
    ctx[...] = (nt(dqb[...], wq[...]) + nt(A[own, :], wk[...]) + nt(I[own, :], wv[...])).astype(bf)
    gxc = pltpu.make_async_copy(ctx, gx_o, ld.at[14])
    gxc.start()
    s1(11)
    vround = 0
    hj = 4
    for step in range(t + 4, NH + LAG * (len(stages) - 1)):
        if step < NH:
            tick(step)
        elif (step - NH) % 2 == 0:
            both(step)
        halo(hj)
        hj += 1
        if vround <= len(peers) and step % 2 == 0:
            if vround > 0:
                exchange.wait()
                vacc[vround] = vacc[vround - 1] + VR[vround - 1]
            if vround < len(peers):
                exchange = remote(vacc.at[vround], VR.at[vround], vs.at[vround], vr.at[vround], peers[vround])
                exchange.start()
            vround += 1
    while vround <= len(peers):
        exchange.wait()
        vacc[vround] = vacc[vround - 1] + VR[vround - 1]
        if vround < len(peers):
            exchange = remote(vacc.at[vround], VR.at[vround], vs.at[vround], vr.at[vround], peers[vround])
            exchange.start()
        vround += 1
    while hj < HCH + HLAG:
        halo(hj)
        hj += 1
    vout[...] = vacc[len(peers)]
    for j in range(HCH):
        leg2(j).wait()

        @pl.when(has_fwd)
        def _():
            leg1(od, j).wait_send()

    def done(m, _):
        core(lax.div(m, 2), lax.rem(m, 2)).wait_send()
        for i in range(6 + len(extra)):
            copy(m, i).wait_send()
        return 0

    lax.fori_loop(0, NH, done, 0)
    gxc.wait()


def back(n, act, od, nrm, idel, ctx, ad, q, k, v, sd, xe, wq, wk, wv, gv, ct, se):
    R = q.shape[0]
    ne = len(extra_bits(n))
    nv = 5 + ne
    S = jax.ShapeDtypeStruct
    ANY = pl.BlockSpec(memory_space=pl.ANY)
    big = (act, od, nrm, idel, ctx, ad, q, k, v, sd, xe, wq, wk, wv)
    return pl.pallas_call(
        functools.partial(back_kernel, n),
        out_shape=[S((NP, 2, 192, 384), bf), S((16, D), f32), S((R, D), bf), S((R, D), bf)],
        in_specs=[ANY] * 14 + [FULL] * 3,
        out_specs=[FULL] * 3 + [ANY],
        scratch_shapes=[VM(t.shape, t.dtype) for t in big[:11]]
        + [
            VM((NP, 4, 2, 192, 384), bf),
            VM((NP, 2, 2, 192, 384), bf),
            VM((NP, 2, 192, 384), bf),
            VM((NP, 2, 96, 384), bf),
            VM((NP, 2, 48, 384), bf),
            VM((NP, 2, 48, 384), bf),
            VM((ne, NP, 2, 48, 384) if ne else (1, 1, 2, 48, 384), bf),
            VM((nv, 16, D), f32),
            VM((nv + 1, 16, D), f32),
            VM((R, D), bf),
            VM((3 * R, 128), bf),
            VM((3 * R, 128), f32),
            VM((3 * R, 128), f32),
            DMA((15,)),
            DMA((NP, 2)),
            DMA((NP, 2)),
            DMA((NH, 6 + ne)),
            DMA((NH, 6 + ne)),
            DMA((nv,)),
            DMA((nv,)),
            DMA((2, HCH)),
            DMA((2, HCH)),
        ],
        compiler_params=pltpu.CompilerParams(collective_id=2, has_side_effects=True, vmem_limit_bytes=61 * 2**20),
        name="back",
    )(*big, gv, ct, se)


def last_kernel(g, gv, g1, gx, hin, gq, gk, gw, go, gi, gu, gt, *vecs):
    for h in range(2):
        cs = slice(384 * h, 384 * h + 384)
        for ref, k in ((gw, 9), (gk, 10), (gq, 11), (go, 8)):
            ref[:, cs] = g[k, h].astype(f32)
        for j in range(4):
            gi[:, 768 * j + 384 * h : 768 * j + 384 * h + 384] = g[4 + j, h].astype(f32)
            gu[192 * j : 192 * j + 192, cs] = g[j, h].astype(f32)
    gt[...] = g1[...] + gx[...].astype(f32) + hin[...].astype(f32)
    f = lax.axis_index("fsdp")
    w = D // 4
    own = lax.broadcasted_iota(jnp.int32, (D, w), 0) == lax.broadcasted_iota(jnp.int32, (D, w), 1) + f * w
    rows = lax.dot_general(
        gv[0:8, :],
        jnp.where(own, 1.0, 0.0),
        (((1,), (0,)), ((), ())),
        preferred_element_type=f32,
        precision=lax.Precision.HIGHEST,
    )
    for j in range(8):
        vecs[j][...] = rows[j : j + 1, :].reshape(w)
    vecs[8][...] = gv[pl.ds(8 + f, 1), :].reshape(D)


def last(g, gv, g1, gx, hin):
    R = g1.shape[0]
    S = jax.ShapeDtypeStruct
    outs = [S((192, D), f32)] * 4 + [S((192, 4 * D), f32), S((4 * 192, D), f32), S((R, D), f32)]
    outs += [S((D // 4,), f32)] * 8 + [S((D,), f32)]
    return pl.pallas_call(
        last_kernel,
        out_shape=outs,
        in_specs=[FULL] * 5,
        out_specs=[FULL] * 16,
        compiler_params=pltpu.CompilerParams(vmem_limit_bytes=VLIM),
        name="last",
    )(g, gv, g1, gx, hin)


def local(n, tokens, doc_lengths, cotangent, wq, wk, wv, wo, wi, wu, bq, bv, bo, bi, bu, ga, sa, gf, sf):
    x = tokens[0]
    docs = doc_lengths.shape[1]
    assert docs <= 128 and x.shape[0] == 512
    vecs = (bq, bv, bo, bu, ga, sa, gf, sf, bi)
    wq, wk, wv, xe, q, k, v, ctx, nrm, act, layer_out, od, idel, ad, sd, ct, gv, g1, se = front(
        n, x, (wq, wk, wv, wo, wi, wu), vecs, cotangent[0], doc_lengths
    )
    g, gv, hin, gx = back(n, act, od, nrm, idel, ctx, ad, q, k, v, sd, xe, wq, wk, wv, gv, ct, se)
    gq, gk, gw, go, gi, gu, gt, *gs, gbi = last(g, gv, g1, gx, hin)
    return (layer_out[None], gt[None], gq, gk, gw, go, gi, gu, gs[0], gs[1], gs[2], gbi, *gs[3:])


def solution(mesh):
    n = mesh.shape["ctx"]
    tok = P("fsdp", "ctx", None)
    mat = P("fsdp", None)
    vec = P("fsdp")
    return jax.shard_map(
        functools.partial(local, n),
        mesh=mesh,
        in_specs=(tok, mat, tok) + (mat,) * 6 + (vec,) * 9,
        out_specs=(tok, tok) + (mat,) * 6 + (vec,) * 9,
        check_vma=False,
    )
```

```python
import functools

import jax
import jax.numpy as jnp
from jax import lax
from jax.experimental import pallas as pl
from jax.experimental.pallas import tpu as pltpu
from jax.sharding import PartitionSpec as P

bf = jnp.bfloat16
f32 = jnp.float32
MESH = pl.DeviceIdType.MESH
VM = pltpu.VMEM
DMA = pltpu.SemaphoreType.DMA
D = 768
EPS = 1e-12
BIG = 1e30
C2 = 0.125 * 1.4426950408889634
RSQ2 = 0.7071067811865476
RS2PI = 0.3989422804014327
BQ = 256
WIN = BQ + 1024
TOKP = 8
HS = 192
VLIM = 58 * 2**20
FULL = pl.BlockSpec(memory_space=pltpu.VMEM)


def nt(a, b):
    return lax.dot_general(a, b, (((1,), (1,)), ((), ())), preferred_element_type=f32)


def nn(a, b):
    return lax.dot_general(a, b, (((1,), (0,)), ((), ())), preferred_element_type=f32)


def tn(a, b):
    return lax.dot_general(a, b, (((0,), (0,)), ((), ())), preferred_element_type=f32)


def bit(i, b):
    return lax.rem(lax.div(i, b), 2)


def flip(i, b):
    return i + b * (1 - 2 * bit(i, b))


def remote(src, dst, send, recv, device):
    return pltpu.make_async_remote_copy(
        src_ref=src, dst_ref=dst, send_sem=send, recv_sem=recv, device_id=device, device_id_type=MESH
    )


def greet(peers, others):
    bar = pltpu.get_barrier_semaphore()
    for d in peers:
        pl.semaphore_signal(bar, inc=1, device_id=d, device_id_type=MESH)
    for cond, d in others:

        @pl.when(cond)
        def _():
            pl.semaphore_signal(bar, inc=1, device_id=d, device_id_type=MESH)

    pl.semaphore_wait(bar, len(peers) + sum(cond.astype(jnp.int32) for cond, _ in others))


def vecs_of(vec):
    return (vec[0].astype(f32) + vec[1].astype(f32)) + (vec[2].astype(f32) + vec[3].astype(f32))


def member(pos0, rows, se):
    pos = pos0 + lax.broadcasted_iota(jnp.int32, (rows, 128), 0)
    return jnp.logical_and(pos >= se[0:1, :], pos < se[1:2, :])


def norm(h):
    c = h - jnp.mean(h, 1, keepdims=True)
    r = lax.rsqrt(jnp.mean(c * c, 1, keepdims=True) + EPS)
    return c * r, r


PIECES = [(0, 0, 192, 0, 768, 2), (1, 0, 192, 0, 768, 0), (2, 0, 192, 0, 768, 0), (3, 0, 192, 0, 768, 1)]
PIECES += [(4, 0, 192, None, 768, 1 if j < 3 else 2) for j in range(4)]
PIECES += [(5, 192 * j, 192, 0, 768, 1 if j in (1, 3) else 2) for j in range(4)]
YWIN = 4


def front_kernel(n, *refs):
    tok, *sh = refs[:7]
    *small, inner_v, cot_h, lens = refs[7:18]
    outs = refs[18:37]
    (xe, wq, wk, wv, wo, wi, wu, vecb, q_o, k_o, v_o, ctx, rt, nseg, act, dg, od, nrm, ad, sd, ct, gv, g2, xh1, acc, r1s, cot, lo, se, vec, vrow) = refs[37:68]
    ts, tr, ws, wr, vs, vr, ls, osem = refs[68:]
    full = (wq, wk, wv, wo, wi, wu)
    c = lax.axis_index("ctx")
    f = lax.axis_index("fsdp")
    sib = (c, flip(f, 1))
    yp = (c, flip(f, 2))
    dgn = (c, flip(flip(f, 1), 2))
    c1 = (flip(c, 1), f)
    c2 = (flip(c, 2), f)
    even = bit(c, 1) == 0
    fwd = jnp.where(even, c + 2, c - 2)
    src = jnp.where(even, c - 2, c + 2)
    has_fwd = jnp.logical_and(fwd >= 0, fwd < n)
    has_src = jnp.logical_and(src >= 0, src < n)
    oth = jnp.where(bit(c, 2) == 0, c - 2, c + 2)
    has_oth = jnp.logical_and(oth >= 0, oth < n)
    R = xe.shape[0] // 3

    locs = [pltpu.make_async_copy(tok, xe.at[pl.ds(R, R)], ls.at[0])]
    for i, (s, w) in enumerate(zip(sh, full)):
        H = s.shape[0]
        locs.append(pltpu.make_async_copy(s, w.at[pl.ds(pl.multiple_of(f * H, 16), H)], ls.at[1 + i]))
    locs.append(pltpu.make_async_copy(cot_h, cot, ls.at[7]))
    greet((sib, yp, dgn, c1, c2), ((has_oth, (oth, f)),))
    pr = R // TOKP
    pslot = jnp.where(even, 2 * R, 0)
    dslot = jnp.where(even, 0, 2 * R)
    tcp = [
        remote(
            tok.at[pl.ds(i * pr, pr)],
            xe.at[pl.ds(pl.multiple_of(dslot + i * pr, pr), pr)],
            ts.at[0, i],
            tr.at[0, i],
            c1,
        )
        for i in range(TOKP)
    ]
    vcp = [remote(vec, vecb.at[f], vs.at[i], vr.at[i], (sib, yp, dgn)[i]) for i in range(3)]
    wcp = []
    fy = flip(f, 2)
    for k, (t, r0, H2, c0, C, route) in enumerate(PIECES):
        s = sh[t]
        w = full[t]
        SR = s.shape[0]
        cg = cs_ = slice(c0, c0 + C) if c0 is not None else None
        if c0 is None:
            j = k - 4
            mix = flip(flip(f, 1), 2) if j == 3 else (flip(f, j) if j else f)
            far = flip(mix, 2)
            cg = pl.ds(pl.multiple_of(mix * C, 128), C)
            cs_ = pl.ds(pl.multiple_of(far * C, 128), C)
        own = pl.multiple_of(f * SR + r0, 16)
        if route == 0:
            other = pl.multiple_of(fy * SR + r0, 16)
            wcp.append(
                [
                    remote(s.at[pl.ds(r0, H2), cg], w.at[pl.ds(own, H2), cg], ws.at[k, 0], wr.at[k, 0], sib),
                    remote(s.at[pl.ds(r0, H2), cs_], w.at[pl.ds(own, H2), cs_], ws.at[k, 1], wr.at[k, 1], yp),
                    None,
                    remote(w.at[pl.ds(other, H2), cg], w.at[pl.ds(other, H2), cg], ws.at[k, 3], wr.at[k, 3], sib),
                    None,
                ]
            )
            continue
        H = H2 // 2
        p = c1 if route == 1 else c2
        hb = bit(c, route)
        mine = pl.multiple_of(f * SR + r0 + hb * H, 16)
        gy = pl.multiple_of(fy * SR + r0 + hb * H, 16)
        gx = pl.multiple_of(fy * SR + r0 + (1 - hb) * H, 16)
        wcp.append(
            [
                remote(s.at[pl.ds(r0, H2), cg], w.at[pl.ds(own, H2), cg], ws.at[k, 0], wr.at[k, 0], sib),
                remote(
                    s.at[pl.ds(pl.multiple_of(r0 + hb * H, 16), H), cs_],
                    w.at[pl.ds(mine, H), cs_],
                    ws.at[k, 1],
                    wr.at[k, 1],
                    yp,
                ),
                remote(w.at[pl.ds(gy, H), cg], w.at[pl.ds(gy, H), cg], ws.at[k, 2], wr.at[k, 2], p),
                remote(w.at[pl.ds(gy, H), cg], w.at[pl.ds(gy, H), cg], ws.at[k, 3], wr.at[k, 3], sib),
                remote(w.at[pl.ds(gx, H), cg], w.at[pl.ds(gx, H), cg], ws.at[k, 4], wr.at[k, 4], sib),
            ]
        )
    NPC = len(PIECES)
    for k in range(YWIN):
        wcp[k][1].start()
    for t in tcp[:2]:
        t.start()
    for cp in locs[:4]:
        cp.start()
    for k in range(3):
        wcp[k][0].start()

    w8 = D // 4
    sel = lax.broadcasted_iota(jnp.int32, (w8, D), 0) + f * w8 == lax.broadcasted_iota(jnp.int32, (w8, D), 1)
    place = jnp.where(sel, 1.0, 0.0).astype(bf)
    r8 = lax.broadcasted_iota(jnp.int32, (8, w8), 0)
    rows8 = jnp.zeros((8, w8), f32)
    for j, ref in enumerate(small):
        rows8 = jnp.where(r8 == j, jnp.broadcast_to(ref[...].astype(f32).reshape(1, w8), (8, w8)), rows8)
    rows8 = rows8.astype(bf)
    isf = lax.broadcasted_iota(jnp.int32, (8, D), 0) == f
    inner = jnp.where(isf, jnp.broadcast_to(inner_v[...].astype(f32).reshape(1, D), (8, D)), 0.0)
    vec[...] = jnp.concatenate([nn(rows8, place), inner], 0).astype(bf)
    for v in vcp:
        v.start()
    vecb[f] = vec[...]
    docs = lens.shape[1]
    ln8 = jnp.broadcast_to(lens[...].astype(f32), (8, docs))
    la = lax.broadcasted_iota(jnp.int32, (docs, 128), 0)
    lb = lax.broadcasted_iota(jnp.int32, (docs, 128), 1)
    upto = jnp.where(jnp.logical_and(la <= lb, lb < docs), 1.0, 0.0)
    below = jnp.where(jnp.logical_and(la < lb, lb < docs), 1.0, 0.0)
    hi = lax.Precision.HIGHEST
    ends = jnp.dot(ln8, upto, preferred_element_type=f32, precision=hi)
    starts = jnp.dot(ln8, below, preferred_element_type=f32, precision=hi)
    first_row = lax.broadcasted_iota(jnp.int32, (8, 128), 0) == 0
    se[...] = jnp.where(first_row, starts, ends).astype(jnp.int32)

    @pl.when(jnp.logical_not(has_src))
    def _():
        xe[pl.ds(pl.multiple_of(dslot, R), R), :] = jnp.zeros((R, D), bf)

    tfw = [
        remote(
            xe.at[pl.ds(pl.multiple_of(pslot + i * pr, pr), pr)],
            xe.at[pl.ds(pl.multiple_of(dslot + i * pr, pr), pr)],
            ts.at[1, i],
            tr.at[1, i],
            (fwd, f),
        )
        for i in range(TOKP)
    ]

    def y(k):
        wcp[k][1].wait_recv()
        if wcp[k][2] is not None:
            wcp[k][2].start()
        wcp[k][3].start()
        if k + YWIN < NPC:
            wcp[k + YWIN][1].start()

    def x(k):
        wcp[k][2].wait_recv()
        wcp[k][4].start()

    def t(i):
        tcp[i].wait_recv()
        if i + 2 < TOKP:
            tcp[i + 2].start()

        @pl.when(has_fwd)
        def _():
            tfw[i].start()

    def ready(ks, parts=(0, 3, 4)):
        for k in ks:
            for i in parts:
                if wcp[k][i] is not None:
                    wcp[k][i].wait_recv()

    t(0)
    y(0)
    t(1)
    t(2)
    x(0)
    for cp in locs[4:]:
        cp.start()
    for k in range(3, NPC):
        wcp[k][0].start()
    t(3)
    y(1)
    for i in range(4, TOKP - 1):
        t(i)
    y(2)
    t(TOKP - 1)
    for cp in locs[:4]:
        cp.wait()
    for v in vcp:
        v.wait_recv()
    ready(range(3))
    anchor = c * R
    V = vecs_of(vecb)
    vrow[...] = V

    def row(i):
        return V[i : i + 1, :]

    def out(i, ref):
        cp = pltpu.make_async_copy(ref, outs[i], osem.at[i])
        cp.start()
        sent.append(cp)

    sent = []
    for i, w in enumerate((wq, wk, wv)):
        out(i, w)

    def proj(r):
        def body(i, _):
            rr = pl.ds(pl.multiple_of(r + i * 256, 256), 256)
            xb = xe[rr, :]
            k_o[rr, :] = nn(xb, wk[...]).astype(bf)
            v_o[rr, :] = (nn(xb, wv[...]) + row(1)).astype(bf)
            return 0

        lax.fori_loop(0, R // 256, body, 0)

    def projq(i, _):
        rr = pl.ds(pl.multiple_of(R + i * 256, 256), 256)
        q_o[pl.ds(pl.multiple_of(i * 256, 256), 256), :] = (nn(xe[rr, :], wq[...]) + row(0)).astype(bf)
        return 0

    def seg(i, _):
        rr = pl.ds(pl.multiple_of(i * 256, 256), 256)
        nseg[rr, :] = jnp.where(member(anchor - R + i * 256, 256, se), 0.0, 1.0).astype(bf)
        return 0

    lax.fori_loop(0, 3 * R // 256, seg, 0)
    lax.fori_loop(0, R // 256, projq, 0)
    proj(R)
    y(3)
    proj(pslot)
    y(4)
    x(3)
    for i in range(TOKP):

        @pl.when(has_src)
        def _():
            tfw[i].wait_recv()

    proj(dslot)
    out(18, se)
    out(3, xe)
    out(4, q_o)
    out(5, k_o)
    out(6, v_o)
    lane = lax.broadcasted_iota(jnp.int32, (BQ, 128), 1)
    nqb = R // BQ

    def att(i, _):
        qb = lax.div(i, 6)
        hp = lax.rem(i, 6)
        qr = pl.ds(pl.multiple_of(qb * BQ, BQ), BQ)
        wr_ = pl.ds(pl.multiple_of(qb * BQ, BQ), WIN)
        hc = pl.ds(pl.multiple_of(hp * 128, 128), 128)
        oh = jnp.where(nseg[pl.ds(pl.multiple_of(R + qb * BQ, BQ), BQ), :] == 0, -BIG, 0.0).astype(bf)
        qp = q_o[qr, hc]
        kk = jnp.concatenate([k_o[wr_, hc], nseg[wr_, :]], 1)
        vv = v_o[wr_, hc]
        res = []
        for h in range(2):
            sel = (lane < 64) if h == 0 else (lane >= 64)
            qa = jnp.concatenate([jnp.where(sel, qp, jnp.zeros_like(qp)), oh], 1)
            pe = jnp.exp2(nt(qa, kk) * C2)
            res.append((nn(pe.astype(bf), vv), jnp.sum(pe, 1, keepdims=True)))
        o = jnp.where(lane < 64, res[0][0], res[1][0])
        tot = jnp.where(lane < 64, res[0][1], res[1][1])
        ctx[qr, hc] = (o / tot).astype(bf)
        rt[qr, hc] = tot
        return 0

    pumps = ((y, 5), (x, 4)), ((y, 6), (x, 5)), ((y, 7), (x, 6)), ((y, 8), (x, 7))
    per = 6 * nqb // len(pumps)
    for gidx, steps in enumerate(pumps):
        lax.fori_loop(gidx * per, gidx * per + per, att, 0)
        for step, k in steps:
            step(k)
    out(7, ctx)

    B = 256
    NB = R // B

    def rows(i, j=0):
        return pl.ds(pl.multiple_of(j * R + i * B, B), B)

    ready((3,))
    locs[4].wait()
    gv[...] = jnp.zeros_like(gv)

    def p1(i, _):
        r = rows(i)
        h = xe[pl.ds(pl.multiple_of(R + i * B, B), B), :].astype(f32) + nn(ctx[r, :], wo[...]) + row(2)
        xh, rr = norm(h)
        xh1[r, :] = xh
        r1s[r, :] = jnp.broadcast_to(rr, (B, 128))
        nrm[r, :] = (xh * row(4) + row(5)).astype(bf)
        return 0

    lax.fori_loop(0, NB, p1, 0)
    out(8, nrm)
    for cp in locs[5:]:
        cp.wait()
    ready((4, 5))
    ready(range(6, NPC), (0,))

    acc[...] = jnp.zeros_like(acc)
    low_bit = bit(f, 1)
    high_bit = bit(f, 2)

    def p2(u, _):
        jj = lax.div(u, NB)
        i = lax.rem(u, NB)
        even_jj = 1 - lax.rem(jj, 2)
        j = jnp.where(even_jj == 1, low_bit, 1 - low_bit) + 2 * jnp.where(jj < 2, high_bit, 1 - high_bit)
        cs = pl.ds(pl.multiple_of(768 * j, 128), 768)
        r = rows(i)
        rj = rows(i, j)
        pre = nn(nrm[r, :], wi[:, cs]) + vrow[pl.ds(8 + j, 1), :]
        cdf = 0.5 + 0.5 * lax.erf(pre * RSQ2)
        pdf = jnp.exp(pre * pre * -0.5) * RS2PI
        a = (pre * cdf).astype(bf)
        act[rj, :] = a
        dg[rj, :] = (cdf + pre * pdf).astype(bf)
        acc[r, :] += nn(a, wu[pl.ds(pl.multiple_of(768 * j, 16), 768), :])
        return 0

    lax.fori_loop(0, 2 * NB, p2, 0)
    y(9)
    x(8)
    y(10)
    x(9)
    y(11)
    x(10)
    x(11)
    ready(range(6, NPC), (3, 4))
    lax.fori_loop(2 * NB, 4 * NB, p2, 0)
    out(9, act)

    def p3(i, _):
        r = rows(i)
        h = nrm[r, :].astype(f32) + acc[r, :] + row(3)
        xh, rr = norm(h)
        lo[r, :] = (xh * row(6) + row(7)).astype(bf)
        g = cot[r, :].astype(f32)
        gv[6:7, :] += jnp.sum(g * xh, 0, keepdims=True)
        gv[7:8, :] += jnp.sum(g, 0, keepdims=True)
        e = g * row(6)
        d = rr * (e - jnp.mean(e, 1, keepdims=True) - xh * jnp.mean(e * xh, 1, keepdims=True))
        g2[r, :] = d
        db = d.astype(bf)
        od[r, :] = db
        gv[3:4, :] += jnp.sum(db.astype(f32), 0, keepdims=True)
        return 0

    lax.fori_loop(0, NB, p3, 0)
    out(10, lo)
    out(11, od)

    def p4(u, _):
        j = lax.div(u, NB)
        i = lax.rem(u, NB)
        r = rows(i)
        rj = rows(i, j)
        d = (nt(od[r, :], wu[pl.ds(pl.multiple_of(768 * j, 16), 768), :]) * dg[rj, :].astype(f32)).astype(bf)
        dg[rj, :] = d
        gv[pl.ds(8 + j, 1), :] += jnp.sum(d.astype(f32), 0, keepdims=True)
        g2[r, :] += nt(d, wi[:, pl.ds(pl.multiple_of(768 * j, 128), 768)])
        return 0

    lax.fori_loop(0, 4 * NB, p4, 0)
    out(12, dg)
    heads = lax.broadcasted_iota(jnp.int32, (16, D), 0)
    onehot = jnp.where(lax.div(lax.broadcasted_iota(jnp.int32, (16, D), 1), 64) == heads, 1.0, 0.0)
    for i in range(NB):
        r = slice(i * B, i * B + B)
        g = g2[r, :]
        xh = xh1[r, :]
        rr = r1s[r, 0:1]
        gv[4:5, :] += jnp.sum(g * xh, 0, keepdims=True)
        gv[5:6, :] += jnp.sum(g, 0, keepdims=True)
        e = g * row(4)
        d = rr * (e - jnp.mean(e, 1, keepdims=True) - xh * jnp.mean(e * xh, 1, keepdims=True))
        g2[r, :] = d
        db = d.astype(bf)
        ad[r, :] = db
        gv[2:3, :] += jnp.sum(db.astype(f32), 0, keepdims=True)
        cd = nt(db, wo[...]).astype(bf).astype(f32)
        sc = cd * (1.0 / rt[r, :])
        sd[r, :] = sc.astype(bf)
        ct[:, r] = lax.dot_general(
            onehot,
            sc * ctx[r, :].astype(f32),
            (((1,), (1,)), ((), ())),
            preferred_element_type=f32,
            precision=lax.Precision.HIGHEST,
        )
    for i, ref in ((13, ad), (14, sd), (15, ct), (16, gv), (17, g2)):
        out(i, ref)
    for i in range(TOKP):

        @pl.when(has_fwd)
        def _():
            tfw[i].wait_send()

        tcp[i].wait_send()
    for cps in wcp:
        for cp in cps:
            if cp is not None:
                cp.wait_send()
    for v in vcp:
        v.wait_send()
    for cp in sent:
        cp.wait()


def front(n, tok, shards, vecs, cot, lens):
    R = tok.shape[0]
    S = jax.ShapeDtypeStruct
    ANY = pl.BlockSpec(memory_space=pl.ANY)
    F = shards[4].shape[1]
    NPC = len(PIECES)
    row = (R, D)
    W = (D, D)
    outs = [S(W, bf)] * 3 + [S((3 * R, D), bf), S(row, bf), S((3 * R, D), bf), S((3 * R, D), bf)]
    outs += [S(row, bf), S(row, bf), S((4 * R, D), bf), S(row, bf), S(row, bf), S((4 * R, D), bf)]
    outs += [S(row, bf), S(row, bf), S((16, R), f32), S((16, D), f32), S(row, f32), S((8, 128), jnp.int32)]
    scratch = [VM((3 * R, D), bf)] + [VM(W, bf)] * 4 + [VM((D, F), bf), VM((F, D), bf), VM((4, 16, D), bf)]
    scratch += [VM(row, bf), VM((3 * R, D), bf), VM((3 * R, D), bf), VM(row, bf), VM(row, f32), VM((3 * R, 128), bf)]
    scratch += [VM((4 * R, D), bf), VM((4 * R, D), bf)] + [VM(row, bf)] * 4
    scratch += [VM((16, R), f32), VM((16, D), f32), VM(row, f32), VM(row, f32), VM(row, f32), VM((R, 128), f32)]
    scratch += [VM(row, bf), VM(row, bf), VM((8, 128), jnp.int32), VM((16, D), bf), VM((16, D), f32)]
    scratch += [DMA((2, TOKP)), DMA((2, TOKP)), DMA((NPC, 5)), DMA((NPC, 5)), DMA((3,)), DMA((3,)), DMA((8,)), DMA((19,))]
    return pl.pallas_call(
        functools.partial(front_kernel, n),
        out_shape=outs,
        in_specs=[ANY] * 7 + [FULL] * 9 + [ANY, FULL],
        out_specs=[ANY] * 19,
        scratch_shapes=scratch,
        compiler_params=pltpu.CompilerParams(collective_id=1, has_side_effects=True, vmem_limit_bytes=VLIM),
        name="front",
    )(tok, *shards, *vecs, cot, lens)


NP = 12
NH = 2 * NP
WINDOW = 3
LATE = NH
LAG = 2
TURN = 3
HCH = 16
HLAG = 3


def extra_bits(n):
    return [1 << j for j in range(3, 16) if (1 << j) < n]


def add_rows(dst, a, b, rows, step=48):
    def body(i, _):
        r = pl.ds(pl.multiple_of(i * step, 16), step)
        dst[r, :] = a[r, :] + b[r, :]
        return 0

    lax.fori_loop(0, rows // step, body, 0)


def back_kernel(n, *refs):
    hbm = refs[:14]
    gvin, ct, se = refs[14:17]
    OUT, vout, hin, gx_o = refs[17:21]
    bufs = refs[21:32]
    A, od, nrm, I, ctx, ad, q, k_, v_, sd, xe = bufs
    wq = k_.at[pl.ds(0, D)]
    wk = v_.at[pl.ds(0, D)]
    wv = v_.at[pl.ds(D, D)]
    bufs = bufs + (wq, wk, wv)
    G, RC, RY, RX, RZ, RW, RE, VR, vacc, HR, nseg, dk, dv = refs[32:45]
    ld, cs, cr, ss, sr, vs, vr, hs, hrs = refs[45:]
    dqb = q
    R = q.shape[0]
    extra = extra_bits(n)
    c = lax.axis_index("ctx")
    f = lax.axis_index("fsdp")
    cb = bit(f, 1)
    yb = bit(f, 2)
    sib = (c, flip(f, 1))
    yp = (c, flip(f, 2))
    p = [(flip(c, 1 << j), f) for j in range(3)]
    peers = [sib, yp] + p + [(flip(c, b), f) for b in extra]
    odd = bit(c, 1) == 1
    fwd = jnp.where(odd, c + 2, c - 2)
    src = jnp.where(odd, c - 2, c + 2)
    has_fwd = jnp.logical_and(fwd >= 0, fwd < n)
    has_src = jnp.logical_and(src >= 0, src < n)
    oth = jnp.where(bit(c, 2) == 0, c - 2, c + 2)
    has_oth = jnp.logical_and(oth >= 0, oth < n)
    loads = [pltpu.make_async_copy(hbm[i], bufs[i], ld.at[i]) for i in range(14)]
    for cp in loads[:10]:
        cp.start()
    greet(peers, ((has_oth, (oth, f)),))
    loads[10].start()

    bit0 = bit(c, 1)
    bit1 = bit(c, 2)

    def turned(m):
        return (m % TURN == TURN - 1) if isinstance(m, int) else (lax.rem(m, TURN) == TURN - 1)

    def pick(m, one, two):
        t = turned(m)
        if isinstance(t, bool):
            return two if t else one
        return jnp.where(t, two, one)

    def core(k, yy):
        return remote(G.at[k, 2 * yy + (1 - cb)], RC.at[k, yy], cs.at[k, yy], cr.at[k, yy], sib)

    def place(m):
        return (m // 2, m % 2) if isinstance(m, int) else (lax.div(m, 2), lax.rem(m, 2))

    def quarter(m, q):
        k, h = place(m)
        return G.at[k, q, h]

    def part(ref, m, r=None):
        k, h = place(m)
        return ref.at[k, h] if r is None else ref.at[k, h, r]

    def put(k, g):
        for h in range(2):
            G[k, :, h] = g[:, 384 * h : 384 * h + 384].astype(bf).reshape(4, 192, 384)

    def first(m):
        return pl.multiple_of(pick(m, bit0, bit1) * 96, 16)

    def second(m):
        return first(m) + pl.multiple_of(pick(m, bit1, bit0) * 48, 16)

    def rows_of(ref, m, r, size):
        return ref.at[pl.ds(pl.multiple_of(r, 16), size)]

    def acc(m):
        return quarter(m, 2 * yb + cb)

    def spare(m, i):
        return part(RY, m, pl.ds(48 * (i % 4), 48))

    def copy(m, i):
        s = (ss.at[m, i], sr.at[m, i])
        pa = (pick(m, flip(c, 1), flip(c, 2)), f)
        pb = (pick(m, flip(c, 2), flip(c, 1)), f)
        if i == 0:
            return remote(quarter(m, 2 * (1 - yb) + cb), part(RY, m), *s, yp)
        if i == 1:
            return remote(rows_of(acc(m), m, 96 - first(m), 96), part(RX, m), *s, pa)
        if i == 2:
            r = first(m) + 48 - pick(m, bit1, bit0) * 48
            return remote(rows_of(acc(m), m, r, 48), part(RZ, m), *s, pb)
        if i == 3:
            return remote(rows_of(acc(m), m, second(m), 48), part(RW, m), *s, p[2])
        if i == 4:
            o = part(OUT, m, pl.ds(pl.multiple_of(second(m), 16), 48))
            return remote(o, o, *s, pb)
        if i == 5:
            o = part(OUT, m, pl.ds(first(m), 96))
            return remote(o, o, *s, pa)
        e = extra[i - 6]
        return remote(spare(m, i - 6), part(RE.at[i - 6], m), *s, (flip(c, e), f))

    def give(k):
        for yy in range(2):
            core(k, yy).start()

    def s1(k):
        for yy in range(2):
            core(k, yy).wait_recv()
        for yy in range(2):
            for h in range(2):
                g = G.at[k, 2 * yy + cb, h]
                add_rows(g, g, RC.at[k, yy, h], 192)

    def s2(m):
        copy(m, 0).wait_recv()
        if isinstance(m, int):
            if m + WINDOW < LATE:
                copy(m + WINDOW, 0).start()
        else:

            @pl.when(m + WINDOW < LATE)
            def _():
                copy(m + WINDOW, 0).start()

        add_rows(acc(m), acc(m), part(RY, m), 192)
        copy(m, 1).start()

    def s3(m):
        copy(m, 1).wait_recv()
        a = rows_of(acc(m), m, first(m), 96)
        add_rows(a, a, part(RX, m), 96)
        copy(m, 2).start()

    def s4(m):
        copy(m, 2).wait_recv()
        a = rows_of(acc(m), m, second(m), 48)
        add_rows(a, a, part(RZ, m), 48)
        copy(m, 3).start()

    def s5(m):
        copy(m, 3).wait_recv()
        last = rows_of(acc(m), m, second(m), 48)
        got = part(RW, m)
        for i in range(len(extra)):
            add_rows(spare(m, i), last, got, 48)
            copy(m, 6 + i).start()
            copy(m, 6 + i).wait_recv()
            last = spare(m, i)
            got = part(RE.at[i], m)
        add_rows(part(OUT, m, pl.ds(pl.multiple_of(second(m), 16), 48)), last, got, 48)
        copy(m, 4).start()

    def s6(m):
        copy(m, 4).wait_recv()
        copy(m, 5).start()

    def s7(m):
        copy(m, 5).wait_recv()

    stages = (s2, s3, s4, s5, s6, s7)

    def tick(t):
        for i in reversed(range(len(stages))):
            m = t - LAG * i
            if isinstance(t, int):
                if 0 <= m < NH:
                    stages[i](m)
            else:

                @pl.when(jnp.logical_and(m >= 0, m < NH))
                def _():
                    stages[i](m)

    def both(t):
        for i in reversed(range(len(stages))):
            for m in (t - LAG * i, t + 1 - LAG * i):
                if 0 <= m < NH:
                    stages[i](m)

    def outer(hh, qq):
        g = tn(A[pl.ds(pl.multiple_of(qq * R, R), R), 384 * hh : 384 * hh + 384], od[...]).astype(bf)
        for h in range(2):
            G[2 * hh, qq, h] = g[:192, 384 * h : 384 * h + 384]
            G[2 * hh + 1, qq, h] = g[192:, 384 * h : 384 * h + 384]

    loads[0].wait()
    loads[1].wait()
    for hh in range(2):
        for yy in range(2):
            outer(hh, 2 * yy + (1 - cb))
        give(2 * hh)
        give(2 * hh + 1)
        for yy in range(2):
            outer(hh, 2 * yy + cb)
    for k in range(2):
        s1(k)
        for m in (2 * k, 2 * k + 1):
            if m < WINDOW:
                copy(m, 0).start()
    loads[2].wait()
    loads[3].wait()
    for j in range(4):
        put(4 + j, tn(nrm[...], I[R * j : R * j + R, :]))
        give(4 + j)
        if j < 2:
            s1(2 + j)
        if j == 2:
            tick(0)
    s1(4)
    tick(1)
    loads[4].wait()
    loads[5].wait()
    put(8, tn(ctx[...], ad[...]))
    give(8)
    for k in (5, 6, 7):
        s1(k)
    tick(2)
    s1(8)

    anchor = c * R

    def prep(i, _):
        r = pl.ds(pl.multiple_of(i * 256, 256), 256)
        nseg[r, :] = jnp.where(member(anchor - R + i * 256, 256, se), 0.0, 1.0).astype(bf)
        dk[r, :] = jnp.zeros((256, 128), f32)
        dv[r, :] = jnp.zeros((256, 128), f32)
        return 0

    lax.fori_loop(0, 3 * R // 256, prep, 0)
    lane = lax.broadcasted_iota(jnp.int32, (BQ, 128), 1)
    nqb = R // BQ
    for i in range(6, 10):
        loads[i].wait()

    def head(i, _):
        hp = lax.div(i, nqb)
        qb = lax.rem(i, nqb)
        hc = pl.ds(pl.multiple_of(hp * 128, 128), 128)
        qr = pl.ds(pl.multiple_of(qb * BQ, BQ), BQ)
        wr = pl.ds(pl.multiple_of(qb * BQ, BQ), WIN)
        oh = jnp.where(nseg[pl.ds(pl.multiple_of(R + qb * BQ, BQ), BQ), :] == 0, -BIG, 0.0).astype(bf)
        qp = q[qr, hc]
        sp = sd[qr, hc]
        kp = k_[wr, hc]
        vp = v_[wr, hc]
        kk = jnp.concatenate([kp, nseg[wr, :]], 1)
        z = jnp.zeros_like(qp)
        dkp = []
        dvp = []
        dqs = []
        for h in range(2):
            sel = (lane < 64) if h == 0 else (lane >= 64)
            qm = jnp.where(sel, qp, z)
            sm = jnp.where(sel, sp, z)
            pr = jnp.exp2(nt(kk, jnp.concatenate([qm, oh], 1)) * C2)
            dp = nt(vp, sm)
            ds = (pr * (dp - ct[pl.ds(2 * hp + h, 1), qr])).astype(bf)
            dvp.append(nn(pr.astype(bf), sm))
            dkp.append(nn(ds, qm))
            dqs.append(tn(ds, kp))
        dk[wr, :] += dkp[0] + dkp[1]
        dv[wr, :] += dvp[0] + dvp[1]
        dqb[qr, hc] = (jnp.where(lane < 64, dqs[0], dqs[1]) * 0.125).astype(bf)

        @pl.when(qb == nqb - 1)
        def _():
            def fin(j, _):
                r = pl.ds(pl.multiple_of(j * 256, 256), 256)
                A[r, hc] = (dk[r, :] * 0.125).astype(bf)
                I[r, hc] = dv[r, :].astype(bf)
                dk[r, :] = jnp.zeros((256, 128), f32)
                dv[r, :] = jnp.zeros((256, 128), f32)
                return 0

            lax.fori_loop(0, 3 * R // 256, fin, 0)

        tick(i + 3)

        return 0

    lax.fori_loop(0, 6 * nqb, head, 0)
    t = 6 * nqb + 3

    W3 = 3 * R
    own = slice(R, 2 * R)
    for cp in loads[11:]:
        cp.start()
    loads[10].wait()
    vacc[0] = gvin[...]
    vacc[0, 0:1, :] = jnp.sum(dqb[...].astype(f32), 0, keepdims=True)
    vacc[0, 1:2, :] = jnp.sum(I[0:W3, :].astype(f32), 0, keepdims=True)
    for cp in loads[11:]:
        cp.wait()
    for dst, r in ((od, slice(0, R)), (nrm, slice(2 * R, W3))):
        dst[...] = (nt(A[r, :], wk[...]) + nt(I[r, :], wv[...])).astype(bf)

    @pl.when(odd)
    def _():
        ad[...] = od[...]

    @pl.when(jnp.logical_not(odd))
    def _():
        ad[...] = nrm[...]

    hn = R // HCH

    def leg1(ref, j):
        r = pl.ds(j * hn, hn)
        return remote(ref.at[r], HR.at[r], hs.at[0, j], hrs.at[0, j], (fwd, f))

    def leg2(j):
        r = pl.ds(j * hn, hn)
        return remote(ad.at[r], hin.at[r], hs.at[1, j], hrs.at[1, j], p[0])

    def halo(j):
        if 0 <= j < HCH:

            @pl.when(jnp.logical_and(has_fwd, odd))
            def _():
                leg1(nrm, j).start()

            @pl.when(jnp.logical_and(has_fwd, jnp.logical_not(odd)))
            def _():
                leg1(od, j).start()

        j = j - HLAG
        if 0 <= j < HCH:

            @pl.when(has_src)
            def _():
                leg1(od, j).wait_recv()
                r = pl.ds(j * hn, hn)
                add_rows(ad.at[r], ad.at[r], HR.at[r], hn, 32)

            leg2(j).start()

    halo(0)
    put(9, tn(xe[...], I[0:W3, :]))
    give(9)
    halo(1)
    put(10, tn(xe[...], A[0:W3, :]))
    give(10)
    s1(9)
    tick(t)
    halo(2)
    tick(t + 1)
    put(11, tn(xe[own, :], dqb[...]))
    give(11)
    s1(10)
    tick(t + 2)
    halo(3)
    tick(t + 3)
    ctx[...] = (nt(dqb[...], wq[...]) + nt(A[own, :], wk[...]) + nt(I[own, :], wv[...])).astype(bf)
    gxc = pltpu.make_async_copy(ctx, gx_o, ld.at[14])
    gxc.start()
    s1(11)
    vround = 0
    hj = 4
    for step in range(t + 4, NH + LAG * (len(stages) - 1)):
        if step < NH:
            tick(step)
        elif (step - NH) % 2 == 0:
            both(step)
        halo(hj)
        hj += 1
        if vround <= len(peers) and step % 2 == 0:
            if vround > 0:
                exchange.wait()
                vacc[vround] = vacc[vround - 1] + VR[vround - 1]
            if vround < len(peers):
                exchange = remote(vacc.at[vround], VR.at[vround], vs.at[vround], vr.at[vround], peers[vround])
                exchange.start()
            vround += 1
    while vround <= len(peers):
        exchange.wait()
        vacc[vround] = vacc[vround - 1] + VR[vround - 1]
        if vround < len(peers):
            exchange = remote(vacc.at[vround], VR.at[vround], vs.at[vround], vr.at[vround], peers[vround])
            exchange.start()
        vround += 1
    while hj < HCH + HLAG:
        halo(hj)
        hj += 1
    vout[...] = vacc[len(peers)]
    for j in range(HCH):
        leg2(j).wait()

        @pl.when(has_fwd)
        def _():
            leg1(od, j).wait_send()

    def done(m, _):
        core(lax.div(m, 2), lax.rem(m, 2)).wait_send()
        for i in range(6 + len(extra)):
            copy(m, i).wait_send()
        return 0

    lax.fori_loop(0, NH, done, 0)
    gxc.wait()


def back(n, act, od, nrm, idel, ctx, ad, q, k, v, sd, xe, wq, wk, wv, gv, ct, se):
    R = q.shape[0]
    ne = len(extra_bits(n))
    nv = 5 + ne
    S = jax.ShapeDtypeStruct
    ANY = pl.BlockSpec(memory_space=pl.ANY)
    big = (act, od, nrm, idel, ctx, ad, q, k, v, sd, xe, wq, wk, wv)
    return pl.pallas_call(
        functools.partial(back_kernel, n),
        out_shape=[S((NP, 2, 192, 384), bf), S((16, D), f32), S((R, D), bf), S((R, D), bf)],
        in_specs=[ANY] * 14 + [FULL] * 3,
        out_specs=[FULL] * 3 + [ANY],
        scratch_shapes=[VM(t.shape, t.dtype) for t in big[:11]]
        + [
            VM((NP, 4, 2, 192, 384), bf),
            VM((NP, 2, 2, 192, 384), bf),
            VM((NP, 2, 192, 384), bf),
            VM((NP, 2, 96, 384), bf),
            VM((NP, 2, 48, 384), bf),
            VM((NP, 2, 48, 384), bf),
            VM((ne, NP, 2, 48, 384) if ne else (1, 1, 2, 48, 384), bf),
            VM((nv, 16, D), f32),
            VM((nv + 1, 16, D), f32),
            VM((R, D), bf),
            VM((3 * R, 128), bf),
            VM((3 * R, 128), f32),
            VM((3 * R, 128), f32),
            DMA((15,)),
            DMA((NP, 2)),
            DMA((NP, 2)),
            DMA((NH, 6 + ne)),
            DMA((NH, 6 + ne)),
            DMA((nv,)),
            DMA((nv,)),
            DMA((2, HCH)),
            DMA((2, HCH)),
        ],
        compiler_params=pltpu.CompilerParams(collective_id=2, has_side_effects=True, vmem_limit_bytes=61 * 2**20),
        name="back",
    )(*big, gv, ct, se)


def last_kernel(g, gv, g1, gx, hin, gq, gk, gw, go, gi, gu, gt, *vecs):
    for h in range(2):
        cs = slice(384 * h, 384 * h + 384)
        for ref, k in ((gw, 9), (gk, 10), (gq, 11), (go, 8)):
            ref[:, cs] = g[k, h].astype(f32)
        for j in range(4):
            gi[:, 768 * j + 384 * h : 768 * j + 384 * h + 384] = g[4 + j, h].astype(f32)
            gu[192 * j : 192 * j + 192, cs] = g[j, h].astype(f32)
    gt[...] = g1[...] + gx[...].astype(f32) + hin[...].astype(f32)
    f = lax.axis_index("fsdp")
    w = D // 4
    own = lax.broadcasted_iota(jnp.int32, (D, w), 0) == lax.broadcasted_iota(jnp.int32, (D, w), 1) + f * w
    rows = lax.dot_general(
        gv[0:8, :],
        jnp.where(own, 1.0, 0.0),
        (((1,), (0,)), ((), ())),
        preferred_element_type=f32,
        precision=lax.Precision.HIGHEST,
    )
    for j in range(8):
        vecs[j][...] = rows[j : j + 1, :].reshape(w)
    vecs[8][...] = gv[pl.ds(8 + f, 1), :].reshape(D)


def last(g, gv, g1, gx, hin):
    R = g1.shape[0]
    S = jax.ShapeDtypeStruct
    outs = [S((192, D), f32)] * 4 + [S((192, 4 * D), f32), S((4 * 192, D), f32), S((R, D), f32)]
    outs += [S((D // 4,), f32)] * 8 + [S((D,), f32)]
    return pl.pallas_call(
        last_kernel,
        out_shape=outs,
        in_specs=[FULL] * 5,
        out_specs=[FULL] * 16,
        compiler_params=pltpu.CompilerParams(vmem_limit_bytes=VLIM),
        name="last",
    )(g, gv, g1, gx, hin)


def local(n, tokens, doc_lengths, cotangent, wq, wk, wv, wo, wi, wu, bq, bv, bo, bi, bu, ga, sa, gf, sf):
    x = tokens[0]
    docs = doc_lengths.shape[1]
    assert docs <= 128 and x.shape[0] == 512
    vecs = (bq, bv, bo, bu, ga, sa, gf, sf, bi)
    wq, wk, wv, xe, q, k, v, ctx, nrm, act, layer_out, od, idel, ad, sd, ct, gv, g1, se = front(
        n, x, (wq, wk, wv, wo, wi, wu), vecs, cotangent[0], doc_lengths
    )
    g, gv, hin, gx = back(n, act, od, nrm, idel, ctx, ad, q, k, v, sd, xe, wq, wk, wv, gv, ct, se)
    gq, gk, gw, go, gi, gu, gt, *gs, gbi = last(g, gv, g1, gx, hin)
    return (layer_out[None], gt[None], gq, gk, gw, go, gi, gu, gs[0], gs[1], gs[2], gbi, *gs[3:])


def solution(mesh):
    n = mesh.shape["ctx"]
    tok = P("fsdp", "ctx", None)
    mat = P("fsdp", None)
    vec = P("fsdp")
    return jax.shard_map(
        functools.partial(local, n),
        mesh=mesh,
        in_specs=(tok, mat, tok) + (mat,) * 6 + (vec,) * 9,
        out_specs=(tok, tok) + (mat,) * 6 + (vec,) * 9,
        check_vma=False,
    )
```

```python
import functools

import jax
import jax.numpy as jnp
from jax import lax
from jax.experimental import pallas as pl
from jax.experimental.pallas import tpu as pltpu
from jax.sharding import PartitionSpec as P

bf = jnp.bfloat16
f32 = jnp.float32
MESH = pl.DeviceIdType.MESH
VM = pltpu.VMEM
DMA = pltpu.SemaphoreType.DMA
D = 768
EPS = 1e-12
BIG = 1e30
C2 = 0.125 * 1.4426950408889634
RSQ2 = 0.7071067811865476
RS2PI = 0.3989422804014327
BQ = 256
WIN = BQ + 1024
TOKP = 8
HS = 192
VLIM = 58 * 2**20
FULL = pl.BlockSpec(memory_space=pltpu.VMEM)


def nt(a, b):
    return lax.dot_general(a, b, (((1,), (1,)), ((), ())), preferred_element_type=f32)


def nn(a, b):
    return lax.dot_general(a, b, (((1,), (0,)), ((), ())), preferred_element_type=f32)


def tn(a, b):
    return lax.dot_general(a, b, (((0,), (0,)), ((), ())), preferred_element_type=f32)


def bit(i, b):
    return lax.rem(lax.div(i, b), 2)


def flip(i, b):
    return i + b * (1 - 2 * bit(i, b))


def remote(src, dst, send, recv, device):
    return pltpu.make_async_remote_copy(
        src_ref=src, dst_ref=dst, send_sem=send, recv_sem=recv, device_id=device, device_id_type=MESH
    )


def greet(peers, others):
    bar = pltpu.get_barrier_semaphore()
    for d in peers:
        pl.semaphore_signal(bar, inc=1, device_id=d, device_id_type=MESH)
    for cond, d in others:

        @pl.when(cond)
        def _():
            pl.semaphore_signal(bar, inc=1, device_id=d, device_id_type=MESH)

    pl.semaphore_wait(bar, len(peers) + sum(cond.astype(jnp.int32) for cond, _ in others))


def vecs_of(vec):
    return (vec[0].astype(f32) + vec[1].astype(f32)) + (vec[2].astype(f32) + vec[3].astype(f32))


def member(pos0, rows, se):
    pos = pos0 + lax.broadcasted_iota(jnp.int32, (rows, 128), 0)
    return jnp.logical_and(pos >= se[0:1, :], pos < se[1:2, :])


def norm(h):
    c = h - jnp.mean(h, 1, keepdims=True)
    r = lax.rsqrt(jnp.mean(c * c, 1, keepdims=True) + EPS)
    return c * r, r


PIECES = [(0, 0, 192, 0, 768, 2), (1, 0, 192, 0, 768, 0), (2, 0, 192, 0, 768, 0), (3, 0, 192, 0, 768, 1)]
PIECES += [(4, 0, 192, None, 768, 1 if j < 3 else 2) for j in range(4)]
PIECES += [(5, 192 * j, 192, 0, 768, 1 if j in (1, 3) else 2) for j in range(4)]
YWIN = 4


def front_kernel(n, *refs):
    tok, *sh = refs[:7]
    *small, inner_v, cot_h, lens = refs[7:18]
    outs = refs[18:37]
    (xe, wq, wk, wv, wo, wi, wu, vecb, q_o, k_o, v_o, ctx, rt, nseg, act, dg, od, nrm, ad, sd, ct, gv, g2, xh1, acc, r1s, cot, lo, se, vec, vrow) = refs[37:68]
    ts, tr, ws, wr, vs, vr, ls, osem = refs[68:]
    full = (wq, wk, wv, wo, wi, wu)
    c = lax.axis_index("ctx")
    f = lax.axis_index("fsdp")
    sib = (c, flip(f, 1))
    yp = (c, flip(f, 2))
    dgn = (c, flip(flip(f, 1), 2))
    c1 = (flip(c, 1), f)
    c2 = (flip(c, 2), f)
    even = bit(c, 1) == 0
    fwd = jnp.where(even, c + 2, c - 2)
    src = jnp.where(even, c - 2, c + 2)
    has_fwd = jnp.logical_and(fwd >= 0, fwd < n)
    has_src = jnp.logical_and(src >= 0, src < n)
    oth = jnp.where(bit(c, 2) == 0, c - 2, c + 2)
    has_oth = jnp.logical_and(oth >= 0, oth < n)
    R = xe.shape[0] // 3

    locs = [pltpu.make_async_copy(tok, xe.at[pl.ds(R, R)], ls.at[0])]
    for i, (s, w) in enumerate(zip(sh, full)):
        H = s.shape[0]
        locs.append(pltpu.make_async_copy(s, w.at[pl.ds(pl.multiple_of(f * H, 16), H)], ls.at[1 + i]))
    locs.append(pltpu.make_async_copy(cot_h, cot, ls.at[7]))
    greet((sib, yp, dgn, c1, c2), ((has_oth, (oth, f)),))
    pr = R // TOKP
    pslot = jnp.where(even, 2 * R, 0)
    dslot = jnp.where(even, 0, 2 * R)
    tcp = [
        remote(
            tok.at[pl.ds(i * pr, pr)],
            xe.at[pl.ds(pl.multiple_of(dslot + i * pr, pr), pr)],
            ts.at[0, i],
            tr.at[0, i],
            c1,
        )
        for i in range(TOKP)
    ]
    vcp = [remote(vec, vecb.at[f], vs.at[i], vr.at[i], (sib, yp, dgn)[i]) for i in range(3)]
    wcp = []
    fy = flip(f, 2)
    for k, (t, r0, H2, c0, C, route) in enumerate(PIECES):
        s = sh[t]
        w = full[t]
        SR = s.shape[0]
        cg = cs_ = slice(c0, c0 + C) if c0 is not None else None
        if c0 is None:
            j = k - 4
            mix = flip(flip(f, 1), 2) if j == 3 else (flip(f, j) if j else f)
            far = flip(mix, 2)
            cg = pl.ds(pl.multiple_of(mix * C, 128), C)
            cs_ = pl.ds(pl.multiple_of(far * C, 128), C)
        own = pl.multiple_of(f * SR + r0, 16)
        if route == 0:
            other = pl.multiple_of(fy * SR + r0, 16)
            wcp.append(
                [
                    remote(s.at[pl.ds(r0, H2), cg], w.at[pl.ds(own, H2), cg], ws.at[k, 0], wr.at[k, 0], sib),
                    remote(s.at[pl.ds(r0, H2), cs_], w.at[pl.ds(own, H2), cs_], ws.at[k, 1], wr.at[k, 1], yp),
                    None,
                    remote(w.at[pl.ds(other, H2), cg], w.at[pl.ds(other, H2), cg], ws.at[k, 3], wr.at[k, 3], sib),
                    None,
                ]
            )
            continue
        H = H2 // 2
        p = c1 if route == 1 else c2
        hb = bit(c, route)
        mine = pl.multiple_of(f * SR + r0 + hb * H, 16)
        gy = pl.multiple_of(fy * SR + r0 + hb * H, 16)
        gx = pl.multiple_of(fy * SR + r0 + (1 - hb) * H, 16)
        wcp.append(
            [
                remote(s.at[pl.ds(r0, H2), cg], w.at[pl.ds(own, H2), cg], ws.at[k, 0], wr.at[k, 0], sib),
                remote(
                    s.at[pl.ds(pl.multiple_of(r0 + hb * H, 16), H), cs_],
                    w.at[pl.ds(mine, H), cs_],
                    ws.at[k, 1],
                    wr.at[k, 1],
                    yp,
                ),
                remote(w.at[pl.ds(gy, H), cg], w.at[pl.ds(gy, H), cg], ws.at[k, 2], wr.at[k, 2], p),
                remote(w.at[pl.ds(gy, H), cg], w.at[pl.ds(gy, H), cg], ws.at[k, 3], wr.at[k, 3], sib),
                remote(w.at[pl.ds(gx, H), cg], w.at[pl.ds(gx, H), cg], ws.at[k, 4], wr.at[k, 4], sib),
            ]
        )
    NPC = len(PIECES)
    for k in range(YWIN):
        wcp[k][1].start()
    for t in tcp[:2]:
        t.start()
    for cp in locs[:4]:
        cp.start()
    for k in range(3):
        wcp[k][0].start()

    w8 = D // 4
    sel = lax.broadcasted_iota(jnp.int32, (w8, D), 0) + f * w8 == lax.broadcasted_iota(jnp.int32, (w8, D), 1)
    place = jnp.where(sel, 1.0, 0.0).astype(bf)
    r8 = lax.broadcasted_iota(jnp.int32, (8, w8), 0)
    rows8 = jnp.zeros((8, w8), f32)
    for j, ref in enumerate(small):
        rows8 = jnp.where(r8 == j, jnp.broadcast_to(ref[...].astype(f32).reshape(1, w8), (8, w8)), rows8)
    rows8 = rows8.astype(bf)
    isf = lax.broadcasted_iota(jnp.int32, (8, D), 0) == f
    inner = jnp.where(isf, jnp.broadcast_to(inner_v[...].astype(f32).reshape(1, D), (8, D)), 0.0)
    vec[...] = jnp.concatenate([nn(rows8, place), inner], 0).astype(bf)
    for v in vcp:
        v.start()
    vecb[f] = vec[...]
    docs = lens.shape[1]
    ln8 = jnp.broadcast_to(lens[...].astype(f32), (8, docs))
    la = lax.broadcasted_iota(jnp.int32, (docs, 128), 0)
    lb = lax.broadcasted_iota(jnp.int32, (docs, 128), 1)
    upto = jnp.where(jnp.logical_and(la <= lb, lb < docs), 1.0, 0.0)
    below = jnp.where(jnp.logical_and(la < lb, lb < docs), 1.0, 0.0)
    hi = lax.Precision.HIGHEST
    ends = jnp.dot(ln8, upto, preferred_element_type=f32, precision=hi)
    starts = jnp.dot(ln8, below, preferred_element_type=f32, precision=hi)
    first_row = lax.broadcasted_iota(jnp.int32, (8, 128), 0) == 0
    se[...] = jnp.where(first_row, starts, ends).astype(jnp.int32)

    @pl.when(jnp.logical_not(has_src))
    def _():
        xe[pl.ds(pl.multiple_of(dslot, R), R), :] = jnp.zeros((R, D), bf)

    tfw = [
        remote(
            xe.at[pl.ds(pl.multiple_of(pslot + i * pr, pr), pr)],
            xe.at[pl.ds(pl.multiple_of(dslot + i * pr, pr), pr)],
            ts.at[1, i],
            tr.at[1, i],
            (fwd, f),
        )
        for i in range(TOKP)
    ]

    def y(k):
        wcp[k][1].wait_recv()
        if wcp[k][2] is not None:
            wcp[k][2].start()
        wcp[k][3].start()
        if k + YWIN < NPC:
            wcp[k + YWIN][1].start()

    def x(k):
        wcp[k][2].wait_recv()
        wcp[k][4].start()

    def t(i):
        tcp[i].wait_recv()
        if i + 2 < TOKP:
            tcp[i + 2].start()

        @pl.when(has_fwd)
        def _():
            tfw[i].start()

    def ready(ks, parts=(0, 3, 4)):
        for k in ks:
            for i in parts:
                if wcp[k][i] is not None:
                    wcp[k][i].wait_recv()

    t(0)
    y(0)
    t(1)
    t(2)
    x(0)
    for cp in locs[4:]:
        cp.start()
    for k in range(3, NPC):
        wcp[k][0].start()
    t(3)
    y(1)
    for i in range(4, TOKP - 1):
        t(i)
    y(2)
    t(TOKP - 1)
    for cp in locs[:4]:
        cp.wait()
    for v in vcp:
        v.wait_recv()
    ready(range(3))
    anchor = c * R
    V = vecs_of(vecb)
    vrow[...] = V

    def row(i):
        return V[i : i + 1, :]

    def out(i, ref):
        cp = pltpu.make_async_copy(ref, outs[i], osem.at[i])
        cp.start()
        sent.append(cp)

    sent = []
    for i, w in enumerate((wq, wk, wv)):
        out(i, w)

    def proj(r):
        def body(i, _):
            rr = pl.ds(pl.multiple_of(r + i * 256, 256), 256)
            xb = xe[rr, :]
            k_o[rr, :] = nn(xb, wk[...]).astype(bf)
            v_o[rr, :] = (nn(xb, wv[...]) + row(1)).astype(bf)
            return 0

        lax.fori_loop(0, R // 256, body, 0)

    def projq(i, _):
        rr = pl.ds(pl.multiple_of(R + i * 256, 256), 256)
        q_o[pl.ds(pl.multiple_of(i * 256, 256), 256), :] = (nn(xe[rr, :], wq[...]) + row(0)).astype(bf)
        return 0

    def seg(i, _):
        rr = pl.ds(pl.multiple_of(i * 256, 256), 256)
        nseg[rr, :] = jnp.where(member(anchor - R + i * 256, 256, se), 0.0, 1.0).astype(bf)
        return 0

    lax.fori_loop(0, 3 * R // 256, seg, 0)
    lax.fori_loop(0, R // 256, projq, 0)
    proj(R)
    y(3)
    proj(pslot)
    y(4)
    x(3)
    for i in range(TOKP):

        @pl.when(has_src)
        def _():
            tfw[i].wait_recv()

    proj(dslot)
    out(18, se)
    out(3, xe)
    out(4, q_o)
    out(5, k_o)
    out(6, v_o)
    lane = lax.broadcasted_iota(jnp.int32, (BQ, 128), 1)
    nqb = R // BQ

    def att(i, _):
        qb = lax.div(i, 6)
        hp = lax.rem(i, 6)
        qr = pl.ds(pl.multiple_of(qb * BQ, BQ), BQ)
        wr_ = pl.ds(pl.multiple_of(qb * BQ, BQ), WIN)
        hc = pl.ds(pl.multiple_of(hp * 128, 128), 128)
        oh = jnp.where(nseg[pl.ds(pl.multiple_of(R + qb * BQ, BQ), BQ), :] == 0, -BIG, 0.0).astype(bf)
        qp = q_o[qr, hc]
        kk = jnp.concatenate([k_o[wr_, hc], nseg[wr_, :]], 1)
        vv = v_o[wr_, hc]
        res = []
        for h in range(2):
            sel = (lane < 64) if h == 0 else (lane >= 64)
            qa = jnp.concatenate([jnp.where(sel, qp, jnp.zeros_like(qp)), oh], 1)
            pe = jnp.exp2(nt(qa, kk) * C2)
            res.append((nn(pe.astype(bf), vv), jnp.sum(pe, 1, keepdims=True)))
        o = jnp.where(lane < 64, res[0][0], res[1][0])
        tot = jnp.where(lane < 64, res[0][1], res[1][1])
        ctx[qr, hc] = (o / tot).astype(bf)
        rt[qr, hc] = tot
        return 0

    pumps = ((y, 5), (x, 4)), ((y, 6), (x, 5)), ((y, 7), (x, 6)), ((y, 8), (x, 7))
    per = 6 * nqb // len(pumps)
    for gidx, steps in enumerate(pumps):
        lax.fori_loop(gidx * per, gidx * per + per, att, 0)
        for step, k in steps:
            step(k)
    out(7, ctx)

    B = 256
    NB = R // B

    def rows(i, j=0):
        return pl.ds(pl.multiple_of(j * R + i * B, B), B)

    ready((3,))
    locs[4].wait()
    gv[...] = jnp.zeros_like(gv)

    def p1(i, _):
        r = rows(i)
        h = xe[pl.ds(pl.multiple_of(R + i * B, B), B), :].astype(f32) + nn(ctx[r, :], wo[...]) + row(2)
        xh, rr = norm(h)
        xh1[r, :] = xh
        r1s[r, :] = jnp.broadcast_to(rr, (B, 128))
        nrm[r, :] = (xh * row(4) + row(5)).astype(bf)
        return 0

    lax.fori_loop(0, NB, p1, 0)
    out(8, nrm)
    for cp in locs[5:]:
        cp.wait()
    ready((4, 5))
    ready(range(6, NPC), (0,))

    acc[...] = jnp.zeros_like(acc)
    low_bit = bit(f, 1)
    high_bit = bit(f, 2)

    def p2(u, _):
        jj = lax.div(u, NB)
        i = lax.rem(u, NB)
        even_jj = 1 - lax.rem(jj, 2)
        j = jnp.where(even_jj == 1, low_bit, 1 - low_bit) + 2 * jnp.where(jj < 2, high_bit, 1 - high_bit)
        cs = pl.ds(pl.multiple_of(768 * j, 128), 768)
        r = rows(i)
        rj = rows(i, j)
        pre = nn(nrm[r, :], wi[:, cs]) + vrow[pl.ds(8 + j, 1), :]
        cdf = 0.5 + 0.5 * lax.erf(pre * RSQ2)
        pdf = jnp.exp(pre * pre * -0.5) * RS2PI
        a = (pre * cdf).astype(bf)
        act[rj, :] = a
        dg[rj, :] = (cdf + pre * pdf).astype(bf)
        acc[r, :] += nn(a, wu[pl.ds(pl.multiple_of(768 * j, 16), 768), :])
        return 0

    lax.fori_loop(0, NB, p2, 0)
    y(9)
    x(8)
    lax.fori_loop(NB, 2 * NB, p2, 0)
    y(10)
    x(9)
    y(11)
    x(10)
    x(11)
    ready(range(6, NPC), (3, 4))
    lax.fori_loop(2 * NB, 4 * NB, p2, 0)
    out(9, act)

    def p3(i, _):
        r = rows(i)
        h = nrm[r, :].astype(f32) + acc[r, :] + row(3)
        xh, rr = norm(h)
        lo[r, :] = (xh * row(6) + row(7)).astype(bf)
        g = cot[r, :].astype(f32)
        gv[6:7, :] += jnp.sum(g * xh, 0, keepdims=True)
        gv[7:8, :] += jnp.sum(g, 0, keepdims=True)
        e = g * row(6)
        d = rr * (e - jnp.mean(e, 1, keepdims=True) - xh * jnp.mean(e * xh, 1, keepdims=True))
        g2[r, :] = d
        db = d.astype(bf)
        od[r, :] = db
        gv[3:4, :] += jnp.sum(db.astype(f32), 0, keepdims=True)
        return 0

    lax.fori_loop(0, NB, p3, 0)
    out(10, lo)
    out(11, od)

    def p4(u, _):
        j = lax.div(u, NB)
        i = lax.rem(u, NB)
        r = rows(i)
        rj = rows(i, j)
        d = (nt(od[r, :], wu[pl.ds(pl.multiple_of(768 * j, 16), 768), :]) * dg[rj, :].astype(f32)).astype(bf)
        dg[rj, :] = d
        gv[pl.ds(8 + j, 1), :] += jnp.sum(d.astype(f32), 0, keepdims=True)
        g2[r, :] += nt(d, wi[:, pl.ds(pl.multiple_of(768 * j, 128), 768)])
        return 0

    lax.fori_loop(0, 4 * NB, p4, 0)
    out(12, dg)
    heads = lax.broadcasted_iota(jnp.int32, (16, D), 0)
    onehot = jnp.where(lax.div(lax.broadcasted_iota(jnp.int32, (16, D), 1), 64) == heads, 1.0, 0.0)
    for i in range(NB):
        r = slice(i * B, i * B + B)
        g = g2[r, :]
        xh = xh1[r, :]
        rr = r1s[r, 0:1]
        gv[4:5, :] += jnp.sum(g * xh, 0, keepdims=True)
        gv[5:6, :] += jnp.sum(g, 0, keepdims=True)
        e = g * row(4)
        d = rr * (e - jnp.mean(e, 1, keepdims=True) - xh * jnp.mean(e * xh, 1, keepdims=True))
        g2[r, :] = d
        db = d.astype(bf)
        ad[r, :] = db
        gv[2:3, :] += jnp.sum(db.astype(f32), 0, keepdims=True)
        cd = nt(db, wo[...]).astype(bf).astype(f32)
        sc = cd * (1.0 / rt[r, :])
        sd[r, :] = sc.astype(bf)
        ct[:, r] = lax.dot_general(
            onehot,
            sc * ctx[r, :].astype(f32),
            (((1,), (1,)), ((), ())),
            preferred_element_type=f32,
            precision=lax.Precision.HIGHEST,
        )
    for i, ref in ((13, ad), (14, sd), (15, ct), (16, gv), (17, g2)):
        out(i, ref)
    for i in range(TOKP):

        @pl.when(has_fwd)
        def _():
            tfw[i].wait_send()

        tcp[i].wait_send()
    for cps in wcp:
        for cp in cps:
            if cp is not None:
                cp.wait_send()
    for v in vcp:
        v.wait_send()
    for cp in sent:
        cp.wait()


def front(n, tok, shards, vecs, cot, lens):
    R = tok.shape[0]
    S = jax.ShapeDtypeStruct
    ANY = pl.BlockSpec(memory_space=pl.ANY)
    F = shards[4].shape[1]
    NPC = len(PIECES)
    row = (R, D)
    W = (D, D)
    outs = [S(W, bf)] * 3 + [S((3 * R, D), bf), S(row, bf), S((3 * R, D), bf), S((3 * R, D), bf)]
    outs += [S(row, bf), S(row, bf), S((4 * R, D), bf), S(row, bf), S(row, bf), S((4 * R, D), bf)]
    outs += [S(row, bf), S(row, bf), S((16, R), f32), S((16, D), f32), S(row, f32), S((8, 128), jnp.int32)]
    scratch = [VM((3 * R, D), bf)] + [VM(W, bf)] * 4 + [VM((D, F), bf), VM((F, D), bf), VM((4, 16, D), bf)]
    scratch += [VM(row, bf), VM((3 * R, D), bf), VM((3 * R, D), bf), VM(row, bf), VM(row, f32), VM((3 * R, 128), bf)]
    scratch += [VM((4 * R, D), bf), VM((4 * R, D), bf)] + [VM(row, bf)] * 4
    scratch += [VM((16, R), f32), VM((16, D), f32), VM(row, f32), VM(row, f32), VM(row, f32), VM((R, 128), f32)]
    scratch += [VM(row, bf), VM(row, bf), VM((8, 128), jnp.int32), VM((16, D), bf), VM((16, D), f32)]
    scratch += [DMA((2, TOKP)), DMA((2, TOKP)), DMA((NPC, 5)), DMA((NPC, 5)), DMA((3,)), DMA((3,)), DMA((8,)), DMA((19,))]
    return pl.pallas_call(
        functools.partial(front_kernel, n),
        out_shape=outs,
        in_specs=[ANY] * 7 + [FULL] * 9 + [ANY, FULL],
        out_specs=[ANY] * 19,
        scratch_shapes=scratch,
        compiler_params=pltpu.CompilerParams(collective_id=1, has_side_effects=True, vmem_limit_bytes=VLIM),
        name="front",
    )(tok, *shards, *vecs, cot, lens)


NP = 12
NH = 2 * NP
WINDOW = 3
LATE = NH
LAG = 2
TURN = 3
HCH = 16
HLAG = 3


def extra_bits(n):
    return [1 << j for j in range(3, 16) if (1 << j) < n]


def add_rows(dst, a, b, rows, step=48):
    def body(i, _):
        r = pl.ds(pl.multiple_of(i * step, 16), step)
        dst[r, :] = a[r, :] + b[r, :]
        return 0

    lax.fori_loop(0, rows // step, body, 0)


def back_kernel(n, *refs):
    hbm = refs[:14]
    gvin, ct, se = refs[14:17]
    OUT, vout, hin, gx_o = refs[17:21]
    bufs = refs[21:32]
    A, od, nrm, I, ctx, ad, q, k_, v_, sd, xe = bufs
    wq = k_.at[pl.ds(0, D)]
    wk = v_.at[pl.ds(0, D)]
    wv = v_.at[pl.ds(D, D)]
    bufs = bufs + (wq, wk, wv)
    G, RC, RY, RX, RZ, RW, RE, VR, vacc, HR, nseg, dk, dv = refs[32:45]
    ld, cs, cr, ss, sr, vs, vr, hs, hrs = refs[45:]
    dqb = q
    R = q.shape[0]
    extra = extra_bits(n)
    c = lax.axis_index("ctx")
    f = lax.axis_index("fsdp")
    cb = bit(f, 1)
    yb = bit(f, 2)
    sib = (c, flip(f, 1))
    yp = (c, flip(f, 2))
    p = [(flip(c, 1 << j), f) for j in range(3)]
    peers = [sib, yp] + p + [(flip(c, b), f) for b in extra]
    odd = bit(c, 1) == 1
    fwd = jnp.where(odd, c + 2, c - 2)
    src = jnp.where(odd, c - 2, c + 2)
    has_fwd = jnp.logical_and(fwd >= 0, fwd < n)
    has_src = jnp.logical_and(src >= 0, src < n)
    oth = jnp.where(bit(c, 2) == 0, c - 2, c + 2)
    has_oth = jnp.logical_and(oth >= 0, oth < n)
    loads = [pltpu.make_async_copy(hbm[i], bufs[i], ld.at[i]) for i in range(14)]
    for cp in loads[:10]:
        cp.start()
    greet(peers, ((has_oth, (oth, f)),))
    loads[10].start()

    bit0 = bit(c, 1)
    bit1 = bit(c, 2)

    def turned(m):
        return (m % TURN == TURN - 1) if isinstance(m, int) else (lax.rem(m, TURN) == TURN - 1)

    def pick(m, one, two):
        t = turned(m)
        if isinstance(t, bool):
            return two if t else one
        return jnp.where(t, two, one)

    def core(k, yy):
        return remote(G.at[k, 2 * yy + (1 - cb)], RC.at[k, yy], cs.at[k, yy], cr.at[k, yy], sib)

    def place(m):
        return (m // 2, m % 2) if isinstance(m, int) else (lax.div(m, 2), lax.rem(m, 2))

    def quarter(m, q):
        k, h = place(m)
        return G.at[k, q, h]

    def part(ref, m, r=None):
        k, h = place(m)
        return ref.at[k, h] if r is None else ref.at[k, h, r]

    def put(k, g):
        for h in range(2):
            G[k, :, h] = g[:, 384 * h : 384 * h + 384].astype(bf).reshape(4, 192, 384)

    def first(m):
        return pl.multiple_of(pick(m, bit0, bit1) * 96, 16)

    def second(m):
        return first(m) + pl.multiple_of(pick(m, bit1, bit0) * 48, 16)

    def rows_of(ref, m, r, size):
        return ref.at[pl.ds(pl.multiple_of(r, 16), size)]

    def acc(m):
        return quarter(m, 2 * yb + cb)

    def spare(m, i):
        return part(RY, m, pl.ds(48 * (i % 4), 48))

    def copy(m, i):
        s = (ss.at[m, i], sr.at[m, i])
        pa = (pick(m, flip(c, 1), flip(c, 2)), f)
        pb = (pick(m, flip(c, 2), flip(c, 1)), f)
        if i == 0:
            return remote(quarter(m, 2 * (1 - yb) + cb), part(RY, m), *s, yp)
        if i == 1:
            return remote(rows_of(acc(m), m, 96 - first(m), 96), part(RX, m), *s, pa)
        if i == 2:
            r = first(m) + 48 - pick(m, bit1, bit0) * 48
            return remote(rows_of(acc(m), m, r, 48), part(RZ, m), *s, pb)
        if i == 3:
            return remote(rows_of(acc(m), m, second(m), 48), part(RW, m), *s, p[2])
        if i == 4:
            o = part(OUT, m, pl.ds(pl.multiple_of(second(m), 16), 48))
            return remote(o, o, *s, pb)
        if i == 5:
            o = part(OUT, m, pl.ds(first(m), 96))
            return remote(o, o, *s, pa)
        e = extra[i - 6]
        return remote(spare(m, i - 6), part(RE.at[i - 6], m), *s, (flip(c, e), f))

    def give(k):
        for yy in range(2):
            core(k, yy).start()

    def s1(k):
        for yy in range(2):
            core(k, yy).wait_recv()
        for yy in range(2):
            for h in range(2):
                g = G.at[k, 2 * yy + cb, h]
                add_rows(g, g, RC.at[k, yy, h], 192)

    def s2(m):
        copy(m, 0).wait_recv()
        if isinstance(m, int):
            if m + WINDOW < LATE:
                copy(m + WINDOW, 0).start()
        else:

            @pl.when(m + WINDOW < LATE)
            def _():
                copy(m + WINDOW, 0).start()

        add_rows(acc(m), acc(m), part(RY, m), 192)
        copy(m, 1).start()

    def s3(m):
        copy(m, 1).wait_recv()
        a = rows_of(acc(m), m, first(m), 96)
        add_rows(a, a, part(RX, m), 96)
        copy(m, 2).start()

    def s4(m):
        copy(m, 2).wait_recv()
        a = rows_of(acc(m), m, second(m), 48)
        add_rows(a, a, part(RZ, m), 48)
        copy(m, 3).start()

    def s5(m):
        copy(m, 3).wait_recv()
        last = rows_of(acc(m), m, second(m), 48)
        got = part(RW, m)
        for i in range(len(extra)):
            add_rows(spare(m, i), last, got, 48)
            copy(m, 6 + i).start()
            copy(m, 6 + i).wait_recv()
            last = spare(m, i)
            got = part(RE.at[i], m)
        add_rows(part(OUT, m, pl.ds(pl.multiple_of(second(m), 16), 48)), last, got, 48)
        copy(m, 4).start()

    def s6(m):
        copy(m, 4).wait_recv()
        copy(m, 5).start()

    def s7(m):
        copy(m, 5).wait_recv()

    stages = (s2, s3, s4, s5, s6, s7)

    def tick(t):
        for i in range(len(stages)):
            m = t - LAG * i
            if isinstance(t, int):
                if 0 <= m < NH:
                    stages[i](m)
            else:

                @pl.when(jnp.logical_and(m >= 0, m < NH))
                def _():
                    stages[i](m)

    def both(t):
        for i in reversed(range(len(stages))):
            for m in (t - LAG * i, t + 1 - LAG * i):
                if 0 <= m < NH:
                    stages[i](m)

    def outer(hh, qq):
        g = tn(A[pl.ds(pl.multiple_of(qq * R, R), R), 384 * hh : 384 * hh + 384], od[...]).astype(bf)
        for h in range(2):
            G[2 * hh, qq, h] = g[:192, 384 * h : 384 * h + 384]
            G[2 * hh + 1, qq, h] = g[192:, 384 * h : 384 * h + 384]

    loads[0].wait()
    loads[1].wait()
    for hh in range(2):
        for yy in range(2):
            outer(hh, 2 * yy + (1 - cb))
        give(2 * hh)
        give(2 * hh + 1)
        for yy in range(2):
            outer(hh, 2 * yy + cb)
    for k in range(2):
        s1(k)
        for m in (2 * k, 2 * k + 1):
            if m < WINDOW:
                copy(m, 0).start()
    loads[2].wait()
    loads[3].wait()
    for j in range(4):
        put(4 + j, tn(nrm[...], I[R * j : R * j + R, :]))
        give(4 + j)
        if j < 2:
            s1(2 + j)
        if j == 2:
            tick(0)
    s1(4)
    tick(1)
    loads[4].wait()
    loads[5].wait()
    put(8, tn(ctx[...], ad[...]))
    give(8)
    for k in (5, 6, 7):
        s1(k)
    tick(2)
    s1(8)

    anchor = c * R

    def prep(i, _):
        r = pl.ds(pl.multiple_of(i * 256, 256), 256)
        nseg[r, :] = jnp.where(member(anchor - R + i * 256, 256, se), 0.0, 1.0).astype(bf)
        dk[r, :] = jnp.zeros((256, 128), f32)
        dv[r, :] = jnp.zeros((256, 128), f32)
        return 0

    lax.fori_loop(0, 3 * R // 256, prep, 0)
    lane = lax.broadcasted_iota(jnp.int32, (BQ, 128), 1)
    nqb = R // BQ
    for i in range(6, 10):
        loads[i].wait()

    def head(i, _):
        hp = lax.div(i, nqb)
        qb = lax.rem(i, nqb)
        hc = pl.ds(pl.multiple_of(hp * 128, 128), 128)
        qr = pl.ds(pl.multiple_of(qb * BQ, BQ), BQ)
        wr = pl.ds(pl.multiple_of(qb * BQ, BQ), WIN)
        oh = jnp.where(nseg[pl.ds(pl.multiple_of(R + qb * BQ, BQ), BQ), :] == 0, -BIG, 0.0).astype(bf)
        qp = q[qr, hc]
        sp = sd[qr, hc]
        kp = k_[wr, hc]
        vp = v_[wr, hc]
        kk = jnp.concatenate([kp, nseg[wr, :]], 1)
        z = jnp.zeros_like(qp)
        dkp = []
        dvp = []
        dqs = []
        for h in range(2):
            sel = (lane < 64) if h == 0 else (lane >= 64)
            qm = jnp.where(sel, qp, z)
            sm = jnp.where(sel, sp, z)
            pr = jnp.exp2(nt(kk, jnp.concatenate([qm, oh], 1)) * C2)
            dp = nt(vp, sm)
            ds = (pr * (dp - ct[pl.ds(2 * hp + h, 1), qr])).astype(bf)
            dvp.append(nn(pr.astype(bf), sm))
            dkp.append(nn(ds, qm))
            dqs.append(tn(ds, kp))
        dk[wr, :] += dkp[0] + dkp[1]
        dv[wr, :] += dvp[0] + dvp[1]
        dqb[qr, hc] = (jnp.where(lane < 64, dqs[0], dqs[1]) * 0.125).astype(bf)

        @pl.when(qb == nqb - 1)
        def _():
            def fin(j, _):
                r = pl.ds(pl.multiple_of(j * 256, 256), 256)
                A[r, hc] = (dk[r, :] * 0.125).astype(bf)
                I[r, hc] = dv[r, :].astype(bf)
                dk[r, :] = jnp.zeros((256, 128), f32)
                dv[r, :] = jnp.zeros((256, 128), f32)
                return 0

            lax.fori_loop(0, 3 * R // 256, fin, 0)

        tick(i + 3)

        return 0

    lax.fori_loop(0, 6 * nqb, head, 0)
    t = 6 * nqb + 3

    W3 = 3 * R
    own = slice(R, 2 * R)
    for cp in loads[11:]:
        cp.start()
    loads[10].wait()
    vacc[0] = gvin[...]
    vacc[0, 0:1, :] = jnp.sum(dqb[...].astype(f32), 0, keepdims=True)
    vacc[0, 1:2, :] = jnp.sum(I[0:W3, :].astype(f32), 0, keepdims=True)
    for cp in loads[11:]:
        cp.wait()
    for dst, r in ((od, slice(0, R)), (nrm, slice(2 * R, W3))):
        dst[...] = (nt(A[r, :], wk[...]) + nt(I[r, :], wv[...])).astype(bf)

    @pl.when(odd)
    def _():
        ad[...] = od[...]

    @pl.when(jnp.logical_not(odd))
    def _():
        ad[...] = nrm[...]

    hn = R // HCH

    def leg1(ref, j):
        r = pl.ds(j * hn, hn)
        return remote(ref.at[r], HR.at[r], hs.at[0, j], hrs.at[0, j], (fwd, f))

    def leg2(j):
        r = pl.ds(j * hn, hn)
        return remote(ad.at[r], hin.at[r], hs.at[1, j], hrs.at[1, j], p[0])

    def halo(j):
        if 0 <= j < HCH:

            @pl.when(jnp.logical_and(has_fwd, odd))
            def _():
                leg1(nrm, j).start()

            @pl.when(jnp.logical_and(has_fwd, jnp.logical_not(odd)))
            def _():
                leg1(od, j).start()

        j = j - HLAG
        if 0 <= j < HCH:

            @pl.when(has_src)
            def _():
                leg1(od, j).wait_recv()
                r = pl.ds(j * hn, hn)
                add_rows(ad.at[r], ad.at[r], HR.at[r], hn, 32)

            leg2(j).start()

    halo(0)
    put(9, tn(xe[...], I[0:W3, :]))
    give(9)
    halo(1)
    put(10, tn(xe[...], A[0:W3, :]))
    give(10)
    s1(9)
    tick(t)
    halo(2)
    tick(t + 1)
    put(11, tn(xe[own, :], dqb[...]))
    give(11)
    s1(10)
    tick(t + 2)
    halo(3)
    tick(t + 3)
    ctx[...] = (nt(dqb[...], wq[...]) + nt(A[own, :], wk[...]) + nt(I[own, :], wv[...])).astype(bf)
    gxc = pltpu.make_async_copy(ctx, gx_o, ld.at[14])
    gxc.start()
    s1(11)
    vround = 0
    hj = 4
    for step in range(t + 4, NH + LAG * (len(stages) - 1)):
        if step < NH:
            tick(step)
        elif (step - NH) % 2 == 0:
            both(step)
        halo(hj)
        hj += 1
        if vround <= len(peers) and step % 2 == 0:
            if vround > 0:
                exchange.wait()
                vacc[vround] = vacc[vround - 1] + VR[vround - 1]
            if vround < len(peers):
                exchange = remote(vacc.at[vround], VR.at[vround], vs.at[vround], vr.at[vround], peers[vround])
                exchange.start()
            vround += 1
    while vround <= len(peers):
        exchange.wait()
        vacc[vround] = vacc[vround - 1] + VR[vround - 1]
        if vround < len(peers):
            exchange = remote(vacc.at[vround], VR.at[vround], vs.at[vround], vr.at[vround], peers[vround])
            exchange.start()
        vround += 1
    while hj < HCH + HLAG:
        halo(hj)
        hj += 1
    vout[...] = vacc[len(peers)]
    for j in range(HCH):
        leg2(j).wait()

        @pl.when(has_fwd)
        def _():
            leg1(od, j).wait_send()

    def done(m, _):
        core(lax.div(m, 2), lax.rem(m, 2)).wait_send()
        for i in range(6 + len(extra)):
            copy(m, i).wait_send()
        return 0

    lax.fori_loop(0, NH, done, 0)
    gxc.wait()


def back(n, act, od, nrm, idel, ctx, ad, q, k, v, sd, xe, wq, wk, wv, gv, ct, se):
    R = q.shape[0]
    ne = len(extra_bits(n))
    nv = 5 + ne
    S = jax.ShapeDtypeStruct
    ANY = pl.BlockSpec(memory_space=pl.ANY)
    big = (act, od, nrm, idel, ctx, ad, q, k, v, sd, xe, wq, wk, wv)
    return pl.pallas_call(
        functools.partial(back_kernel, n),
        out_shape=[S((NP, 2, 192, 384), bf), S((16, D), f32), S((R, D), bf), S((R, D), bf)],
        in_specs=[ANY] * 14 + [FULL] * 3,
        out_specs=[FULL] * 3 + [ANY],
        scratch_shapes=[VM(t.shape, t.dtype) for t in big[:11]]
        + [
            VM((NP, 4, 2, 192, 384), bf),
            VM((NP, 2, 2, 192, 384), bf),
            VM((NP, 2, 192, 384), bf),
            VM((NP, 2, 96, 384), bf),
            VM((NP, 2, 48, 384), bf),
            VM((NP, 2, 48, 384), bf),
            VM((ne, NP, 2, 48, 384) if ne else (1, 1, 2, 48, 384), bf),
            VM((nv, 16, D), f32),
            VM((nv + 1, 16, D), f32),
            VM((R, D), bf),
            VM((3 * R, 128), bf),
            VM((3 * R, 128), f32),
            VM((3 * R, 128), f32),
            DMA((15,)),
            DMA((NP, 2)),
            DMA((NP, 2)),
            DMA((NH, 6 + ne)),
            DMA((NH, 6 + ne)),
            DMA((nv,)),
            DMA((nv,)),
            DMA((2, HCH)),
            DMA((2, HCH)),
        ],
        compiler_params=pltpu.CompilerParams(collective_id=2, has_side_effects=True, vmem_limit_bytes=61 * 2**20),
        name="back",
    )(*big, gv, ct, se)


def last_kernel(g, gv, g1, gx, hin, gq, gk, gw, go, gi, gu, gt, *vecs):
    for h in range(2):
        cs = slice(384 * h, 384 * h + 384)
        for ref, k in ((gw, 9), (gk, 10), (gq, 11), (go, 8)):
            ref[:, cs] = g[k, h].astype(f32)
        for j in range(4):
            gi[:, 768 * j + 384 * h : 768 * j + 384 * h + 384] = g[4 + j, h].astype(f32)
            gu[192 * j : 192 * j + 192, cs] = g[j, h].astype(f32)
    gt[...] = g1[...] + gx[...].astype(f32) + hin[...].astype(f32)
    f = lax.axis_index("fsdp")
    w = D // 4
    own = lax.broadcasted_iota(jnp.int32, (D, w), 0) == lax.broadcasted_iota(jnp.int32, (D, w), 1) + f * w
    rows = lax.dot_general(
        gv[0:8, :],
        jnp.where(own, 1.0, 0.0),
        (((1,), (0,)), ((), ())),
        preferred_element_type=f32,
        precision=lax.Precision.HIGHEST,
    )
    for j in range(8):
        vecs[j][...] = rows[j : j + 1, :].reshape(w)
    vecs[8][...] = gv[pl.ds(8 + f, 1), :].reshape(D)


def last(g, gv, g1, gx, hin):
    R = g1.shape[0]
    S = jax.ShapeDtypeStruct
    outs = [S((192, D), f32)] * 4 + [S((192, 4 * D), f32), S((4 * 192, D), f32), S((R, D), f32)]
    outs += [S((D // 4,), f32)] * 8 + [S((D,), f32)]
    return pl.pallas_call(
        last_kernel,
        out_shape=outs,
        in_specs=[FULL] * 5,
        out_specs=[FULL] * 16,
        compiler_params=pltpu.CompilerParams(vmem_limit_bytes=VLIM),
        name="last",
    )(g, gv, g1, gx, hin)


def local(n, tokens, doc_lengths, cotangent, wq, wk, wv, wo, wi, wu, bq, bv, bo, bi, bu, ga, sa, gf, sf):
    x = tokens[0]
    docs = doc_lengths.shape[1]
    assert docs <= 128 and x.shape[0] == 512
    vecs = (bq, bv, bo, bu, ga, sa, gf, sf, bi)
    wq, wk, wv, xe, q, k, v, ctx, nrm, act, layer_out, od, idel, ad, sd, ct, gv, g1, se = front(
        n, x, (wq, wk, wv, wo, wi, wu), vecs, cotangent[0], doc_lengths
    )
    g, gv, hin, gx = back(n, act, od, nrm, idel, ctx, ad, q, k, v, sd, xe, wq, wk, wv, gv, ct, se)
    gq, gk, gw, go, gi, gu, gt, *gs, gbi = last(g, gv, g1, gx, hin)
    return (layer_out[None], gt[None], gq, gk, gw, go, gi, gu, gs[0], gs[1], gs[2], gbi, *gs[3:])


def solution(mesh):
    n = mesh.shape["ctx"]
    tok = P("fsdp", "ctx", None)
    mat = P("fsdp", None)
    vec = P("fsdp")
    return jax.shard_map(
        functools.partial(local, n),
        mesh=mesh,
        in_specs=(tok, mat, tok) + (mat,) * 6 + (vec,) * 9,
        out_specs=(tok, tok) + (mat,) * 6 + (vec,) * 9,
        check_vma=False,
    )
```

```python
import functools

import jax
import jax.numpy as jnp
from jax import lax
from jax.experimental import pallas as pl
from jax.experimental.pallas import tpu as pltpu
from jax.sharding import PartitionSpec as P

bf = jnp.bfloat16
f32 = jnp.float32
MESH = pl.DeviceIdType.MESH
VM = pltpu.VMEM
DMA = pltpu.SemaphoreType.DMA
D = 768
EPS = 1e-12
BIG = 1e30
C2 = 0.125 * 1.4426950408889634
RSQ2 = 0.7071067811865476
RS2PI = 0.3989422804014327
BQ = 256
WIN = BQ + 1024
TOKP = 8
HS = 192
VLIM = 58 * 2**20
FULL = pl.BlockSpec(memory_space=pltpu.VMEM)


def nt(a, b):
    return lax.dot_general(a, b, (((1,), (1,)), ((), ())), preferred_element_type=f32)


def nn(a, b):
    return lax.dot_general(a, b, (((1,), (0,)), ((), ())), preferred_element_type=f32)


def tn(a, b):
    return lax.dot_general(a, b, (((0,), (0,)), ((), ())), preferred_element_type=f32)


def bit(i, b):
    return lax.rem(lax.div(i, b), 2)


def flip(i, b):
    return i + b * (1 - 2 * bit(i, b))


def remote(src, dst, send, recv, device):
    return pltpu.make_async_remote_copy(
        src_ref=src, dst_ref=dst, send_sem=send, recv_sem=recv, device_id=device, device_id_type=MESH
    )


def greet(peers, others):
    bar = pltpu.get_barrier_semaphore()
    for d in peers:
        pl.semaphore_signal(bar, inc=1, device_id=d, device_id_type=MESH)
    for cond, d in others:

        @pl.when(cond)
        def _():
            pl.semaphore_signal(bar, inc=1, device_id=d, device_id_type=MESH)

    pl.semaphore_wait(bar, len(peers) + sum(cond.astype(jnp.int32) for cond, _ in others))


def vecs_of(vec):
    return (vec[0].astype(f32) + vec[1].astype(f32)) + (vec[2].astype(f32) + vec[3].astype(f32))


def member(pos0, rows, se):
    pos = pos0 + lax.broadcasted_iota(jnp.int32, (rows, 128), 0)
    return jnp.logical_and(pos >= se[0:1, :], pos < se[1:2, :])


def norm(h):
    c = h - jnp.mean(h, 1, keepdims=True)
    r = lax.rsqrt(jnp.mean(c * c, 1, keepdims=True) + EPS)
    return c * r, r


PIECES = [(0, 0, 192, 0, 768, 2), (1, 0, 192, 0, 768, 0), (2, 0, 192, 0, 768, 0), (3, 0, 192, 0, 768, 1)]
PIECES += [(4, 0, 192, None, 768, 1 if j < 3 else 2) for j in range(4)]
PIECES += [(5, 192 * j, 192, 0, 768, 1 if j in (1, 3) else 2) for j in range(4)]
YWIN = 4


def front_kernel(n, *refs):
    tok, *sh = refs[:7]
    *small, inner_v, cot_h, lens = refs[7:18]
    outs = refs[18:37]
    (xe, wq, wk, wv, wo, wi, wu, vecb, q_o, k_o, v_o, ctx, rt, nseg, act, dg, od, nrm, ad, sd, ct, gv, g2, xh1, acc, r1s, cot, lo, se, vec, vrow) = refs[37:68]
    ts, tr, ws, wr, vs, vr, ls, osem = refs[68:]
    full = (wq, wk, wv, wo, wi, wu)
    c = lax.axis_index("ctx")
    f = lax.axis_index("fsdp")
    sib = (c, flip(f, 1))
    yp = (c, flip(f, 2))
    dgn = (c, flip(flip(f, 1), 2))
    c1 = (flip(c, 1), f)
    c2 = (flip(c, 2), f)
    even = bit(c, 1) == 0
    fwd = jnp.where(even, c + 2, c - 2)
    src = jnp.where(even, c - 2, c + 2)
    has_fwd = jnp.logical_and(fwd >= 0, fwd < n)
    has_src = jnp.logical_and(src >= 0, src < n)
    oth = jnp.where(bit(c, 2) == 0, c - 2, c + 2)
    has_oth = jnp.logical_and(oth >= 0, oth < n)
    R = xe.shape[0] // 3

    locs = [pltpu.make_async_copy(tok, xe.at[pl.ds(R, R)], ls.at[0])]
    for i, (s, w) in enumerate(zip(sh, full)):
        H = s.shape[0]
        locs.append(pltpu.make_async_copy(s, w.at[pl.ds(pl.multiple_of(f * H, 16), H)], ls.at[1 + i]))
    locs.append(pltpu.make_async_copy(cot_h, cot, ls.at[7]))
    greet((sib, yp, dgn, c1, c2), ((has_oth, (oth, f)),))
    pr = R // TOKP
    pslot = jnp.where(even, 2 * R, 0)
    dslot = jnp.where(even, 0, 2 * R)
    tcp = [
        remote(
            tok.at[pl.ds(i * pr, pr)],
            xe.at[pl.ds(pl.multiple_of(dslot + i * pr, pr), pr)],
            ts.at[0, i],
            tr.at[0, i],
            c1,
        )
        for i in range(TOKP)
    ]
    vcp = [remote(vec, vecb.at[f], vs.at[i], vr.at[i], (sib, yp, dgn)[i]) for i in range(3)]
    wcp = []
    fy = flip(f, 2)
    for k, (t, r0, H2, c0, C, route) in enumerate(PIECES):
        s = sh[t]
        w = full[t]
        SR = s.shape[0]
        cg = cs_ = slice(c0, c0 + C) if c0 is not None else None
        if c0 is None:
            j = k - 4
            mix = flip(flip(f, 1), 2) if j == 3 else (flip(f, j) if j else f)
            far = flip(mix, 2)
            cg = pl.ds(pl.multiple_of(mix * C, 128), C)
            cs_ = pl.ds(pl.multiple_of(far * C, 128), C)
        own = pl.multiple_of(f * SR + r0, 16)
        if route == 0:
            other = pl.multiple_of(fy * SR + r0, 16)
            wcp.append(
                [
                    remote(s.at[pl.ds(r0, H2), cg], w.at[pl.ds(own, H2), cg], ws.at[k, 0], wr.at[k, 0], sib),
                    remote(s.at[pl.ds(r0, H2), cs_], w.at[pl.ds(own, H2), cs_], ws.at[k, 1], wr.at[k, 1], yp),
                    None,
                    remote(w.at[pl.ds(other, H2), cg], w.at[pl.ds(other, H2), cg], ws.at[k, 3], wr.at[k, 3], sib),
                    None,
                ]
            )
            continue
        H = H2 // 2
        p = c1 if route == 1 else c2
        hb = bit(c, route)
        mine = pl.multiple_of(f * SR + r0 + hb * H, 16)
        gy = pl.multiple_of(fy * SR + r0 + hb * H, 16)
        gx = pl.multiple_of(fy * SR + r0 + (1 - hb) * H, 16)
        wcp.append(
            [
                remote(s.at[pl.ds(r0, H2), cg], w.at[pl.ds(own, H2), cg], ws.at[k, 0], wr.at[k, 0], sib),
                remote(
                    s.at[pl.ds(pl.multiple_of(r0 + hb * H, 16), H), cs_],
                    w.at[pl.ds(mine, H), cs_],
                    ws.at[k, 1],
                    wr.at[k, 1],
                    yp,
                ),
                remote(w.at[pl.ds(gy, H), cg], w.at[pl.ds(gy, H), cg], ws.at[k, 2], wr.at[k, 2], p),
                remote(w.at[pl.ds(gy, H), cg], w.at[pl.ds(gy, H), cg], ws.at[k, 3], wr.at[k, 3], sib),
                remote(w.at[pl.ds(gx, H), cg], w.at[pl.ds(gx, H), cg], ws.at[k, 4], wr.at[k, 4], sib),
            ]
        )
    NPC = len(PIECES)
    for k in range(YWIN):
        wcp[k][1].start()
    for t in tcp[:2]:
        t.start()
    for cp in locs[:4]:
        cp.start()
    for k in range(3):
        wcp[k][0].start()

    w8 = D // 4
    sel = lax.broadcasted_iota(jnp.int32, (w8, D), 0) + f * w8 == lax.broadcasted_iota(jnp.int32, (w8, D), 1)
    place = jnp.where(sel, 1.0, 0.0).astype(bf)
    r8 = lax.broadcasted_iota(jnp.int32, (8, w8), 0)
    rows8 = jnp.zeros((8, w8), f32)
    for j, ref in enumerate(small):
        rows8 = jnp.where(r8 == j, jnp.broadcast_to(ref[...].astype(f32).reshape(1, w8), (8, w8)), rows8)
    rows8 = rows8.astype(bf)
    isf = lax.broadcasted_iota(jnp.int32, (8, D), 0) == f
    inner = jnp.where(isf, jnp.broadcast_to(inner_v[...].astype(f32).reshape(1, D), (8, D)), 0.0)
    vec[...] = jnp.concatenate([nn(rows8, place), inner], 0).astype(bf)
    for v in vcp:
        v.start()
    vecb[f] = vec[...]
    docs = lens.shape[1]
    ln8 = jnp.broadcast_to(lens[...].astype(f32), (8, docs))
    la = lax.broadcasted_iota(jnp.int32, (docs, 128), 0)
    lb = lax.broadcasted_iota(jnp.int32, (docs, 128), 1)
    upto = jnp.where(jnp.logical_and(la <= lb, lb < docs), 1.0, 0.0)
    below = jnp.where(jnp.logical_and(la < lb, lb < docs), 1.0, 0.0)
    hi = lax.Precision.HIGHEST
    ends = jnp.dot(ln8, upto, preferred_element_type=f32, precision=hi)
    starts = jnp.dot(ln8, below, preferred_element_type=f32, precision=hi)
    first_row = lax.broadcasted_iota(jnp.int32, (8, 128), 0) == 0
    se[...] = jnp.where(first_row, starts, ends).astype(jnp.int32)

    @pl.when(jnp.logical_not(has_src))
    def _():
        xe[pl.ds(pl.multiple_of(dslot, R), R), :] = jnp.zeros((R, D), bf)

    tfw = [
        remote(
            xe.at[pl.ds(pl.multiple_of(pslot + i * pr, pr), pr)],
            xe.at[pl.ds(pl.multiple_of(dslot + i * pr, pr), pr)],
            ts.at[1, i],
            tr.at[1, i],
            (fwd, f),
        )
        for i in range(TOKP)
    ]

    def y(k):
        wcp[k][1].wait_recv()
        if wcp[k][2] is not None:
            wcp[k][2].start()
        wcp[k][3].start()
        if k + YWIN < NPC:
            wcp[k + YWIN][1].start()

    def x(k):
        wcp[k][2].wait_recv()
        wcp[k][4].start()

    def t(i):
        tcp[i].wait_recv()
        if i + 2 < TOKP:
            tcp[i + 2].start()

        @pl.when(has_fwd)
        def _():
            tfw[i].start()

    def ready(ks, parts=(0, 3, 4)):
        for k in ks:
            for i in parts:
                if wcp[k][i] is not None:
                    wcp[k][i].wait_recv()

    t(0)
    y(0)
    t(1)
    t(2)
    x(0)
    for cp in locs[4:]:
        cp.start()
    for k in range(3, NPC):
        wcp[k][0].start()
    t(3)
    y(1)
    for i in range(4, TOKP - 1):
        t(i)
    y(2)
    t(TOKP - 1)
    for cp in locs[:4]:
        cp.wait()
    for v in vcp:
        v.wait_recv()
    ready(range(3))
    anchor = c * R
    V = vecs_of(vecb)
    vrow[...] = V

    def row(i):
        return V[i : i + 1, :]

    def out(i, ref):
        cp = pltpu.make_async_copy(ref, outs[i], osem.at[i])
        cp.start()
        sent.append(cp)

    sent = []
    for i, w in enumerate((wq, wk, wv)):
        out(i, w)

    def proj(r):
        def body(i, _):
            rr = pl.ds(pl.multiple_of(r + i * 256, 256), 256)
            xb = xe[rr, :]
            k_o[rr, :] = nn(xb, wk[...]).astype(bf)
            v_o[rr, :] = (nn(xb, wv[...]) + row(1)).astype(bf)
            return 0

        lax.fori_loop(0, R // 256, body, 0)

    def projq(i, _):
        rr = pl.ds(pl.multiple_of(R + i * 256, 256), 256)
        q_o[pl.ds(pl.multiple_of(i * 256, 256), 256), :] = (nn(xe[rr, :], wq[...]) + row(0)).astype(bf)
        return 0

    def seg(i, _):
        rr = pl.ds(pl.multiple_of(i * 256, 256), 256)
        nseg[rr, :] = jnp.where(member(anchor - R + i * 256, 256, se), 0.0, 1.0).astype(bf)
        return 0

    lax.fori_loop(0, 3 * R // 256, seg, 0)
    lax.fori_loop(0, R // 256, projq, 0)
    proj(R)
    y(3)
    proj(pslot)
    y(4)
    x(3)
    for i in range(TOKP):

        @pl.when(has_src)
        def _():
            tfw[i].wait_recv()

    proj(dslot)
    out(18, se)
    out(3, xe)
    out(4, q_o)
    out(5, k_o)
    out(6, v_o)
    lane = lax.broadcasted_iota(jnp.int32, (BQ, 128), 1)
    nqb = R // BQ

    def att(i, _):
        qb = lax.div(i, 6)
        hp = lax.rem(i, 6)
        qr = pl.ds(pl.multiple_of(qb * BQ, BQ), BQ)
        wr_ = pl.ds(pl.multiple_of(qb * BQ, BQ), WIN)
        hc = pl.ds(pl.multiple_of(hp * 128, 128), 128)
        oh = jnp.where(nseg[pl.ds(pl.multiple_of(R + qb * BQ, BQ), BQ), :] == 0, -BIG, 0.0).astype(bf)
        qp = q_o[qr, hc]
        kk = jnp.concatenate([k_o[wr_, hc], nseg[wr_, :]], 1)
        vv = v_o[wr_, hc]
        res = []
        for h in range(2):
            sel = (lane < 64) if h == 0 else (lane >= 64)
            qa = jnp.concatenate([jnp.where(sel, qp, jnp.zeros_like(qp)), oh], 1)
            pe = jnp.exp2(nt(qa, kk) * C2)
            res.append((nn(pe.astype(bf), vv), jnp.sum(pe, 1, keepdims=True)))
        o = jnp.where(lane < 64, res[0][0], res[1][0])
        tot = jnp.where(lane < 64, res[0][1], res[1][1])
        ctx[qr, hc] = (o / tot).astype(bf)
        rt[qr, hc] = tot
        return 0

    pumps = ((y, 5), (x, 4)), ((y, 6), (x, 5)), ((y, 7), (x, 6)), ((y, 8), (x, 7))
    per = 6 * nqb // len(pumps)
    for gidx, steps in enumerate(pumps):
        lax.fori_loop(gidx * per, gidx * per + per, att, 0)
        for step, k in steps:
            step(k)
    out(7, ctx)

    B = 256
    NB = R // B

    def rows(i, j=0):
        return pl.ds(pl.multiple_of(j * R + i * B, B), B)

    ready((3,))
    locs[4].wait()
    gv[...] = jnp.zeros_like(gv)

    def p1(i, _):
        r = rows(i)
        h = xe[pl.ds(pl.multiple_of(R + i * B, B), B), :].astype(f32) + nn(ctx[r, :], wo[...]) + row(2)
        xh, rr = norm(h)
        xh1[r, :] = xh
        r1s[r, :] = jnp.broadcast_to(rr, (B, 128))
        nrm[r, :] = (xh * row(4) + row(5)).astype(bf)
        return 0

    lax.fori_loop(0, NB, p1, 0)
    out(8, nrm)
    for cp in locs[5:]:
        cp.wait()
    ready((4, 5))
    ready(range(6, NPC), (0,))

    acc[...] = jnp.zeros_like(acc)
    low_bit = bit(f, 1)
    high_bit = bit(f, 2)

    def p2(u, _):
        jj = lax.div(u, NB)
        i = lax.rem(u, NB)
        even_jj = 1 - lax.rem(jj, 2)
        j = jnp.where(even_jj == 1, low_bit, 1 - low_bit) + 2 * jnp.where(jj < 2, high_bit, 1 - high_bit)
        cs = pl.ds(pl.multiple_of(768 * j, 128), 768)
        r = rows(i)
        rj = rows(i, j)
        pre = nn(nrm[r, :], wi[:, cs]) + vrow[pl.ds(8 + j, 1), :]
        cdf = 0.5 + 0.5 * lax.erf(pre * RSQ2)
        pdf = jnp.exp(pre * pre * -0.5) * RS2PI
        a = (pre * cdf).astype(bf)
        act[rj, :] = a
        dg[rj, :] = (cdf + pre * pdf).astype(bf)
        acc[r, :] += nn(a, wu[pl.ds(pl.multiple_of(768 * j, 16), 768), :])
        return 0

    lax.fori_loop(0, NB, p2, 0)
    y(9)
    x(8)
    lax.fori_loop(NB, 2 * NB, p2, 0)
    y(10)
    x(9)
    y(11)
    x(10)
    x(11)
    ready(range(6, NPC), (3, 4))
    lax.fori_loop(2 * NB, 4 * NB, p2, 0)
    out(9, act)

    def p3(i, _):
        r = rows(i)
        h = nrm[r, :].astype(f32) + acc[r, :] + row(3)
        xh, rr = norm(h)
        lo[r, :] = (xh * row(6) + row(7)).astype(bf)
        g = cot[r, :].astype(f32)
        gv[6:7, :] += jnp.sum(g * xh, 0, keepdims=True)
        gv[7:8, :] += jnp.sum(g, 0, keepdims=True)
        e = g * row(6)
        d = rr * (e - jnp.mean(e, 1, keepdims=True) - xh * jnp.mean(e * xh, 1, keepdims=True))
        g2[r, :] = d
        db = d.astype(bf)
        od[r, :] = db
        gv[3:4, :] += jnp.sum(db.astype(f32), 0, keepdims=True)
        return 0

    lax.fori_loop(0, NB, p3, 0)
    out(10, lo)
    out(11, od)

    def p4(u, _):
        j = lax.div(u, NB)
        i = lax.rem(u, NB)
        r = rows(i)
        rj = rows(i, j)
        d = (nt(od[r, :], wu[pl.ds(pl.multiple_of(768 * j, 16), 768), :]) * dg[rj, :].astype(f32)).astype(bf)
        dg[rj, :] = d
        gv[pl.ds(8 + j, 1), :] += jnp.sum(d.astype(f32), 0, keepdims=True)
        g2[r, :] += nt(d, wi[:, pl.ds(pl.multiple_of(768 * j, 128), 768)])
        return 0

    lax.fori_loop(0, 4 * NB, p4, 0)
    out(12, dg)
    heads = lax.broadcasted_iota(jnp.int32, (16, D), 0)
    onehot = jnp.where(lax.div(lax.broadcasted_iota(jnp.int32, (16, D), 1), 64) == heads, 1.0, 0.0)
    for i in range(NB):
        r = slice(i * B, i * B + B)
        g = g2[r, :]
        xh = xh1[r, :]
        rr = r1s[r, 0:1]
        gv[4:5, :] += jnp.sum(g * xh, 0, keepdims=True)
        gv[5:6, :] += jnp.sum(g, 0, keepdims=True)
        e = g * row(4)
        d = rr * (e - jnp.mean(e, 1, keepdims=True) - xh * jnp.mean(e * xh, 1, keepdims=True))
        g2[r, :] = d
        db = d.astype(bf)
        ad[r, :] = db
        gv[2:3, :] += jnp.sum(db.astype(f32), 0, keepdims=True)
        cd = nt(db, wo[...]).astype(bf).astype(f32)
        sc = cd * (1.0 / rt[r, :])
        sd[r, :] = sc.astype(bf)
        ct[:, r] = lax.dot_general(
            onehot,
            sc * ctx[r, :].astype(f32),
            (((1,), (1,)), ((), ())),
            preferred_element_type=f32,
            precision=lax.Precision.HIGHEST,
        )
    for i, ref in ((13, ad), (14, sd), (15, ct), (16, gv), (17, g2)):
        out(i, ref)
    for i in range(TOKP):

        @pl.when(has_fwd)
        def _():
            tfw[i].wait_send()

        tcp[i].wait_send()
    for cps in wcp:
        for cp in cps:
            if cp is not None:
                cp.wait_send()
    for v in vcp:
        v.wait_send()
    for cp in sent:
        cp.wait()


def front(n, tok, shards, vecs, cot, lens):
    R = tok.shape[0]
    S = jax.ShapeDtypeStruct
    ANY = pl.BlockSpec(memory_space=pl.ANY)
    F = shards[4].shape[1]
    NPC = len(PIECES)
    row = (R, D)
    W = (D, D)
    outs = [S(W, bf)] * 3 + [S((3 * R, D), bf), S(row, bf), S((3 * R, D), bf), S((3 * R, D), bf)]
    outs += [S(row, bf), S(row, bf), S((4 * R, D), bf), S(row, bf), S(row, bf), S((4 * R, D), bf)]
    outs += [S(row, bf), S(row, bf), S((16, R), f32), S((16, D), f32), S(row, f32), S((8, 128), jnp.int32)]
    scratch = [VM((3 * R, D), bf)] + [VM(W, bf)] * 4 + [VM((D, F), bf), VM((F, D), bf), VM((4, 16, D), bf)]
    scratch += [VM(row, bf), VM((3 * R, D), bf), VM((3 * R, D), bf), VM(row, bf), VM(row, f32), VM((3 * R, 128), bf)]
    scratch += [VM((4 * R, D), bf), VM((4 * R, D), bf)] + [VM(row, bf)] * 4
    scratch += [VM((16, R), f32), VM((16, D), f32), VM(row, f32), VM(row, f32), VM(row, f32), VM((R, 128), f32)]
    scratch += [VM(row, bf), VM(row, bf), VM((8, 128), jnp.int32), VM((16, D), bf), VM((16, D), f32)]
    scratch += [DMA((2, TOKP)), DMA((2, TOKP)), DMA((NPC, 5)), DMA((NPC, 5)), DMA((3,)), DMA((3,)), DMA((8,)), DMA((19,))]
    return pl.pallas_call(
        functools.partial(front_kernel, n),
        out_shape=outs,
        in_specs=[ANY] * 7 + [FULL] * 9 + [ANY, FULL],
        out_specs=[ANY] * 19,
        scratch_shapes=scratch,
        compiler_params=pltpu.CompilerParams(collective_id=1, has_side_effects=True, vmem_limit_bytes=VLIM),
        name="front",
    )(tok, *shards, *vecs, cot, lens)


NP = 12
NH = 2 * NP
WINDOW = 3
LATE = NH
LAG = 2
TURN = 3
HCH = 16
HLAG = 3


def extra_bits(n):
    return [1 << j for j in range(3, 16) if (1 << j) < n]


def add_rows(dst, a, b, rows, step=48):
    def body(i, _):
        r = pl.ds(pl.multiple_of(i * step, 16), step)
        dst[r, :] = a[r, :] + b[r, :]
        return 0

    lax.fori_loop(0, rows // step, body, 0)


def back_kernel(n, *refs):
    hbm = refs[:14]
    gvin, ct, se = refs[14:17]
    OUT, vout, hin, gx_o = refs[17:21]
    bufs = refs[21:32]
    A, od, nrm, I, ctx, ad, q, k_, v_, sd, xe = bufs
    wq = k_.at[pl.ds(0, D)]
    wk = v_.at[pl.ds(0, D)]
    wv = v_.at[pl.ds(D, D)]
    bufs = bufs + (wq, wk, wv)
    G, RC, RY, RX, RZ, RW, RE, VR, vacc, HR, nseg, dk, dv = refs[32:45]
    ld, cs, cr, ss, sr, vs, vr, hs, hrs = refs[45:]
    dqb = q
    R = q.shape[0]
    extra = extra_bits(n)
    c = lax.axis_index("ctx")
    f = lax.axis_index("fsdp")
    cb = bit(f, 1)
    yb = bit(f, 2)
    sib = (c, flip(f, 1))
    yp = (c, flip(f, 2))
    p = [(flip(c, 1 << j), f) for j in range(3)]
    peers = [sib, yp] + p + [(flip(c, b), f) for b in extra]
    odd = bit(c, 1) == 1
    fwd = jnp.where(odd, c + 2, c - 2)
    src = jnp.where(odd, c - 2, c + 2)
    has_fwd = jnp.logical_and(fwd >= 0, fwd < n)
    has_src = jnp.logical_and(src >= 0, src < n)
    oth = jnp.where(bit(c, 2) == 0, c - 2, c + 2)
    has_oth = jnp.logical_and(oth >= 0, oth < n)
    loads = [pltpu.make_async_copy(hbm[i], bufs[i], ld.at[i]) for i in range(14)]
    for cp in loads[:2]:
        cp.start()
    greet(peers, ((has_oth, (oth, f)),))

    bit0 = bit(c, 1)
    bit1 = bit(c, 2)

    def turned(m):
        return (m % TURN == TURN - 1) if isinstance(m, int) else (lax.rem(m, TURN) == TURN - 1)

    def pick(m, one, two):
        t = turned(m)
        if isinstance(t, bool):
            return two if t else one
        return jnp.where(t, two, one)

    def core(k, yy):
        return remote(G.at[k, 2 * yy + (1 - cb)], RC.at[k, yy], cs.at[k, yy], cr.at[k, yy], sib)

    def place(m):
        return (m // 2, m % 2) if isinstance(m, int) else (lax.div(m, 2), lax.rem(m, 2))

    def quarter(m, q):
        k, h = place(m)
        return G.at[k, q, h]

    def part(ref, m, r=None):
        k, h = place(m)
        return ref.at[k, h] if r is None else ref.at[k, h, r]

    def put(k, g):
        for h in range(2):
            G[k, :, h] = g[:, 384 * h : 384 * h + 384].astype(bf).reshape(4, 192, 384)

    def first(m):
        return pl.multiple_of(pick(m, bit0, bit1) * 96, 16)

    def second(m):
        return first(m) + pl.multiple_of(pick(m, bit1, bit0) * 48, 16)

    def rows_of(ref, m, r, size):
        return ref.at[pl.ds(pl.multiple_of(r, 16), size)]

    def acc(m):
        return quarter(m, 2 * yb + cb)

    def spare(m, i):
        return part(RY, m, pl.ds(48 * (i % 4), 48))

    def copy(m, i):
        s = (ss.at[m, i], sr.at[m, i])
        pa = (pick(m, flip(c, 1), flip(c, 2)), f)
        pb = (pick(m, flip(c, 2), flip(c, 1)), f)
        if i == 0:
            return remote(quarter(m, 2 * (1 - yb) + cb), part(RY, m), *s, yp)
        if i == 1:
            return remote(rows_of(acc(m), m, 96 - first(m), 96), part(RX, m), *s, pa)
        if i == 2:
            r = first(m) + 48 - pick(m, bit1, bit0) * 48
            return remote(rows_of(acc(m), m, r, 48), part(RZ, m), *s, pb)
        if i == 3:
            return remote(rows_of(acc(m), m, second(m), 48), part(RW, m), *s, p[2])
        if i == 4:
            o = part(OUT, m, pl.ds(pl.multiple_of(second(m), 16), 48))
            return remote(o, o, *s, pb)
        if i == 5:
            o = part(OUT, m, pl.ds(first(m), 96))
            return remote(o, o, *s, pa)
        e = extra[i - 6]
        return remote(spare(m, i - 6), part(RE.at[i - 6], m), *s, (flip(c, e), f))

    def give(k):
        for yy in range(2):
            core(k, yy).start()

    def s1(k):
        for yy in range(2):
            core(k, yy).wait_recv()
        for yy in range(2):
            for h in range(2):
                g = G.at[k, 2 * yy + cb, h]
                add_rows(g, g, RC.at[k, yy, h], 192)

    def s2(m):
        copy(m, 0).wait_recv()
        if isinstance(m, int):
            if m + WINDOW < LATE:
                copy(m + WINDOW, 0).start()
        else:

            @pl.when(m + WINDOW < LATE)
            def _():
                copy(m + WINDOW, 0).start()

        add_rows(acc(m), acc(m), part(RY, m), 192)
        copy(m, 1).start()

    def s3(m):
        copy(m, 1).wait_recv()
        a = rows_of(acc(m), m, first(m), 96)
        add_rows(a, a, part(RX, m), 96)
        copy(m, 2).start()

    def s4(m):
        copy(m, 2).wait_recv()
        a = rows_of(acc(m), m, second(m), 48)
        add_rows(a, a, part(RZ, m), 48)
        copy(m, 3).start()

    def s5(m):
        copy(m, 3).wait_recv()
        last = rows_of(acc(m), m, second(m), 48)
        got = part(RW, m)
        for i in range(len(extra)):
            add_rows(spare(m, i), last, got, 48)
            copy(m, 6 + i).start()
            copy(m, 6 + i).wait_recv()
            last = spare(m, i)
            got = part(RE.at[i], m)
        add_rows(part(OUT, m, pl.ds(pl.multiple_of(second(m), 16), 48)), last, got, 48)
        copy(m, 4).start()

    def s6(m):
        copy(m, 4).wait_recv()
        copy(m, 5).start()

    def s7(m):
        copy(m, 5).wait_recv()

    stages = (s2, s3, s4, s5, s6, s7)

    def tick(t):
        for i in range(len(stages)):
            m = t - LAG * i
            if isinstance(t, int):
                if 0 <= m < NH:
                    stages[i](m)
            else:

                @pl.when(jnp.logical_and(m >= 0, m < NH))
                def _():
                    stages[i](m)

    def both(t):
        for i in reversed(range(len(stages))):
            for m in (t - LAG * i, t + 1 - LAG * i):
                if 0 <= m < NH:
                    stages[i](m)

    def outer(hh, qq):
        g = tn(A[pl.ds(pl.multiple_of(qq * R, R), R), 384 * hh : 384 * hh + 384], od[...]).astype(bf)
        for h in range(2):
            G[2 * hh, qq, h] = g[:192, 384 * h : 384 * h + 384]
            G[2 * hh + 1, qq, h] = g[192:, 384 * h : 384 * h + 384]

    loads[0].wait()
    loads[1].wait()
    for cp in loads[2:11]:
        cp.start()
    for hh in range(2):
        for yy in range(2):
            outer(hh, 2 * yy + (1 - cb))
        give(2 * hh)
        give(2 * hh + 1)
        for yy in range(2):
            outer(hh, 2 * yy + cb)
    for k in range(2):
        s1(k)
        for m in (2 * k, 2 * k + 1):
            if m < WINDOW:
                copy(m, 0).start()
    loads[2].wait()
    loads[3].wait()
    for j in range(4):
        put(4 + j, tn(nrm[...], I[R * j : R * j + R, :]))
        give(4 + j)
        if j < 2:
            s1(2 + j)
        if j == 2:
            tick(0)
    s1(4)
    tick(1)
    loads[4].wait()
    loads[5].wait()
    put(8, tn(ctx[...], ad[...]))
    give(8)
    for k in (5, 6, 7):
        s1(k)
    tick(2)
    s1(8)

    anchor = c * R

    def prep(i, _):
        r = pl.ds(pl.multiple_of(i * 256, 256), 256)
        nseg[r, :] = jnp.where(member(anchor - R + i * 256, 256, se), 0.0, 1.0).astype(bf)
        dk[r, :] = jnp.zeros((256, 128), f32)
        dv[r, :] = jnp.zeros((256, 128), f32)
        return 0

    lax.fori_loop(0, 3 * R // 256, prep, 0)
    lane = lax.broadcasted_iota(jnp.int32, (BQ, 128), 1)
    nqb = R // BQ
    for i in range(6, 10):
        loads[i].wait()

    def head(i, _):
        hp = lax.div(i, nqb)
        qb = lax.rem(i, nqb)
        hc = pl.ds(pl.multiple_of(hp * 128, 128), 128)
        qr = pl.ds(pl.multiple_of(qb * BQ, BQ), BQ)
        wr = pl.ds(pl.multiple_of(qb * BQ, BQ), WIN)
        oh = jnp.where(nseg[pl.ds(pl.multiple_of(R + qb * BQ, BQ), BQ), :] == 0, -BIG, 0.0).astype(bf)
        qp = q[qr, hc]
        sp = sd[qr, hc]
        kp = k_[wr, hc]
        vp = v_[wr, hc]
        kk = jnp.concatenate([kp, nseg[wr, :]], 1)
        z = jnp.zeros_like(qp)
        dkp = []
        dvp = []
        dqs = []
        for h in range(2):
            sel = (lane < 64) if h == 0 else (lane >= 64)
            qm = jnp.where(sel, qp, z)
            sm = jnp.where(sel, sp, z)
            pr = jnp.exp2(nt(kk, jnp.concatenate([qm, oh], 1)) * C2)
            dp = nt(vp, sm)
            ds = (pr * (dp - ct[pl.ds(2 * hp + h, 1), qr])).astype(bf)
            dvp.append(nn(pr.astype(bf), sm))
            dkp.append(nn(ds, qm))
            dqs.append(tn(ds, kp))
        dk[wr, :] += dkp[0] + dkp[1]
        dv[wr, :] += dvp[0] + dvp[1]
        dqb[qr, hc] = (jnp.where(lane < 64, dqs[0], dqs[1]) * 0.125).astype(bf)

        @pl.when(qb == nqb - 1)
        def _():
            def fin(j, _):
                r = pl.ds(pl.multiple_of(j * 256, 256), 256)
                A[r, hc] = (dk[r, :] * 0.125).astype(bf)
                I[r, hc] = dv[r, :].astype(bf)
                dk[r, :] = jnp.zeros((256, 128), f32)
                dv[r, :] = jnp.zeros((256, 128), f32)
                return 0

            lax.fori_loop(0, 3 * R // 256, fin, 0)

        tick(i + 3)

        return 0

    lax.fori_loop(0, 6 * nqb, head, 0)
    t = 6 * nqb + 3

    W3 = 3 * R
    own = slice(R, 2 * R)
    for cp in loads[11:]:
        cp.start()
    loads[10].wait()
    vacc[0] = gvin[...]
    vacc[0, 0:1, :] = jnp.sum(dqb[...].astype(f32), 0, keepdims=True)
    vacc[0, 1:2, :] = jnp.sum(I[0:W3, :].astype(f32), 0, keepdims=True)
    for cp in loads[11:]:
        cp.wait()
    for dst, r in ((od, slice(0, R)), (nrm, slice(2 * R, W3))):
        dst[...] = (nt(A[r, :], wk[...]) + nt(I[r, :], wv[...])).astype(bf)

    @pl.when(odd)
    def _():
        ad[...] = od[...]

    @pl.when(jnp.logical_not(odd))
    def _():
        ad[...] = nrm[...]

    hn = R // HCH

    def leg1(ref, j):
        r = pl.ds(j * hn, hn)
        return remote(ref.at[r], HR.at[r], hs.at[0, j], hrs.at[0, j], (fwd, f))

    def leg2(j):
        r = pl.ds(j * hn, hn)
        return remote(ad.at[r], hin.at[r], hs.at[1, j], hrs.at[1, j], p[0])

    def halo(j):
        if 0 <= j < HCH:

            @pl.when(jnp.logical_and(has_fwd, odd))
            def _():
                leg1(nrm, j).start()

            @pl.when(jnp.logical_and(has_fwd, jnp.logical_not(odd)))
            def _():
                leg1(od, j).start()

        j = j - HLAG
        if 0 <= j < HCH:

            @pl.when(has_src)
            def _():
                leg1(od, j).wait_recv()
                r = pl.ds(j * hn, hn)
                add_rows(ad.at[r], ad.at[r], HR.at[r], hn, 32)

            leg2(j).start()

    halo(0)
    put(9, tn(xe[...], I[0:W3, :]))
    give(9)
    halo(1)
    put(10, tn(xe[...], A[0:W3, :]))
    give(10)
    s1(9)
    tick(t)
    halo(2)
    tick(t + 1)
    put(11, tn(xe[own, :], dqb[...]))
    give(11)
    s1(10)
    tick(t + 2)
    halo(3)
    tick(t + 3)
    ctx[...] = (nt(dqb[...], wq[...]) + nt(A[own, :], wk[...]) + nt(I[own, :], wv[...])).astype(bf)
    gxc = pltpu.make_async_copy(ctx, gx_o, ld.at[14])
    gxc.start()
    s1(11)
    vround = 0
    hj = 4
    for step in range(t + 4, NH + LAG * (len(stages) - 1)):
        if step < NH:
            tick(step)
        elif (step - NH) % 2 == 0:
            both(step)
        halo(hj)
        hj += 1
        if vround <= len(peers) and step % 2 == 0:
            if vround > 0:
                exchange.wait()
                vacc[vround] = vacc[vround - 1] + VR[vround - 1]
            if vround < len(peers):
                exchange = remote(vacc.at[vround], VR.at[vround], vs.at[vround], vr.at[vround], peers[vround])
                exchange.start()
            vround += 1
    while vround <= len(peers):
        exchange.wait()
        vacc[vround] = vacc[vround - 1] + VR[vround - 1]
        if vround < len(peers):
            exchange = remote(vacc.at[vround], VR.at[vround], vs.at[vround], vr.at[vround], peers[vround])
            exchange.start()
        vround += 1
    while hj < HCH + HLAG:
        halo(hj)
        hj += 1
    vout[...] = vacc[len(peers)]
    for j in range(HCH):
        leg2(j).wait()

        @pl.when(has_fwd)
        def _():
            leg1(od, j).wait_send()

    def done(m, _):
        core(lax.div(m, 2), lax.rem(m, 2)).wait_send()
        for i in range(6 + len(extra)):
            copy(m, i).wait_send()
        return 0

    lax.fori_loop(0, NH, done, 0)
    gxc.wait()


def back(n, act, od, nrm, idel, ctx, ad, q, k, v, sd, xe, wq, wk, wv, gv, ct, se):
    R = q.shape[0]
    ne = len(extra_bits(n))
    nv = 5 + ne
    S = jax.ShapeDtypeStruct
    ANY = pl.BlockSpec(memory_space=pl.ANY)
    big = (act, od, nrm, idel, ctx, ad, q, k, v, sd, xe, wq, wk, wv)
    return pl.pallas_call(
        functools.partial(back_kernel, n),
        out_shape=[S((NP, 2, 192, 384), bf), S((16, D), f32), S((R, D), bf), S((R, D), bf)],
        in_specs=[ANY] * 14 + [FULL] * 3,
        out_specs=[FULL] * 3 + [ANY],
        scratch_shapes=[VM(t.shape, t.dtype) for t in big[:11]]
        + [
            VM((NP, 4, 2, 192, 384), bf),
            VM((NP, 2, 2, 192, 384), bf),
            VM((NP, 2, 192, 384), bf),
            VM((NP, 2, 96, 384), bf),
            VM((NP, 2, 48, 384), bf),
            VM((NP, 2, 48, 384), bf),
            VM((ne, NP, 2, 48, 384) if ne else (1, 1, 2, 48, 384), bf),
            VM((nv, 16, D), f32),
            VM((nv + 1, 16, D), f32),
            VM((R, D), bf),
            VM((3 * R, 128), bf),
            VM((3 * R, 128), f32),
            VM((3 * R, 128), f32),
            DMA((15,)),
            DMA((NP, 2)),
            DMA((NP, 2)),
            DMA((NH, 6 + ne)),
            DMA((NH, 6 + ne)),
            DMA((nv,)),
            DMA((nv,)),
            DMA((2, HCH)),
            DMA((2, HCH)),
        ],
        compiler_params=pltpu.CompilerParams(collective_id=2, has_side_effects=True, vmem_limit_bytes=61 * 2**20),
        name="back",
    )(*big, gv, ct, se)


def last_kernel(g, gv, g1, gx, hin, gq, gk, gw, go, gi, gu, gt, *vecs):
    for h in range(2):
        cs = slice(384 * h, 384 * h + 384)
        for ref, k in ((gw, 9), (gk, 10), (gq, 11), (go, 8)):
            ref[:, cs] = g[k, h].astype(f32)
        for j in range(4):
            gi[:, 768 * j + 384 * h : 768 * j + 384 * h + 384] = g[4 + j, h].astype(f32)
            gu[192 * j : 192 * j + 192, cs] = g[j, h].astype(f32)
    gt[...] = g1[...] + gx[...].astype(f32) + hin[...].astype(f32)
    f = lax.axis_index("fsdp")
    w = D // 4
    own = lax.broadcasted_iota(jnp.int32, (D, w), 0) == lax.broadcasted_iota(jnp.int32, (D, w), 1) + f * w
    rows = lax.dot_general(
        gv[0:8, :],
        jnp.where(own, 1.0, 0.0),
        (((1,), (0,)), ((), ())),
        preferred_element_type=f32,
        precision=lax.Precision.HIGHEST,
    )
    for j in range(8):
        vecs[j][...] = rows[j : j + 1, :].reshape(w)
    vecs[8][...] = gv[pl.ds(8 + f, 1), :].reshape(D)


def last(g, gv, g1, gx, hin):
    R = g1.shape[0]
    S = jax.ShapeDtypeStruct
    outs = [S((192, D), f32)] * 4 + [S((192, 4 * D), f32), S((4 * 192, D), f32), S((R, D), f32)]
    outs += [S((D // 4,), f32)] * 8 + [S((D,), f32)]
    return pl.pallas_call(
        last_kernel,
        out_shape=outs,
        in_specs=[FULL] * 5,
        out_specs=[FULL] * 16,
        compiler_params=pltpu.CompilerParams(vmem_limit_bytes=VLIM),
        name="last",
    )(g, gv, g1, gx, hin)


def local(n, tokens, doc_lengths, cotangent, wq, wk, wv, wo, wi, wu, bq, bv, bo, bi, bu, ga, sa, gf, sf):
    x = tokens[0]
    docs = doc_lengths.shape[1]
    assert docs <= 128 and x.shape[0] == 512
    vecs = (bq, bv, bo, bu, ga, sa, gf, sf, bi)
    wq, wk, wv, xe, q, k, v, ctx, nrm, act, layer_out, od, idel, ad, sd, ct, gv, g1, se = front(
        n, x, (wq, wk, wv, wo, wi, wu), vecs, cotangent[0], doc_lengths
    )
    g, gv, hin, gx = back(n, act, od, nrm, idel, ctx, ad, q, k, v, sd, xe, wq, wk, wv, gv, ct, se)
    gq, gk, gw, go, gi, gu, gt, *gs, gbi = last(g, gv, g1, gx, hin)
    return (layer_out[None], gt[None], gq, gk, gw, go, gi, gu, gs[0], gs[1], gs[2], gbi, *gs[3:])


def solution(mesh):
    n = mesh.shape["ctx"]
    tok = P("fsdp", "ctx", None)
    mat = P("fsdp", None)
    vec = P("fsdp")
    return jax.shard_map(
        functools.partial(local, n),
        mesh=mesh,
        in_specs=(tok, mat, tok) + (mat,) * 6 + (vec,) * 9,
        out_specs=(tok, tok) + (mat,) * 6 + (vec,) * 9,
        check_vma=False,
    )
```
